32 devices in a mesh: parts: 2 (over y), seq: 8 (over z, core), rep: 2 (over x), head: 1.
Axes of the slice: x: 2, y: 2, z: 4, core: 2. Of those that a mesh axis runs over, the one named last changes fastest.
Arguments:
- activations: bfloat16 [4, 1024, 2048], P(('parts', 'rep'), 'seq', 'head'), parts along dimension 0, may hold values from -6 to 6
- value_weight: bfloat16 [2048, 2048], P(('seq', 'rep'), 'head'), may hold values from -0.125 to 0.125
- query_in: bfloat16 [4, 1024, 2048], P(('parts', 'rep'), 'seq', 'head'), parts along dimension 0, may hold values from -6 to 6
- key_in: bfloat16 [4, 1024, 2048], P(('parts', 'rep'), 'seq', 'head'), parts along dimension 0, may hold values from -6 to 6
- grad_out: bfloat16 [4, 1024, 2048], P(('parts', 'rep'), 'seq', 'head'), parts along dimension 0, may hold values from -6 to 6
- conv_kernel: float32 [3, 4, 2048], P(None, None, 'head'), may hold values from -3 to 3
- log_gate: float32 [4, 16, 1024], P(('parts', 'rep'), 'head', 'seq'), parts along dimension 0, as said below
Outputs:
- attn_out: bfloat16 [4, 1024, 2048], P(('parts', 'rep'), 'seq', 'head'), parts along dimension 0
- grad_query: bfloat16 [4, 1024, 2048], P(('parts', 'rep'), 'seq', 'head'), parts along dimension 0
- grad_key: bfloat16 [4, 1024, 2048], P(('parts', 'rep'), 'seq', 'head'), parts along dimension 0
- grad_x: bfloat16 [4, 1024, 2048], P(('parts', 'rep'), 'seq', 'head'), parts along dimension 0
- grad_w: float32 [4096, 2048], P(('parts', 'seq', 'rep'), 'head'), parts along dimension 0
- grad_conv: float32 [6, 4, 2048], P('parts', None, 'head'), parts along dimension 0
The draws below stay inside these ranges and needn't reach their ends.
There are 2 independent parts, one for each index of `parts`. The reference program is written for one: setup_inputs(seed, part) draws one part's arguments, and reference() takes and returns one part's arrays. A program takes and returns all parts, laid end to end along the dimension named above; an argument that names none is the same for every part. Nothing has to cross between parts.
Inputs may be any that keep to these rules, and one draw needn't show every extreme that they name: `log_gate`: every entry is below zero.
All inputs are finite; a program needn't handle non-finite values.
Results may differ from the reference program's by a relative error of at most 0.015.
Values may be sent and summed in bfloat16 or wider, within the bound.
A program may use at most 128 MiB of HBM per device.

```python
import math
import jax
import jax.numpy as jnp
from jax import lax

D = 2048
HEADS = 16
DH = 128
KW = 4
TOK_DEV = 128
C = 2048
STREAMS = 2
LENGTH = 1024
N_SEQ = 8


def draw_log_gate(key, part):
    order_key, slow_key, fast_key, block_key, rough_key, place_key, loss_key = jax.random.split(key, 7)
    stream_keys = jax.random.split(order_key, STREAMS)
    ranking = jax.vmap(lambda one_key: jax.random.permutation(one_key, HEADS))(stream_keys)
    fast_count = HEADS // 2
    fast_heads = ranking < fast_count
    slow_rate = jnp.exp(jax.random.uniform(slow_key, (STREAMS, HEADS), jnp.float32, jnp.log(0.1), jnp.log(0.6))) / LENGTH
    fast_span = jax.random.uniform(fast_key, (STREAMS, HEADS), jnp.float32, 30.0, 50.0) * (TOK_DEV / 512.0)
    reference_frequency = jnp.where(fast_heads, 1.0 / fast_span, slow_rate)
    block_count = LENGTH // TOK_DEV
    segment_factor = jnp.exp(jax.random.uniform(block_key, (STREAMS, HEADS, block_count), jnp.float32, jnp.log(0.7), jnp.log(1.4)))
    segment_factor = jnp.repeat(segment_factor, TOK_DEV, axis=2)
    roughness_measure = jax.random.uniform(rough_key, (STREAMS, HEADS, LENGTH), jnp.float32, 0.5, 1.5)
    spot_sequence = jax.random.randint(place_key, (STREAMS, 3), 0, LENGTH)
    objective_samples = jax.random.uniform(loss_key, (STREAMS, 3), jnp.float32, 0.2, 0.4)
    ordinal_numbers = jnp.arange(LENGTH)
    spike_tally = (ordinal_numbers[None, None, :] == spot_sequence[:, :, None]).astype(jnp.float32)
    spike_surcharge = jnp.sum(spike_tally * (-jnp.log1p(-objective_samples))[:, :, None], axis=1)
    return -(reference_frequency[:, :, None] * segment_factor * roughness_measure + spike_surcharge[:, None, :])


def raised(values, stream_key, source, target, parts, factor):
    def block_of(axis_at):
        return (jnp.arange(values.shape[axis_at]) // (values.shape[axis_at] // parts)).reshape((-1,) + (1,) * (values.ndim - 1 - axis_at))

    one_side = jax.random.permutation(stream_key, parts)[block_of(target)]
    other_side = (block_of(target) + parts // 2) % parts
    return jnp.where((block_of(source) == one_side) | (block_of(source) == other_side), factor * values, values)


def level_of(rng, shape, shards, least, largest):
    gain = 1.0
    for dim, parts in shards:
        heights = jax.random.uniform(jax.random.fold_in(jax.random.fold_in(rng, 6), dim), (parts,), jnp.float32, least / len(shards), largest / len(shards))
        gain = gain * jnp.repeat(jnp.exp(heights), shape[dim] // parts).reshape((-1,) + (1,) * (len(shape) - 1 - dim))
    return gain


def bell_draw(stream_key, dims, scale, reach, cuts=(), kind=jnp.bfloat16):
    entries = jax.random.normal(stream_key, dims, jnp.float32) * scale
    if len(cuts) > 0:
        entries = level_of(stream_key, dims, cuts, -0.22, 0.18) * entries
    return jnp.clip(entries, min=-reach, max=reach).astype(kind)


def noise_with(rng, shape, scale, reach, pieces, heavy, held_as=jnp.bfloat16):
    entries = scale * jax.random.normal(rng, shape, jnp.float32)
    if pieces:
        entries = entries * level_of(rng, shape, pieces, -0.22, 0.18)
    return jnp.clip(raised(entries, jax.random.fold_in(rng, 3), *heavy), -reach, reach).astype(held_as)


def setup_inputs(seed: int = 0, part: int = 0) -> dict:
    seeds = jax.random.split(jax.random.key(seed), 8)
    part_keys = jax.random.split(jax.random.fold_in(seeds[7], part), 8)
    activations = noise_with(part_keys[0], (STREAMS, LENGTH, D), 1.0, 6.0, ((0, 2), (1, 8)), (1, 2, 8, 2.0))
    value_weight = bell_draw(seeds[1], (D, C), D ** -0.5, 0.125, ((0, 16),))
    query_in = bell_draw(part_keys[2], (STREAMS, LENGTH, C), 1.0, 6.0, ((0, 2), (1, 8)))
    key_in = bell_draw(part_keys[3], (STREAMS, LENGTH, C), 1.0, 6.0, ((0, 2), (1, 8)))
    grad_out = bell_draw(part_keys[4], (STREAMS, LENGTH, C), 1.0, 6.0, ((0, 2), (1, 8)))
    conv_kernel = bell_draw(seeds[5], (3, KW, C), 0.5, 3.0, (), jnp.float32)
    log_gate = draw_log_gate(jax.random.fold_in(jax.random.fold_in(seeds[7], part), 71), part)
    return {"activations": activations, "value_weight": value_weight, "query_in": query_in, "key_in": key_in, "grad_out": grad_out, "conv_kernel": conv_kernel, "log_gate": log_gate}


EPSILON = 1e-06

def rounded(array):
    return lax.optimization_barrier(array.astype(jnp.bfloat16)).astype(jnp.float32)

def causal_filter(stream_rows, kernel_taps):
    rim_rows = kernel_taps.shape[0] - 1
    length = stream_rows.shape[1]
    extended = jnp.pad(stream_rows.astype(jnp.float32), ((0, 0), (rim_rows, 0), (0, 0)))
    result = jnp.zeros(stream_rows.shape, jnp.float32)
    for offset in range(kernel_taps.shape[0]):
        result = result + kernel_taps[offset] * extended[:, rim_rows - offset:rim_rows - offset + length]
    return result

def filter_back(post_rows, kernel_taps):
    rim_rows = kernel_taps.shape[0] - 1
    length = post_rows.shape[1]
    extended = jnp.pad(post_rows, ((0, 0), (0, rim_rows), (0, 0)))
    result = jnp.zeros(post_rows.shape, jnp.float32)
    for offset in range(kernel_taps.shape[0]):
        result = result + kernel_taps[offset] * extended[:, offset:offset + length]
    return result

def tap_sums(post_rows, stream_rows, kernel_width):
    rim_rows = kernel_width - 1
    length = stream_rows.shape[1]
    extended = jnp.pad(stream_rows.astype(jnp.float32), ((0, 0), (rim_rows, 0), (0, 0)))
    return jnp.stack([lax.optimization_barrier(jnp.sum(post_rows * extended[:, rim_rows - offset:rim_rows - offset + length], axis=(0, 1))) for offset in range(kernel_width)])

def block_states(decay, sums, reverse):

    def advance(carry, item):
        one_decay, one_sum = item
        return (one_decay[:, :, None, None] * carry + one_sum, carry)
    start = jnp.zeros((STREAMS, HEADS, DH, DH), jnp.float32)
    _, states = lax.scan(advance, start, (jnp.moveaxis(decay, 1, 0), jnp.moveaxis(sums, 1, 0)), reverse=reverse)
    return jnp.moveaxis(states, 0, 1)

def mixing_of(cum_block):
    cum_heads = cum_block.T
    return jnp.exp(-jnp.abs(cum_heads[:, :, None] - cum_heads[:, None, :]))

def local_forward(item):
    query_block, key_block, value_block, cum_block = item
    mixing = mixing_of(cum_block)
    scores = rounded(mixing * jnp.einsum('thd,shd->hts', query_block.astype(jnp.float32), key_block.astype(jnp.float32)))
    return jnp.einsum('hts,she->the', scores, value_block.astype(jnp.float32))

def local_backward(item):
    query_block, key_block, value_block, cum_block, grad_block = item
    mixing = mixing_of(cum_block)
    query_f = query_block.astype(jnp.float32)
    key_f = key_block.astype(jnp.float32)
    value_f = value_block.astype(jnp.float32)
    grad_f = grad_block.astype(jnp.float32)
    scores = rounded(mixing * jnp.einsum('thd,shd->hts', query_f, key_f))
    grad_scores = rounded(mixing * jnp.einsum('the,she->hts', grad_f, value_f))
    query_part = jnp.einsum('hts,shd->thd', grad_scores, key_f)
    key_part = jnp.einsum('hts,thd->shd', grad_scores, query_f)
    value_part = jnp.einsum('hts,the->she', scores, grad_f)
    return (query_part, key_part, value_part)

def reference(activations, value_weight, query_in, key_in, grad_out, conv_kernel, log_gate):
    blocks = N_SEQ
    grad_scale = 1.0 / math.sqrt(STREAMS * LENGTH)
    value_raw = jnp.dot(activations.reshape(STREAMS * LENGTH, D), value_weight, preferred_element_type=jnp.float32).astype(jnp.bfloat16).reshape(STREAMS, LENGTH, C)
    raw_inputs = (query_in, key_in, value_raw)
    convolved = [causal_filter(raw_inputs[which], conv_kernel[which]).astype(jnp.bfloat16) for which in range(3)]
    shape_blocks = (STREAMS, blocks, TOK_DEV, HEADS, DH)
    query_heads = convolved[0].reshape(shape_blocks)
    key_heads = convolved[1].reshape(shape_blocks)
    value_heads = convolved[2].reshape(shape_blocks)
    cumulative = jnp.cumsum(log_gate.reshape(STREAMS, HEADS, blocks, TOK_DEV), axis=3)
    final_cum = cumulative[:, :, :, -1]
    block_decay = jnp.exp(jnp.transpose(final_cum, (0, 2, 1)))
    cum_rows = jnp.transpose(cumulative, (0, 2, 3, 1))
    rising = jnp.exp(cum_rows)[..., None]
    shrink = jnp.exp(jnp.transpose(final_cum, (0, 2, 1))[:, :, None, :] - cum_rows)[..., None]
    query_f = query_heads.astype(jnp.float32)
    key_f = key_heads.astype(jnp.float32)
    value_f = value_heads.astype(jnp.float32)
    fwd_sum = jnp.einsum('sbthd,sbthe->sbhde', rounded(shrink * key_f), value_f)
    back_sum = jnp.einsum('sbthd,sbthe->sbhde', rounded(rising * key_f), value_f)
    left_b = rounded(block_states(block_decay, fwd_sum, False))
    right_b = rounded(block_states(block_decay, back_sum, True))
    flat = (STREAMS * blocks, TOK_DEV, HEADS, DH)
    flat_cum = cum_rows.reshape(STREAMS * blocks, TOK_DEV, HEADS)
    local_attn = lax.map(local_forward, (query_heads.reshape(flat), key_heads.reshape(flat), value_heads.reshape(flat), flat_cum)).reshape(shape_blocks)
    attn = rising * jnp.einsum('sbthd,sbhde->sbthe', query_f, left_b) + shrink * jnp.einsum('sbthd,sbhde->sbthe', query_f, right_b) + local_attn
    root_mean = jnp.sqrt(lax.optimization_barrier(jnp.mean(attn * attn, axis=4, keepdims=True)) + EPSILON)
    normed = attn / root_mean
    attn_out = normed.astype(jnp.bfloat16).reshape(STREAMS, LENGTH, C)
    upstream = grad_out.reshape(shape_blocks).astype(jnp.float32)
    grad_attn = ((upstream - normed * lax.optimization_barrier(jnp.mean(upstream * normed, axis=4, keepdims=True))) / root_mean).astype(jnp.bfloat16)
    grad_f = grad_attn.astype(jnp.float32)
    fwd_grad = jnp.einsum('sbthd,sbthe->sbhde', rounded(shrink * query_f), grad_f)
    back_grad = jnp.einsum('sbthd,sbthe->sbhde', rounded(rising * query_f), grad_f)
    left_gb = rounded(block_states(block_decay, fwd_grad, False))
    right_gb = rounded(block_states(block_decay, back_grad, True))
    local_query, local_key, local_value = lax.map(local_backward, (query_heads.reshape(flat), key_heads.reshape(flat), value_heads.reshape(flat), flat_cum, grad_attn.reshape(flat)))
    query_post = rising * jnp.einsum('sbthe,sbhde->sbthd', grad_f, left_b) + shrink * jnp.einsum('sbthe,sbhde->sbthd', grad_f, right_b) + local_query.reshape(shape_blocks)
    key_post = rising * jnp.einsum('sbthe,sbhde->sbthd', value_f, left_gb) + shrink * jnp.einsum('sbthe,sbhde->sbthd', value_f, right_gb) + local_key.reshape(shape_blocks)
    value_post = rising * jnp.einsum('sbthd,sbhde->sbthe', key_f, left_gb) + shrink * jnp.einsum('sbthd,sbhde->sbthe', key_f, right_gb) + local_value.reshape(shape_blocks)
    post_rows = [part.reshape(STREAMS, LENGTH, C) for part in (query_post, key_post, value_post)]
    grad_query = filter_back(post_rows[0], conv_kernel[0]).astype(jnp.bfloat16)
    grad_key = filter_back(post_rows[1], conv_kernel[1]).astype(jnp.bfloat16)
    grad_value = filter_back(post_rows[2], conv_kernel[2]).astype(jnp.bfloat16)
    grad_conv = jnp.stack([tap_sums(post_rows[which], raw_inputs[which], KW) for which in range(3)]) * grad_scale
    grad_x = jnp.dot(grad_value.reshape(STREAMS * LENGTH, C), value_weight.T, preferred_element_type=jnp.float32).astype(jnp.bfloat16).reshape(STREAMS, LENGTH, D)
    grad_w = jnp.dot(activations.reshape(STREAMS * LENGTH, D).T, grad_value.reshape(STREAMS * LENGTH, C), preferred_element_type=jnp.float32) * grad_scale
    return (attn_out, grad_query, grad_key, grad_x, grad_w, grad_conv)
```

```python
import functools
import math

import jax
import jax.numpy as jnp
from jax import lax
from jax.experimental import pallas as pl
from jax.experimental.pallas import tpu as pltpu
from jax.sharding import PartitionSpec as P

EPSILON = 1e-06
EDGE = 16
LAG = 2
F32 = jnp.float32
BF16 = jnp.bfloat16


def dot(a, b):
    return lax.dot_general(a, b, (((1,), (0,)), ((), ())), preferred_element_type=F32)


def dot_t(a, b):
    return lax.dot_general(a, b, (((1,), (1,)), ((), ())), preferred_element_type=F32)


def kernel(n, reps, scale, *refs):
    (act, w, q, k, go, ck, lg) = refs[:7]
    (ao, gq, gk, px, gw, gc) = refs[7:13]
    (
        acta, wg, vout, vr, qkh, xf, cumr, rise, shrink, mx, qh, kh, vh, gh, lhs1, lhs2, kt, qt, rsv,
        sums, sin, sout, po, phs, phr, actt, actc, gvg, gxi, pxf, pxs, pxi, gws, gwi, gwa,
        gcp, gca, gcb, gcf,
        wxs, wxr, axs, axr, ahs, ahr, qhs, qhr, wgs, wgr, vxs, vxr, ats, atr, ss, sr, phss, phsr,
        gvs, gvrs, gxs, gxr, pxss, pxsr, gwss, gwsr, cs1, cr1, cs2, cr2, cs3, cr3,
    ) = refs[13:]
    T, F = act.shape
    FB, C = w.shape
    H = lg.shape[0]
    D = C // H
    TH = T + EDGE
    NW, _, _, CC = wg.shape
    NT, _, _, CT = gvg.shape
    half = C // reps
    NH = NT // reps
    UP = 2 * H // n
    me = lax.axis_index("seq")
    r = lax.axis_index("rep")
    first, last = me == 0, me == n - 1
    right, left = lax.rem(me + 1, n), lax.rem(me + n - 1, n)

    def peer(d):
        return lax.rem(r + d, reps)

    def remote(src, dst, send, recv, seq, rep):
        return pltpu.make_async_remote_copy(
            src_ref=src, dst_ref=dst, send_sem=send, recv_sem=recv,
            device_id={"seq": seq, "rep": rep}, device_id_type=pl.DeviceIdType.MESH,
        )

    def lanes(h):
        return pl.ds(pl.multiple_of(h * D, D), D)

    barrier = pltpu.get_barrier_semaphore()
    for ds in range(n):
        for dr in range(reps):
            if ds or dr:
                pl.semaphore_signal(
                    barrier, inc=1, device_id={"seq": lax.rem(me + ds, n), "rep": peer(dr)},
                    device_id_type=pl.DeviceIdType.MESH,
                )
    pl.semaphore_wait(barrier, n * reps - 1)

    def w_swap(c, d):
        to = peer(d)
        return remote(
            w.at[:, pl.ds(pl.multiple_of(to * half + c * CC, CC), CC)],
            wg.at[c, me, pl.ds(r * FB, FB), :], wxs.at[c, d - 1], wxr.at[c, d - 1], me, to,
        )

    def act_swap(d):
        return remote(act, acta.at[pl.ds(r * TH + EDGE, T), :], axs.at[d - 1], axr.at[d - 1], me, peer(d))

    def act_edge(d):
        return remote(
            act.at[pl.ds(T - EDGE, EDGE), :], acta.at[pl.ds(r * TH, EDGE), :], ahs.at[d], ahr.at[d], right, peer(d)
        )

    def qk_edge(i):
        return remote((q, k)[i].at[pl.ds(T - EDGE, EDGE), :], qkh.at[i], qhs.at[i], qhr.at[i], right, r)

    for d in range(1, reps):
        w_swap(0, d).start()

    @pl.when(jnp.logical_not(last))
    def _():
        for i in range(2):
            qk_edge(i).start()

    for c in range(1, NW):
        for d in range(1, reps):
            w_swap(c, d).start()
    for d in range(1, reps):
        act_swap(d).start()

    @pl.when(jnp.logical_not(last))
    def _():
        for d in range(reps):
            act_edge(d).start()

    for c in range(NW):
        wg[c, me, pl.ds(r * FB, FB), :] = w[:, pl.ds(pl.multiple_of(r * half + c * CC, CC), CC)]
    acta[pl.ds(r * TH + EDGE, T), :] = act[...]

    @pl.when(first)
    def _():
        for d in range(reps):
            acta[pl.ds(d * TH, EDGE), :] = jnp.zeros((EDGE, F), BF16)
        qkh[...] = jnp.zeros(qkh.shape, BF16)
        sin[0] = jnp.zeros(sin.shape[1:], BF16)
        sin[2] = jnp.zeros(sin.shape[1:], BF16)

    @pl.when(last)
    def _():
        sin[1] = jnp.zeros(sin.shape[1:], BF16)
        sin[3] = jnp.zeros(sin.shape[1:], BF16)
        phr[...] = jnp.zeros(phr.shape, BF16)

    def hop(buf, send, recv, c, o, way):
        return remote(buf.at[c, o], buf.at[c, o], send.at[way, c, o], recv.at[c, o], (right, left)[way], r)

    def own(buf, send, recv, c):
        @pl.when(jnp.logical_not(last))
        def _():
            hop(buf, send, recv, c, me, 0).start()

        @pl.when(jnp.logical_not(first))
        def _():
            hop(buf, send, recv, c, me, 1).start()

    def pass_on(buf, send, recv, c, t):
        lower, upper = me - t, me + t

        @pl.when(lower >= 0)
        def _():
            hop(buf, send, recv, c, lower, 0).wait_recv()

            @pl.when(jnp.logical_not(last))
            def _():
                hop(buf, send, recv, c, lower, 0).start()

        @pl.when(upper < n)
        def _():
            hop(buf, send, recv, c, upper, 1).wait_recv()

            @pl.when(jnp.logical_not(first))
            def _():
                hop(buf, send, recv, c, upper, 1).start()

    def sent(buf, send, recv, chunks):
        def one(i, _):
            c, o = i // n, lax.rem(i, n)

            @pl.when(jnp.logical_and(jnp.logical_not(last), o <= me))
            def _():
                hop(buf, send, recv, c, o, 0).wait_send()

            @pl.when(jnp.logical_and(jnp.logical_not(first), o >= me))
            def _():
                hop(buf, send, recv, c, o, 1).wait_send()

            return 0

        lax.fori_loop(0, chunks * n, one, 0)

    total = lg[...]
    place = lax.broadcasted_iota(jnp.int32, total.shape, 1)
    distance = 1
    while distance < T:
        moved = pltpu.roll(total, distance, 1)
        total = total + jnp.where(place >= distance, moved, 0.0)
        distance *= 2
    cumr[...] = total
    columns = jnp.concatenate([total, jnp.zeros((T - H, T), F32)], axis=0).T
    for h in range(H):
        rise[h] = jnp.broadcast_to(columns[:, h : h + 1], (T, D))

    def filtered(i, x, taps):
        out = taps[0:1] * x[i, EDGE : EDGE + T]
        for j in range(1, 4):
            out = out + taps[j : j + 1] * x[i, EDGE - j : EDGE - j + T]
        return out.astype(BF16)

    def load_rows(i, h):
        if i < 2:
            xf[i, 0:EDGE] = qkh[i, :, lanes(h)].astype(F32)
            xf[i, EDGE:] = (q, k)[i][:, lanes(h)].astype(F32)
        else:
            per = CC // D
            xf[i] = vr[h // per, :, pl.ds(pl.multiple_of(lax.rem(h, per) * D, D), D)].astype(F32)

    def prepare(h):
        cc = rise[h]
        fin = cc[T - 1 : T]
        rising = jnp.exp(cc)
        shrinking = jnp.exp(fin - cc)
        mixing = jnp.exp(-jnp.abs(cc - cumr[pl.ds(h, 1), :]))
        rise[h] = rising
        shrink[h] = shrinking
        mx[h] = mixing
        for i in range(2):
            load_rows(i, h)
        qv = filtered(0, xf, ck[0, :, lanes(h)])
        kv = filtered(1, xf, ck[1, :, lanes(h)])
        qh[h] = qv
        kh[h] = kv
        qf, kf = qv.astype(F32), kv.astype(F32)
        rq, sq = (rising * qf), (shrinking * qf)
        rk, sk = (rising * kf), (shrinking * kf)
        lhs1[h, :, 0:D] = (mixing * dot_t(qv, kv)).astype(BF16)
        lhs1[h, :, D : 2 * D] = rq.astype(BF16)
        lhs1[h, :, 2 * D :] = sq.astype(BF16)
        lhs2[h, :, 0:D] = (mixing * dot_t(kv, qv)).astype(BF16)
        lhs2[h, :, D : 2 * D] = rk.astype(BF16)
        lhs2[h, :, 2 * D :] = sk.astype(BF16)
        qt[h, 0:D] = sq.T.astype(BF16)
        qt[h, D:] = rq.T.astype(BF16)
        kt[h, 0:D] = sk.T.astype(BF16)
        kt[h, D:] = rk.T.astype(BF16)

    def turn(b):
        rows = pl.ds(pl.multiple_of(b * T, T), T)
        actt[rows, :] = act[:, rows].astype(F32).T.astype(BF16)

    def ready(c):
        for d in range(1, reps):
            w_swap(c, d).wait_recv()
        own(wg, wgs, wgr, c)

    def v_swap(c, d):
        to = peer(d)
        return remote(
            vout.at[c, pl.ds(to * TH, TH), :], vr.at[r * NW + c], vxs.at[c, d - 1], vxr.at[c, d - 1], me, to
        )

    ready(0)

    @pl.when(jnp.logical_not(first))
    def _():
        for i in range(2):
            qk_edge(i).wait_recv()

    def w_step(i, _):
        c, t = i // (n - 1), lax.rem(i, n - 1) + 1

        @pl.when(jnp.logical_and(t == 1, c + 1 < NW))
        def _():
            ready(c + 1)

        @pl.when(i < H)
        def _():
            prepare(i)

        pass_on(wg, wgs, wgr, c, t)

        @pl.when(i < F // T)
        def _():
            turn(i)

        @pl.when(t == n - 1)
        def _():
            @pl.when(c == 0)
            def _():
                for d in range(1, reps):
                    act_swap(d).wait_recv()

                @pl.when(jnp.logical_not(first))
                def _():
                    for d in range(reps):
                        act_edge(d).wait_recv()

            vout[c] = dot(acta[...], wg[c].reshape(F, CC)).astype(BF16)
            for d in range(1, reps):
                v_swap(c, d).start()
            vr[r * NW + c] = vout[c, pl.ds(r * TH, TH), :]

        return 0

    W_STEPS = NW * (n - 1)
    lax.fori_loop(0, W_STEPS, w_step, 0)
    lax.fori_loop(W_STEPS, max(W_STEPS, H), lambda i, _: (prepare(i), 0)[1], 0)
    lax.fori_loop(W_STEPS, max(W_STEPS, F // T), lambda i, _: (turn(i), 0)[1], 0)

    def a_swap(d):
        to = lax.rem(me + d, n)
        return remote(
            actt.at[pl.ds(to * reps * FB, reps * FB), :], actc.at[:, pl.ds(pl.multiple_of(me * T, T), T)],
            ats.at[d - 1], atr.at[d - 1], to, r,
        )

    def a_swap_from(d):
        source = lax.rem(me + n - d, n)
        return remote(
            actt.at[pl.ds(0, reps * FB), :], actc.at[:, pl.ds(pl.multiple_of(source * T, T), T)],
            ats.at[d - 1], atr.at[d - 1], source, r,
        )

    for d in range(1, n):
        a_swap(d).start()
    actc[:, pl.ds(pl.multiple_of(me * T, T), T)] = actt[pl.ds(me * reps * FB, reps * FB), :]

    def v_arrival(c, d):
        source = lax.rem(r + reps - d, reps)
        return remote(
            vout.at[c, pl.ds(0, TH), :], vr.at[source * NW + c], vxs.at[c, d - 1], vxr.at[c, d - 1], me, source
        )

    for c in range(NW):
        for d in range(1, reps):
            v_arrival(c, d).wait_recv()

    def values(h):
        load_rows(2, h)
        v = filtered(2, xf, ck[2, :, lanes(h)])
        vh[h] = v
        vf = v.astype(F32)
        rsv[h, :, 0:D] = (rise[h] * vf).astype(BF16)
        rsv[h, :, D:] = (shrink[h] * vf).astype(BF16)
        both = dot(kt[h], v)
        sums[0, h] = both[0:D]
        sums[1, h] = both[D:]

    def message(i, h):
        return remote(sout.at[i, h], sin.at[i, h], ss.at[i, h], sr.at[i, h], (right, left)[i % 2], r)

    def carry(i, h):
        begins, ends = ((first, last), (last, first))[i % 2]

        @pl.when(jnp.logical_not(begins))
        def _():
            message(i, h).wait_recv()

        @pl.when(jnp.logical_not(ends))
        def _():
            decay = rise[h, T - 1 : T]
            sout[i, h] = (decay * sin[i, h].astype(F32) + sums[i, h]).astype(BF16)
            message(i, h).start()

    def attend(h):
        v, before, after = vh[h], sin[0, h], sin[1, h]
        attn = dot(lhs1[h], jnp.concatenate([v, before, after], axis=0))
        inverse = lax.rsqrt(jnp.mean(attn * attn, axis=1, keepdims=True) + EPSILON)
        normed = attn * inverse
        ao[:, lanes(h)] = normed.astype(BF16)
        up = go[:, lanes(h)].astype(F32)
        g = ((up - normed * jnp.mean(up * normed, axis=1, keepdims=True)) * inverse).astype(BF16)
        gh[h] = g
        both = dot(qt[h], g)
        sums[2, h] = both[0:D]
        sums[3, h] = both[D:]

    def query_side(h):
        v, before, after, g, mixing = vh[h], sin[0, h], sin[1, h], gh[h], mx[h]
        gf = g.astype(F32)
        decayed = jnp.concatenate([(rise[h] * gf).astype(BF16), (shrink[h] * gf).astype(BF16)], axis=1)
        grad_scores = (mixing * dot_t(g, v)).astype(BF16)
        grad_scores_t = (mixing * dot_t(v, g)).astype(BF16)
        po[0, h, 0:T] = dot(grad_scores, kh[h]) + dot_t(decayed, jnp.concatenate([before, after], axis=1))
        po[1, h, 0:T] = dot(grad_scores_t, qh[h])

    def key_side(h):
        before, after = sin[2, h], sin[3, h]
        po[1, h, 0:T] = po[1, h, 0:T] + dot_t(rsv[h], jnp.concatenate([before, after], axis=1))
        po[2, h, 0:T] = dot(lhs2[h], jnp.concatenate([gh[h], before, after], axis=0))
        rows = []
        for i in range(3):
            load_rows(i, h)
            post = po[i, h, 0:T]
            phs[i, h] = post[0:EDGE].astype(BF16)
            for j in range(4):
                rows.append(jnp.sum(post * xf[i, EDGE - j : EDGE - j + T], axis=0, keepdims=True))
        zero = jnp.zeros((4, D), F32)
        gcp[2 * h] = jnp.concatenate(rows[0:8], axis=0)
        gcp[2 * h + 1] = jnp.concatenate(rows[8:12] + [zero], axis=0)

    far = (n - 1) * LAG

    def scan_step(s, _):
        def at(h, work):
            @pl.when(jnp.logical_and(h >= 0, h < H))
            def _():
                work(h)

        at(s, values)
        at(s - me * LAG, functools.partial(carry, 0))
        at(s - (n - 1 - me) * LAG, functools.partial(carry, 1))
        at(s - far, attend)
        at(s - far - me * LAG, functools.partial(carry, 2))
        at(s - far - (n - 1 - me) * LAG, functools.partial(carry, 3))
        at(s - far, query_side)
        at(s - 2 * far, key_side)
        return 0

    lax.fori_loop(0, H + 2 * far, scan_step, 0)

    def post_edge(i):
        return remote(phs.at[i], phr.at[i], phss.at[i], phsr.at[i], left, r)

    @pl.when(jnp.logical_not(first))
    def _():
        for i in (2, 0, 1):
            post_edge(i).start()

    def taps_out(d):
        to = lax.rem(me + d, n)
        return remote(gcp.at[pl.ds(to * UP, UP)], gca.at[me], cs1.at[d - 1], cr1.at[d - 1], to, r)

    def taps_in(d):
        source = lax.rem(me + n - d, n)
        return remote(gcp.at[pl.ds(0, UP)], gca.at[source], cs1.at[d - 1], cr1.at[d - 1], source, r)

    def taps_swap(d):
        return remote(gcb.at[r], gcb.at[r], cs2.at[d - 1], cr2.at[d - 1], me, peer(d))

    def taps_swap_in(d):
        source = lax.rem(r + reps - d, reps)
        return remote(gcb.at[r], gcb.at[source], cs2.at[d - 1], cr2.at[d - 1], me, source)

    def taps_back(d):
        to = lax.rem(me + d, n)
        return remote(gcf.at[pl.ds(me * UP, UP)], gcf.at[pl.ds(me * UP, UP)], cs3.at[d - 1], cr3.at[d - 1], to, r)

    def taps_back_in(d):
        source = lax.rem(me + n - d, n)
        return remote(
            gcf.at[pl.ds(me * UP, UP)], gcf.at[pl.ds(source * UP, UP)], cs3.at[d - 1], cr3.at[d - 1], source, r
        )

    for d in range(1, n):
        taps_out(d).start()
    gca[me] = gcp[pl.ds(me * UP, UP)]

    def back(i, h):
        po[i, h, T : T + 8] = phr[i, h].astype(F32)[0:8]
        taps = ck[i, :, lanes(h)]
        out = taps[0:1] * po[i, h, 0:T]
        for j in range(1, 4):
            out = out + taps[j : j + 1] * po[i, h, j : j + T]
        return out.astype(BF16)

    @pl.when(jnp.logical_not(last))
    def _():
        post_edge(2).wait_recv()

    for c in range(NT):
        for j in range(CT // D):
            gvg[c, me, :, j * D : (j + 1) * D] = back(2, c * (CT // D) + j)
        if c < 2:
            own(gvg, gvs, gvrs, c)

    def gx_swap(j, d):
        to = peer(d)
        return remote(gvg.at[to * NH + j, me], gxi.at[r, j], gxs.at[j, d - 1], gxr.at[j, d - 1], me, to)

    def gx_swap_in(j, d):
        source = lax.rem(r + reps - d, reps)
        return remote(gvg.at[j, me], gxi.at[source, j], gxs.at[j, d - 1], gxr.at[j, d - 1], me, source)

    for j in range(NH):
        for d in range(1, reps):
            gx_swap(j, d).start()
        gxi[r, j] = gvg[r * NH + j, me]

    @pl.when(jnp.logical_not(last))
    def _():
        for i in range(2):
            post_edge(i).wait_recv()

    TILE = 512

    def input_grad(b):
        rows = wg.shape[2]
        per = TILE // rows
        out = jnp.zeros((reps * T, TILE), F32)
        for c in range(NW):
            j, at = divmod(c * CC, CT)
            x = gxi[:, j, :, at : at + CC].reshape(reps * T, CC)
            out = out + dot_t(x, wg[c, pl.ds(b * per, per)].reshape(TILE, CC))
        cols = pl.ds(pl.multiple_of(b * TILE, TILE), TILE)
        for i in range(reps):
            pxf[i, :, cols] = out[i * T : (i + 1) * T]
            pxs[i, :, cols] = out[i * T : (i + 1) * T].astype(BF16)

    def px_swap(d):
        to = peer(d)
        return remote(pxs.at[to], pxi.at[d - 1], pxss.at[d - 1], pxsr.at[d - 1], me, to)

    def gw_swap(c, d):
        to = peer(d)
        return remote(gws.at[c, pl.ds(to * FB, FB), :], gwi.at[c, d - 1], gwss.at[c, d - 1], gwsr.at[c, d - 1], me, to)

    X_TILES = F // TILE

    def last_step(i, _):
        c, t = i // (n - 1), lax.rem(i, n - 1) + 1

        @pl.when(jnp.logical_and(t == 1, jnp.logical_and(c >= 1, c + 1 < NT)))
        def _():
            own(gvg, gvs, gvrs, c + 1)

        pass_on(gvg, gvs, gvrs, c, t)

        @pl.when(i < H)
        def _():
            gq[:, lanes(i)] = back(0, i)
            gk[:, lanes(i)] = back(1, i)

        @pl.when(i == 3)
        def _():
            for d in range(1, n):
                taps_in(d).wait_recv()
            part = gca[0]
            for s in range(1, n):
                part = part + gca[s]
            gcb[r] = part
            for d in range(1, reps):
                taps_swap(d).start()

        @pl.when(i == 6)
        def _():
            for d in range(1, reps):
                taps_swap_in(d).wait_recv()
            part = gcb[0]
            for s in range(1, reps):
                part = part + gcb[s]
            gcf[pl.ds(me * UP, UP)] = part * scale
            for d in range(1, n):
                taps_back(d).start()

        @pl.when(i == 7)
        def _():
            for j in range(NH):
                for d in range(1, reps):
                    gx_swap_in(j, d).wait_recv()

        @pl.when(jnp.logical_and(i >= 8, i < 8 + X_TILES))
        def _():
            input_grad(i - 8)

        @pl.when(i == 8 + X_TILES)
        def _():
            for d in range(1, reps):
                px_swap(d).start()

        @pl.when(t == n - 1)
        def _():
            @pl.when(c == 0)
            def _():
                for d in range(1, n):
                    a_swap_from(d).wait_recv()

            gwa[c] = dot(actc[...], gvg[c].reshape(n * T, CT))
            gws[c] = gwa[c].astype(BF16)
            for d in range(1, reps):
                gw_swap(c, d).start()

        return 0

    lax.fori_loop(0, NT * (n - 1), last_step, 0)
    for d in range(1, reps):
        px_swap(d).wait_recv()
    out = pxf[r]
    for d in range(1, reps):
        out = out + pxi[d - 1].astype(F32)
    px[...] = out.astype(BF16)
    for d in range(1, n):
        taps_back_in(d).wait_recv()
    for h in range(H):
        gc[0, :, h * D : (h + 1) * D] = gcf[2 * h, 0:4]
        gc[1, :, h * D : (h + 1) * D] = gcf[2 * h, 4:8]
        gc[2, :, h * D : (h + 1) * D] = gcf[2 * h + 1, 0:4]
    for c in range(NT):
        for d in range(1, reps):
            gw_swap(c, d).wait_recv()
        out = gwa[c, pl.ds(r * FB, FB), :]
        for d in range(1, reps):
            out = out + gwi[c, d - 1].astype(F32)
        gw[:, c * CT : (c + 1) * CT] = out * scale

    for d in range(1, reps):
        act_swap(d).wait_send()
        px_swap(d).wait_send()
        taps_swap(d).wait_send()
        for c in range(NW):
            w_swap(c, d).wait_send()
            v_swap(c, d).wait_send()
        for c in range(NT):
            gw_swap(c, d).wait_send()
        for j in range(NH):
            gx_swap(j, d).wait_send()
    for d in range(1, n):
        a_swap(d).wait_send()
        taps_out(d).wait_send()
        taps_back(d).wait_send()

    @pl.when(jnp.logical_not(last))
    def _():
        for i in range(2):
            qk_edge(i).wait_send()
        for d in range(reps):
            act_edge(d).wait_send()

    @pl.when(jnp.logical_not(first))
    def _():
        for i in range(3):
            post_edge(i).wait_send()

    sent(wg, wgs, wgr, NW)
    sent(gvg, gvs, gvrs, NT)

    def states_sent(h, _):
        @pl.when(jnp.logical_not(last))
        def _():
            message(0, h).wait_send()
            message(2, h).wait_send()

        @pl.when(jnp.logical_not(first))
        def _():
            message(1, h).wait_send()
            message(3, h).wait_send()

        return 0

    lax.fori_loop(0, H, states_sent, 0)


def local(n, reps, activations, value_weight, query_in, key_in, grad_out, conv_kernel, log_gate):
    act = lax.all_gather(activations, "head", axis=2, tiled=True)[0]
    T, F = act.shape
    FB, C = value_weight.shape
    H = log_gate.shape[1]
    D = C // H
    TH = T + EDGE
    CC = min(256, C // reps)
    CT = min(512, C // reps)
    NW, NT = C // reps // CC, C // CT
    NH = NT // reps
    UP = 2 * H // n
    scale = 1.0 / math.sqrt(n * reps * T)
    dma = pltpu.SemaphoreType.DMA
    peers = max(reps - 1, 1)
    scratch = [
        pltpu.VMEM((reps * TH, F), BF16),
        pltpu.VMEM((NW, n, reps * FB, CC), BF16),
        pltpu.VMEM((NW, reps * TH, CC), BF16),
        pltpu.VMEM((reps * NW, TH, CC), BF16),
        pltpu.VMEM((2, EDGE, C), BF16),
        pltpu.VMEM((3, TH, D), F32),
        pltpu.VMEM((H, T), F32),
        pltpu.VMEM((H, T, D), F32),
        pltpu.VMEM((H, T, D), F32),
        pltpu.VMEM((H, T, T), F32),
        pltpu.VMEM((H, T, D), BF16),
        pltpu.VMEM((H, T, D), BF16),
        pltpu.VMEM((H, T, D), BF16),
        pltpu.VMEM((H, T, D), BF16),
        pltpu.VMEM((H, T, 3 * D), BF16),
        pltpu.VMEM((H, T, 3 * D), BF16),
        pltpu.VMEM((H, 2 * D, T), BF16),
        pltpu.VMEM((H, 2 * D, T), BF16),
        pltpu.VMEM((H, T, 2 * D), BF16),
        pltpu.VMEM((4, H, D, D), F32),
        pltpu.VMEM((4, H, D, D), BF16),
        pltpu.VMEM((4, H, D, D), BF16),
        pltpu.VMEM((3, H, T + 8, D), F32),
        pltpu.VMEM((3, H, EDGE, D), BF16),
        pltpu.VMEM((3, H, EDGE, D), BF16),
        pltpu.VMEM((F, T), BF16),
        pltpu.VMEM((reps * FB, n * T), BF16),
        pltpu.VMEM((NT, n, T, CT), BF16),
        pltpu.VMEM((reps, NH, T, CT), BF16),
        pltpu.VMEM((reps, T, F), F32),
        pltpu.VMEM((reps, T, F), BF16),
        pltpu.VMEM((peers, T, F), BF16),
        pltpu.VMEM((NT, reps * FB, CT), BF16),
        pltpu.VMEM((NT, peers, FB, CT), BF16),
        pltpu.VMEM((NT, reps * FB, CT), F32),
        pltpu.VMEM((n * UP, 8, D), F32),
        pltpu.VMEM((n, UP, 8, D), F32),
        pltpu.VMEM((reps, UP, 8, D), F32),
        pltpu.VMEM((n * UP, 8, D), F32),
        dma((NW, peers)), dma((NW, peers)),
        dma((peers,)), dma((peers,)),
        dma((reps,)), dma((reps,)),
        dma((2,)), dma((2,)),
        dma((2, NW, n)), dma((NW, n)),
        dma((NW, peers)), dma((NW, peers)),
        dma((n - 1,)), dma((n - 1,)),
        dma((4, H)), dma((4, H)),
        dma((3,)), dma((3,)),
        dma((2, NT, n)), dma((NT, n)),
        dma((NH, peers)), dma((NH, peers)),
        dma((peers,)), dma((peers,)),
        dma((NT, peers)), dma((NT, peers)),
        dma((n - 1,)), dma((n - 1,)),
        dma((peers,)), dma((peers,)),
        dma((n - 1,)), dma((n - 1,)),
    ]
    vmem = pl.BlockSpec(memory_space=pltpu.VMEM)
    attn_out, grad_query, grad_key, part_x, grad_w, grad_conv = pl.pallas_call(
        functools.partial(kernel, n, reps, scale),
        out_shape=(
            jax.ShapeDtypeStruct((T, C), BF16),
            jax.ShapeDtypeStruct((T, C), BF16),
            jax.ShapeDtypeStruct((T, C), BF16),
            jax.ShapeDtypeStruct((T, F), BF16),
            jax.ShapeDtypeStruct((FB, C), F32),
            jax.ShapeDtypeStruct(conv_kernel.shape, F32),
        ),
        in_specs=[vmem] * 7,
        out_specs=[vmem] * 6,
        scratch_shapes=scratch,
        compiler_params=pltpu.CompilerParams(
            collective_id=0, has_side_effects=True, vmem_limit_bytes=60 * 2**20
        ),
        cost_estimate=pl.CostEstimate(flops=5 * 10**9, bytes_accessed=8 * 2**20, transcendentals=10**6),
    )(act, value_weight, query_in[0], key_in[0], grad_out[0], conv_kernel, log_gate[0])
    grad_x = lax.psum_scatter(part_x[None], "head", scatter_dimension=2, tiled=True)
    return attn_out[None], grad_query[None], grad_key[None], grad_x, grad_w, grad_conv


def solution(mesh):
    placed = (
        P(("parts", "rep"), "seq", "head"),
        P(("seq", "rep"), "head"),
        P(("parts", "rep"), "seq", "head"),
        P(("parts", "rep"), "seq", "head"),
        P(("parts", "rep"), "seq", "head"),
        P(None, None, "head"),
        P(("parts", "rep"), "head", "seq"),
    )
    return jax.shard_map(
        functools.partial(local, mesh.shape["seq"], mesh.shape["rep"]),
        mesh=mesh,
        in_specs=placed,
        out_specs=(
            P(("parts", "rep"), "seq", "head"),
            P(("parts", "rep"), "seq", "head"),
            P(("parts", "rep"), "seq", "head"),
            P(("parts", "rep"), "seq", "head"),
            P(("parts", "seq", "rep"), "head"),
            P("parts", None, "head"),
        ),
        check_vma=False,
    )
```

```python
import functools
import math

import jax
import jax.numpy as jnp
from jax import lax
from jax.experimental import pallas as pl
from jax.experimental.pallas import tpu as pltpu
from jax.sharding import PartitionSpec as P

EPSILON = 1e-06
EDGE = 16
LAG = 3
W_SKEW = 1
G_SKEW = 2
TILE = 512
F32 = jnp.float32
BF16 = jnp.bfloat16


def dot(a, b):
    return lax.dot_general(a, b, (((1,), (0,)), ((), ())), preferred_element_type=F32)


def dot_t(a, b):
    return lax.dot_general(a, b, (((1,), (1,)), ((), ())), preferred_element_type=F32)


def kernel(n, reps, scale, *refs):
    (act, w, q, k, go, ck, lg) = refs[:7]
    (ao, gq, gk, px, gw, gc) = refs[7:13]
    (
        acta, wg, vout, vr, qkh, xf, cumr, rise, shrink, mx, qh, kh, vh, gh, lhs1, lhs2, kt, qt, rsv,
        sums, sin, sout, po, phs, phr, actt, actc, gvg, gxi, pxf, pxs, pxi, gws, gwi, gwa,
        gcp, gca, gcb, gcf,
        wxs, wxr, axs, axr, ahs, ahr, qhs, qhr, wgs, wgr, vxs, vxr, ats, atr, ss, sr, phss, phsr,
        gvs, gvrs, gxs, gxr, pxss, pxsr, gwss, gwsr, cs1, cr1, cs2, cr2, cs3, cr3,
    ) = refs[13:]
    T, F = act.shape
    FB, C = w.shape
    H = lg.shape[0]
    D = C // H
    TH = T + EDGE
    NW, _, _, CC = wg.shape
    NT, _, _, CT = gvg.shape
    half = C // reps
    NH = NT // reps
    UP = 2 * H // n
    me = lax.axis_index("seq")
    r = lax.axis_index("rep")
    first, last = me == 0, me == n - 1
    right, left = lax.rem(me + 1, n), lax.rem(me + n - 1, n)

    def peer(d):
        return lax.rem(r + d, reps)

    def remote(src, dst, send, recv, seq, rep):
        return pltpu.make_async_remote_copy(
            src_ref=src, dst_ref=dst, send_sem=send, recv_sem=recv,
            device_id={"seq": seq, "rep": rep}, device_id_type=pl.DeviceIdType.MESH,
        )

    def lanes(h):
        return pl.ds(pl.multiple_of(h * D, D), D)

    barrier = pltpu.get_barrier_semaphore()
    for ds in range(n):
        for dr in range(reps):
            if ds or dr:
                pl.semaphore_signal(
                    barrier, inc=1, device_id={"seq": lax.rem(me + ds, n), "rep": peer(dr)},
                    device_id_type=pl.DeviceIdType.MESH,
                )
    pl.semaphore_wait(barrier, n * reps - 1)

    def w_swap(c, d):
        to = peer(d)
        return remote(
            w.at[:, pl.ds(pl.multiple_of(to * half + c * CC, CC), CC)],
            wg.at[c, me, pl.ds(r * FB, FB), :], wxs.at[c, d - 1], wxr.at[c, d - 1], me, to,
        )

    def act_swap(d):
        return remote(act, acta.at[pl.ds(r * TH + EDGE, T), :], axs.at[d - 1], axr.at[d - 1], me, peer(d))

    def act_edge(d):
        return remote(
            act.at[pl.ds(T - EDGE, EDGE), :], acta.at[pl.ds(r * TH, EDGE), :], ahs.at[d], ahr.at[d], right, peer(d)
        )

    def qk_edge(i):
        return remote((q, k)[i].at[pl.ds(T - EDGE, EDGE), :], qkh.at[i], qhs.at[i], qhr.at[i], right, r)

    for d in range(1, reps):
        w_swap(0, d).start()

    @pl.when(jnp.logical_not(last))
    def _():
        for i in range(2):
            qk_edge(i).start()

    for c in range(1, NW):
        for d in range(1, reps):
            w_swap(c, d).start()
    for d in range(1, reps):
        act_swap(d).start()

    @pl.when(jnp.logical_not(last))
    def _():
        for d in range(reps):
            act_edge(d).start()

    for c in range(NW):
        wg[c, me, pl.ds(r * FB, FB), :] = w[:, pl.ds(pl.multiple_of(r * half + c * CC, CC), CC)]
    acta[pl.ds(r * TH + EDGE, T), :] = act[...]

    @pl.when(first)
    def _():
        for d in range(reps):
            acta[pl.ds(d * TH, EDGE), :] = jnp.zeros((EDGE, F), BF16)
        qkh[...] = jnp.zeros(qkh.shape, BF16)
        sin[0] = jnp.zeros(sin.shape[1:], BF16)
        sin[2] = jnp.zeros(sin.shape[1:], BF16)

    @pl.when(last)
    def _():
        sin[1] = jnp.zeros(sin.shape[1:], BF16)
        sin[3] = jnp.zeros(sin.shape[1:], BF16)
        phr[...] = jnp.zeros(phr.shape, BF16)

    def hop(buf, send, recv, c, o, way):
        return remote(buf.at[c, o], buf.at[c, o], send.at[way, c, o], recv.at[c, o], (right, left)[way], r)

    def own(buf, send, recv, c):
        @pl.when(jnp.logical_not(last))
        def _():
            hop(buf, send, recv, c, me, 0).start()

        @pl.when(jnp.logical_not(first))
        def _():
            hop(buf, send, recv, c, me, 1).start()

    def pass_on(buf, send, recv, c, t):
        lower, upper = me - t, me + t

        @pl.when(lower >= 0)
        def _():
            hop(buf, send, recv, c, lower, 0).wait_recv()

            @pl.when(jnp.logical_not(last))
            def _():
                hop(buf, send, recv, c, lower, 0).start()

        @pl.when(upper < n)
        def _():
            hop(buf, send, recv, c, upper, 1).wait_recv()

            @pl.when(jnp.logical_not(first))
            def _():
                hop(buf, send, recv, c, upper, 1).start()

    def sent(buf, send, recv, chunks):
        def one(i, _):
            c, o = i // n, lax.rem(i, n)

            @pl.when(jnp.logical_and(jnp.logical_not(last), o <= me))
            def _():
                hop(buf, send, recv, c, o, 0).wait_send()

            @pl.when(jnp.logical_and(jnp.logical_not(first), o >= me))
            def _():
                hop(buf, send, recv, c, o, 1).wait_send()

            return 0

        lax.fori_loop(0, chunks * n, one, 0)

    total = lg[...]
    place = lax.broadcasted_iota(jnp.int32, total.shape, 1)
    distance = 1
    while distance < T:
        moved = pltpu.roll(total, distance, 1)
        total = total + jnp.where(place >= distance, moved, 0.0)
        distance *= 2
    cumr[...] = total
    columns = jnp.concatenate([total, jnp.zeros((T - H, T), F32)], axis=0).T
    for h in range(H):
        rise[h] = jnp.broadcast_to(columns[:, h : h + 1], (T, D))

    def filtered(i, x, taps):
        out = taps[0:1] * x[i, EDGE : EDGE + T]
        for j in range(1, 4):
            out = out + taps[j : j + 1] * x[i, EDGE - j : EDGE - j + T]
        return out.astype(BF16)

    def load_rows(i, h):
        if i < 2:
            xf[i, 0:EDGE] = qkh[i, :, lanes(h)].astype(F32)
            xf[i, EDGE:] = (q, k)[i][:, lanes(h)].astype(F32)
        else:
            per = CC // D
            xf[i] = vr[h // per, :, pl.ds(pl.multiple_of(lax.rem(h, per) * D, D), D)].astype(F32)

    def prepare(h):
        cc = rise[h]
        fin = cc[T - 1 : T]
        rising = jnp.exp(cc)
        shrinking = jnp.exp(fin - cc)
        mixing = jnp.exp(-jnp.abs(cc - cumr[pl.ds(h, 1), :]))
        rise[h] = rising
        shrink[h] = shrinking
        mx[h] = mixing
        for i in range(2):
            load_rows(i, h)
        qv = filtered(0, xf, ck[0, :, lanes(h)])
        kv = filtered(1, xf, ck[1, :, lanes(h)])
        qh[h] = qv
        kh[h] = kv
        qf, kf = qv.astype(F32), kv.astype(F32)
        rq, sq = (rising * qf), (shrinking * qf)
        rk, sk = (rising * kf), (shrinking * kf)
        lhs1[h, :, 0:D] = (mixing * dot_t(qv, kv)).astype(BF16)
        lhs1[h, :, D : 2 * D] = rq.astype(BF16)
        lhs1[h, :, 2 * D :] = sq.astype(BF16)
        lhs2[h, :, 0:D] = (mixing * dot_t(kv, qv)).astype(BF16)
        lhs2[h, :, D : 2 * D] = rk.astype(BF16)
        lhs2[h, :, 2 * D :] = sk.astype(BF16)
        qt[h, 0:D] = sq.T.astype(BF16)
        qt[h, D:] = rq.T.astype(BF16)
        kt[h, 0:D] = sk.T.astype(BF16)
        kt[h, D:] = rk.T.astype(BF16)

    def turn(b):
        rows = pl.ds(pl.multiple_of(b * T, T), T)
        actt[rows, :] = act[:, rows].astype(F32).T.astype(BF16)

    def ready(c):
        for d in range(1, reps):
            w_swap(c, d).wait_recv()
        own(wg, wgs, wgr, c)

    def v_swap(c, d):
        to = peer(d)
        return remote(
            vout.at[c, pl.ds(to * TH, TH), :], vr.at[r * NW + c], vxs.at[c, d - 1], vxr.at[c, d - 1], me, to
        )

    @pl.when(jnp.logical_not(first))
    def _():
        for i in range(2):
            qk_edge(i).wait_recv()

    def jobs(work, count, step, steps):
        per = -(-count // steps)
        for j in range(per):
            @pl.when(step * per + j < count)
            def _():
                work(step * per + j)

    W_STEPS = n + W_SKEW * (NW - 1)

    def w_step(s, _):
        for c in range(NW):
            t = s - W_SKEW * c

            @pl.when(t == 0)
            def _():
                ready(c)

            @pl.when(jnp.logical_and(t >= 1, t < n))
            def _():
                pass_on(wg, wgs, wgr, c, t)

            @pl.when(t == n - 1)
            def _():
                if c == 0:
                    for d in range(1, reps):
                        act_swap(d).wait_recv()

                    @pl.when(jnp.logical_not(first))
                    def _():
                        for d in range(reps):
                            act_edge(d).wait_recv()

                vout[c] = dot(acta[...], wg[c].reshape(F, CC)).astype(BF16)
                for d in range(1, reps):
                    v_swap(c, d).start()
                vr[r * NW + c] = vout[c, pl.ds(r * TH, TH), :]

        jobs(prepare, H, s, n)
        jobs(turn, F // T, s, n)
        return 0

    lax.fori_loop(0, W_STEPS, w_step, 0)

    def a_swap(d):
        to = lax.rem(me + d, n)
        return remote(
            actt.at[pl.ds(to * reps * FB, reps * FB), :], actc.at[:, pl.ds(pl.multiple_of(me * T, T), T)],
            ats.at[d - 1], atr.at[d - 1], to, r,
        )

    def a_swap_from(d):
        source = lax.rem(me + n - d, n)
        return remote(
            actt.at[pl.ds(0, reps * FB), :], actc.at[:, pl.ds(pl.multiple_of(source * T, T), T)],
            ats.at[d - 1], atr.at[d - 1], source, r,
        )

    for d in range(1, n):
        a_swap(d).start()
    actc[:, pl.ds(pl.multiple_of(me * T, T), T)] = actt[pl.ds(me * reps * FB, reps * FB), :]

    def v_arrival(c, d):
        source = lax.rem(r + reps - d, reps)
        return remote(
            vout.at[c, pl.ds(0, TH), :], vr.at[source * NW + c], vxs.at[c, d - 1], vxr.at[c, d - 1], me, source
        )

    for c in range(NW):
        for d in range(1, reps):
            v_arrival(c, d).wait_recv()

    def values(h):
        load_rows(2, h)
        v = filtered(2, xf, ck[2, :, lanes(h)])
        vh[h] = v
        vf = v.astype(F32)
        rsv[h, :, 0:D] = (rise[h] * vf).astype(BF16)
        rsv[h, :, D:] = (shrink[h] * vf).astype(BF16)
        both = dot(kt[h], v)
        sums[0, h] = both[0:D]
        sums[1, h] = both[D:]

    def message(i, h):
        return remote(sout.at[i, h], sin.at[i, h], ss.at[i, h], sr.at[i, h], (right, left)[i % 2], r)

    def carry(i, h):
        begins, ends = ((first, last), (last, first))[i % 2]

        @pl.when(jnp.logical_not(begins))
        def _():
            message(i, h).wait_recv()

        @pl.when(jnp.logical_not(ends))
        def _():
            decay = rise[h, T - 1 : T]
            sout[i, h] = (decay * sin[i, h].astype(F32) + sums[i, h]).astype(BF16)
            message(i, h).start()

    def attend(h):
        v, before, after = vh[h], sin[0, h], sin[1, h]
        attn = dot(lhs1[h], jnp.concatenate([v, before, after], axis=0))
        inverse = lax.rsqrt(jnp.mean(attn * attn, axis=1, keepdims=True) + EPSILON)
        normed = attn * inverse
        ao[:, lanes(h)] = normed.astype(BF16)
        up = go[:, lanes(h)].astype(F32)
        g = ((up - normed * jnp.mean(up * normed, axis=1, keepdims=True)) * inverse).astype(BF16)
        gh[h] = g
        both = dot(qt[h], g)
        sums[2, h] = both[0:D]
        sums[3, h] = both[D:]

    def query_side(h):
        v, before, after, g, mixing = vh[h], sin[0, h], sin[1, h], gh[h], mx[h]
        gf = g.astype(F32)
        decayed = jnp.concatenate([(rise[h] * gf).astype(BF16), (shrink[h] * gf).astype(BF16)], axis=1)
        grad_scores = (mixing * dot_t(g, v)).astype(BF16)
        grad_scores_t = (mixing * dot_t(v, g)).astype(BF16)
        po[0, h, 0:T] = dot(grad_scores, kh[h]) + dot_t(decayed, jnp.concatenate([before, after], axis=1))
        po[1, h, 0:T] = dot(grad_scores_t, qh[h])

    def key_side(h):
        before, after = sin[2, h], sin[3, h]
        po[1, h, 0:T] = po[1, h, 0:T] + dot_t(rsv[h], jnp.concatenate([before, after], axis=1))
        po[2, h, 0:T] = dot(lhs2[h], jnp.concatenate([gh[h], before, after], axis=0))
        rows = []
        for i in range(3):
            load_rows(i, h)
            post = po[i, h, 0:T]
            phs[i, h] = post[0:EDGE].astype(BF16)
            for j in range(4):
                rows.append(jnp.sum(post * xf[i, EDGE - j : EDGE - j + T], axis=0, keepdims=True))
        zero = jnp.zeros((4, D), F32)
        gcp[2 * h] = jnp.concatenate(rows[0:8], axis=0)
        gcp[2 * h + 1] = jnp.concatenate(rows[8:12] + [zero], axis=0)

    far = (n - 1) * LAG

    def scan_step(s, _):
        def at(h, work):
            @pl.when(jnp.logical_and(h >= 0, h < H))
            def _():
                work(h)

        at(s, values)
        at(s - me * LAG, functools.partial(carry, 0))
        at(s - (n - 1 - me) * LAG, functools.partial(carry, 1))
        at(s - far, attend)
        at(s - far - me * LAG, functools.partial(carry, 2))
        at(s - far - (n - 1 - me) * LAG, functools.partial(carry, 3))
        at(s - far, query_side)
        at(s - 2 * far, key_side)
        return 0

    lax.fori_loop(0, H + 2 * far, scan_step, 0)

    def post_edge(i):
        return remote(phs.at[i], phr.at[i], phss.at[i], phsr.at[i], left, r)

    @pl.when(jnp.logical_not(first))
    def _():
        for i in (2, 0, 1):
            post_edge(i).start()

    def taps_out(d):
        to = lax.rem(me + d, n)
        return remote(gcp.at[pl.ds(to * UP, UP)], gca.at[me], cs1.at[d - 1], cr1.at[d - 1], to, r)

    def taps_in(d):
        source = lax.rem(me + n - d, n)
        return remote(gcp.at[pl.ds(0, UP)], gca.at[source], cs1.at[d - 1], cr1.at[d - 1], source, r)

    def taps_swap(d):
        return remote(gcb.at[r], gcb.at[r], cs2.at[d - 1], cr2.at[d - 1], me, peer(d))

    def taps_swap_in(d):
        source = lax.rem(r + reps - d, reps)
        return remote(gcb.at[r], gcb.at[source], cs2.at[d - 1], cr2.at[d - 1], me, source)

    def taps_back(d):
        to = lax.rem(me + d, n)
        return remote(gcf.at[pl.ds(me * UP, UP)], gcf.at[pl.ds(me * UP, UP)], cs3.at[d - 1], cr3.at[d - 1], to, r)

    def taps_back_in(d):
        source = lax.rem(me + n - d, n)
        return remote(
            gcf.at[pl.ds(me * UP, UP)], gcf.at[pl.ds(source * UP, UP)], cs3.at[d - 1], cr3.at[d - 1], source, r
        )

    for d in range(1, n):
        taps_out(d).start()
    gca[me] = gcp[pl.ds(me * UP, UP)]

    def back(i, h):
        po[i, h, T : T + 8] = phr[i, h].astype(F32)[0:8]
        taps = ck[i, :, lanes(h)]
        out = taps[0:1] * po[i, h, 0:T]
        for j in range(1, 4):
            out = out + taps[j : j + 1] * po[i, h, j : j + T]
        return out.astype(BF16)

    @pl.when(jnp.logical_not(last))
    def _():
        post_edge(2).wait_recv()

    for c in range(NT):
        for j in range(CT // D):
            gvg[c, me, :, j * D : (j + 1) * D] = back(2, c * (CT // D) + j)
        if c == 0:
            own(gvg, gvs, gvrs, c)

    def gx_swap(j, d):
        to = peer(d)
        return remote(gvg.at[to * NH + j, me], gxi.at[r, j], gxs.at[j, d - 1], gxr.at[j, d - 1], me, to)

    def gx_swap_in(j, d):
        source = lax.rem(r + reps - d, reps)
        return remote(gvg.at[j, me], gxi.at[source, j], gxs.at[j, d - 1], gxr.at[j, d - 1], me, source)

    for j in range(NH):
        for d in range(1, reps):
            gx_swap(j, d).start()
        gxi[r, j] = gvg[r * NH + j, me]

    @pl.when(jnp.logical_not(last))
    def _():
        for i in range(2):
            post_edge(i).wait_recv()

    def input_grad(b):
        rows = wg.shape[2]
        per = TILE // rows
        out = jnp.zeros((reps * T, TILE), F32)
        for c in range(NW):
            j, at = divmod(c * CC, CT)
            x = gxi[:, j, :, at : at + CC].reshape(reps * T, CC)
            out = out + dot_t(x, wg[c, pl.ds(b * per, per)].reshape(TILE, CC))
        cols = pl.ds(pl.multiple_of(b * TILE, TILE), TILE)
        for i in range(reps):
            pxf[i, :, cols] = out[i * T : (i + 1) * T]
            pxs[i, :, cols] = out[i * T : (i + 1) * T].astype(BF16)

    def px_swap(d):
        to = peer(d)
        return remote(pxs.at[to], pxi.at[d - 1], pxss.at[d - 1], pxsr.at[d - 1], me, to)

    def gw_swap(c, d):
        to = peer(d)
        return remote(gws.at[c, pl.ds(to * FB, FB), :], gwi.at[c, d - 1], gwss.at[c, d - 1], gwsr.at[c, d - 1], me, to)

    X_TILES = F // TILE
    G_STEPS = n + G_SKEW * (NT - 1)

    def both_back(h):
        gq[:, lanes(h)] = back(0, h)
        gk[:, lanes(h)] = back(1, h)

    def last_step(s, _):
        for c in range(NT):
            t = s - G_SKEW * c
            if c:
                @pl.when(t == 0)
                def _():
                    own(gvg, gvs, gvrs, c)

            @pl.when(jnp.logical_and(t >= 1, t < n))
            def _():
                pass_on(gvg, gvs, gvrs, c, t)

            @pl.when(t == n - 1)
            def _():
                if c == 0:
                    for d in range(1, n):
                        a_swap_from(d).wait_recv()

                gwa[c] = dot(actc[...], gvg[c].reshape(n * T, CT))
                gws[c] = gwa[c].astype(BF16)
                for d in range(1, reps):
                    gw_swap(c, d).start()

        jobs(both_back, H, s, n)

        @pl.when(s == 1)
        def _():
            for d in range(1, n):
                taps_in(d).wait_recv()
            part = gca[0]
            for o in range(1, n):
                part = part + gca[o]
            gcb[r] = part
            for d in range(1, reps):
                taps_swap(d).start()

        @pl.when(s == 3)
        def _():
            for d in range(1, reps):
                taps_swap_in(d).wait_recv()
            part = gcb[0]
            for o in range(1, reps):
                part = part + gcb[o]
            gcf[pl.ds(me * UP, UP)] = part * scale
            for d in range(1, n):
                taps_back(d).start()

        @pl.when(s == 2)
        def _():
            for j in range(NH):
                for d in range(1, reps):
                    gx_swap_in(j, d).wait_recv()

        @pl.when(jnp.logical_and(s >= 3, s < 3 + X_TILES))
        def _():
            input_grad(s - 3)

        @pl.when(s == 3 + X_TILES)
        def _():
            for d in range(1, reps):
                px_swap(d).start()

        return 0

    lax.fori_loop(0, G_STEPS, last_step, 0)
    for d in range(1, reps):
        px_swap(d).wait_recv()
    out = pxf[r]
    for d in range(1, reps):
        out = out + pxi[d - 1].astype(F32)
    px[...] = out.astype(BF16)
    for d in range(1, n):
        taps_back_in(d).wait_recv()
    for h in range(H):
        gc[0, :, h * D : (h + 1) * D] = gcf[2 * h, 0:4]
        gc[1, :, h * D : (h + 1) * D] = gcf[2 * h, 4:8]
        gc[2, :, h * D : (h + 1) * D] = gcf[2 * h + 1, 0:4]
    for c in range(NT):
        for d in range(1, reps):
            gw_swap(c, d).wait_recv()
        out = gwa[c, pl.ds(r * FB, FB), :]
        for d in range(1, reps):
            out = out + gwi[c, d - 1].astype(F32)
        gw[:, c * CT : (c + 1) * CT] = out * scale

    for d in range(1, reps):
        act_swap(d).wait_send()
        px_swap(d).wait_send()
        taps_swap(d).wait_send()
        for c in range(NW):
            w_swap(c, d).wait_send()
            v_swap(c, d).wait_send()
        for c in range(NT):
            gw_swap(c, d).wait_send()
        for j in range(NH):
            gx_swap(j, d).wait_send()
    for d in range(1, n):
        a_swap(d).wait_send()
        taps_out(d).wait_send()
        taps_back(d).wait_send()

    @pl.when(jnp.logical_not(last))
    def _():
        for i in range(2):
            qk_edge(i).wait_send()
        for d in range(reps):
            act_edge(d).wait_send()

    @pl.when(jnp.logical_not(first))
    def _():
        for i in range(3):
            post_edge(i).wait_send()

    sent(wg, wgs, wgr, NW)
    sent(gvg, gvs, gvrs, NT)

    def states_sent(h, _):
        @pl.when(jnp.logical_not(last))
        def _():
            message(0, h).wait_send()
            message(2, h).wait_send()

        @pl.when(jnp.logical_not(first))
        def _():
            message(1, h).wait_send()
            message(3, h).wait_send()

        return 0

    lax.fori_loop(0, H, states_sent, 0)


def hand_over(*refs):
    count = len(refs) // 2
    sems = refs[-1]
    copies = [pltpu.make_async_copy(refs[i], refs[count + i], sems.at[i]) for i in range(count)]
    for copy in copies:
        copy.start()
    for copy in copies:
        copy.wait()


def local(n, reps, activations, value_weight, query_in, key_in, grad_out, conv_kernel, log_gate):
    act = lax.all_gather(activations, "head", axis=2, tiled=True)[0]
    T, F = act.shape
    FB, C = value_weight.shape
    H = log_gate.shape[1]
    D = C // H
    TH = T + EDGE
    CC = min(256, C // reps)
    CT = min(512, C // reps)
    NW, NT = C // reps // CC, C // CT
    NH = NT // reps
    UP = 2 * H // n
    scale = 1.0 / math.sqrt(n * reps * T)
    dma = pltpu.SemaphoreType.DMA
    peers = max(reps - 1, 1)
    scratch = [
        pltpu.VMEM((reps * TH, F), BF16),
        pltpu.VMEM((NW, n, reps * FB, CC), BF16),
        pltpu.VMEM((NW, reps * TH, CC), BF16),
        pltpu.VMEM((reps * NW, TH, CC), BF16),
        pltpu.VMEM((2, EDGE, C), BF16),
        pltpu.VMEM((3, TH, D), F32),
        pltpu.VMEM((H, T), F32),
        pltpu.VMEM((H, T, D), F32),
        pltpu.VMEM((H, T, D), F32),
        pltpu.VMEM((H, T, T), F32),
        pltpu.VMEM((H, T, D), BF16),
        pltpu.VMEM((H, T, D), BF16),
        pltpu.VMEM((H, T, D), BF16),
        pltpu.VMEM((H, T, D), BF16),
        pltpu.VMEM((H, T, 3 * D), BF16),
        pltpu.VMEM((H, T, 3 * D), BF16),
        pltpu.VMEM((H, 2 * D, T), BF16),
        pltpu.VMEM((H, 2 * D, T), BF16),
        pltpu.VMEM((H, T, 2 * D), BF16),
        pltpu.VMEM((4, H, D, D), F32),
        pltpu.VMEM((4, H, D, D), BF16),
        pltpu.VMEM((4, H, D, D), BF16),
        pltpu.VMEM((3, H, T + 8, D), F32),
        pltpu.VMEM((3, H, EDGE, D), BF16),
        pltpu.VMEM((3, H, EDGE, D), BF16),
        pltpu.VMEM((F, T), BF16),
        pltpu.VMEM((reps * FB, n * T), BF16),
        pltpu.VMEM((NT, n, T, CT), BF16),
        pltpu.VMEM((reps, NH, T, CT), BF16),
        pltpu.VMEM((reps, T, F), F32),
        pltpu.VMEM((reps, T, F), BF16),
        pltpu.VMEM((peers, T, F), BF16),
        pltpu.VMEM((NT, reps * FB, CT), BF16),
        pltpu.VMEM((NT, peers, FB, CT), BF16),
        pltpu.VMEM((NT, reps * FB, CT), F32),
        pltpu.VMEM((n * UP, 8, D), F32),
        pltpu.VMEM((n, UP, 8, D), F32),
        pltpu.VMEM((reps, UP, 8, D), F32),
        pltpu.VMEM((n * UP, 8, D), F32),
        dma((NW, peers)), dma((NW, peers)),
        dma((peers,)), dma((peers,)),
        dma((reps,)), dma((reps,)),
        dma((2,)), dma((2,)),
        dma((2, NW, n)), dma((NW, n)),
        dma((NW, peers)), dma((NW, peers)),
        dma((n - 1,)), dma((n - 1,)),
        dma((4, H)), dma((4, H)),
        dma((3,)), dma((3,)),
        dma((2, NT, n)), dma((NT, n)),
        dma((NH, peers)), dma((NH, peers)),
        dma((peers,)), dma((peers,)),
        dma((NT, peers)), dma((NT, peers)),
        dma((n - 1,)), dma((n - 1,)),
        dma((peers,)), dma((peers,)),
        dma((n - 1,)), dma((n - 1,)),
    ]
    vmem = pl.BlockSpec(memory_space=pltpu.VMEM)
    results = pl.pallas_call(
        functools.partial(kernel, n, reps, scale),
        out_shape=(
            jax.ShapeDtypeStruct((T, C), BF16),
            jax.ShapeDtypeStruct((T, C), BF16),
            jax.ShapeDtypeStruct((T, C), BF16),
            jax.ShapeDtypeStruct((T, F), BF16),
            jax.ShapeDtypeStruct((FB, C), F32),
            jax.ShapeDtypeStruct(conv_kernel.shape, F32),
        ),
        in_specs=[vmem] * 7,
        out_specs=[vmem] * 6,
        scratch_shapes=scratch,
        compiler_params=pltpu.CompilerParams(
            collective_id=0, has_side_effects=True, vmem_limit_bytes=60 * 2**20
        ),
        cost_estimate=pl.CostEstimate(flops=5 * 10**9, bytes_accessed=8 * 2**20, transcendentals=10**6),
    )(act, value_weight, query_in[0], key_in[0], grad_out[0], conv_kernel, log_gate[0])
    kept = pl.BlockSpec(memory_space=pl.ANY)
    attn_out, grad_query, grad_key, part_x, grad_w, grad_conv = pl.pallas_call(
        hand_over,
        out_shape=tuple(jax.ShapeDtypeStruct(a.shape, a.dtype) for a in results),
        in_specs=[vmem] * len(results),
        out_specs=(kept,) * len(results),
        scratch_shapes=[pltpu.SemaphoreType.DMA((len(results),))],
    )(*results)
    grad_x = lax.psum_scatter(part_x[None], "head", scatter_dimension=2, tiled=True)
    return attn_out[None], grad_query[None], grad_key[None], grad_x, grad_w, grad_conv


def solution(mesh):
    placed = (
        P(("parts", "rep"), "seq", "head"),
        P(("seq", "rep"), "head"),
        P(("parts", "rep"), "seq", "head"),
        P(("parts", "rep"), "seq", "head"),
        P(("parts", "rep"), "seq", "head"),
        P(None, None, "head"),
        P(("parts", "rep"), "head", "seq"),
    )
    return jax.shard_map(
        functools.partial(local, mesh.shape["seq"], mesh.shape["rep"]),
        mesh=mesh,
        in_specs=placed,
        out_specs=(
            P(("parts", "rep"), "seq", "head"),
            P(("parts", "rep"), "seq", "head"),
            P(("parts", "rep"), "seq", "head"),
            P(("parts", "rep"), "seq", "head"),
            P(("parts", "seq", "rep"), "head"),
            P("parts", None, "head"),
        ),
        check_vma=False,
    )
```

```python
import functools
import math

import jax
import jax.numpy as jnp
from jax import lax
from jax.experimental import pallas as pl
from jax.experimental.pallas import tpu as pltpu
from jax.sharding import PartitionSpec as P

EPSILON = 1e-06
EDGE = 16
LAG = 3
TWIN_LAG = 3
W_SKEW = 0
G_SKEW = 2
SWAP_EVERY = 4
TILE = 512
F32 = jnp.float32
BF16 = jnp.bfloat16


def dot(a, b):
    return lax.dot_general(a, b, (((1,), (0,)), ((), ())), preferred_element_type=F32)


def dot_t(a, b):
    return lax.dot_general(a, b, (((1,), (1,)), ((), ())), preferred_element_type=F32)


def kernel(n, reps, parts, scale, *refs):
    (act, w, q, k, go, ck, lg) = refs[:7]
    (ao, gq, gk, px, gw, gc) = refs[7:13]
    (
        acta, wg, vout, vr, qkh, xf, cumr, rise, shrink, mx, qh, kh, vh, gh, lhs1, lhs2, kt, qt, rsv,
        sums, sin, sout, po, phs, phr, actt, actc, gvg, gxi, pxf, pxs, pxi, gws, gwi, gwa,
        gcp, gca, gcb, gcf,
        wxs, wxr, axs, axr, ahs, ahr, qhs, qhr, gas, gar, wys, wms, vxs, vxr, ats, atr, ss, sr, phss, phsr,
        gxs, gxr, pxss, pxsr, gwss, gwsr, cs1, cr1, cs2, cr2, cs3, cr3,
    ) = refs[13:]
    T, F = act.shape
    FB, C = w.shape
    H = lg.shape[0]
    D = C // H
    TH = T + EDGE
    NW, _, _, CW = wg.shape
    NM, _, CC = vout.shape
    NT, _, _, CT = gvg.shape
    half = C // reps
    NH = NT // reps
    UP = 2 * H // n
    me = lax.axis_index("seq")
    r = lax.axis_index("rep")
    y = lax.axis_index("parts")
    mate = me + 1 - 2 * lax.rem(me, 2)
    first, last = me == 0, me == n - 1
    right, left = lax.rem(me + 1, n), lax.rem(me + n - 1, n)

    def peer(d):
        return lax.rem(r + d, reps)

    def remote(src, dst, send, recv, seq, rep, part=None):
        return pltpu.make_async_remote_copy(
            src_ref=src, dst_ref=dst, send_sem=send, recv_sem=recv,
            device_id={"parts": y if part is None else part, "seq": seq, "rep": rep},
            device_id_type=pl.DeviceIdType.MESH,
        )

    def lanes(h):
        return pl.ds(pl.multiple_of(h * D, D), D)

    barrier = pltpu.get_barrier_semaphore()
    for ds in range(n):
        for dr in range(reps):
            if ds or dr:
                pl.semaphore_signal(
                    barrier, inc=1, device_id={"seq": lax.rem(me + ds, n), "rep": peer(dr)},
                    device_id_type=pl.DeviceIdType.MESH,
                )
    for dy in range(1, parts):
        pl.semaphore_signal(
            barrier, inc=1, device_id={"parts": lax.rem(y + dy, parts)}, device_id_type=pl.DeviceIdType.MESH
        )

    total = lg[...]
    place = lax.broadcasted_iota(jnp.int32, total.shape, 1)
    distance = 1
    while distance < T:
        moved = pltpu.roll(total, distance, 1)
        total = total + jnp.where(place >= distance, moved, 0.0)
        distance *= 2
    cumr[...] = total
    columns = jnp.concatenate([total, jnp.zeros((T - H, T), F32)], axis=0).T
    for h in range(H):
        rise[h] = jnp.broadcast_to(columns[:, h : h + 1], (T, D))

    for m in range(NM):
        c = m * parts + y
        wg[c, me, pl.ds(r * FB, FB), :] = w[:, pl.ds(pl.multiple_of(r * half + c * CW, CW), CW)]
    acta[pl.ds(r * TH + EDGE, T), :] = act[...]

    @pl.when(first)
    def _():
        for d in range(reps):
            acta[pl.ds(d * TH, EDGE), :] = jnp.zeros((EDGE, F), BF16)
        qkh[...] = jnp.zeros(qkh.shape, BF16)
        sin[0] = jnp.zeros(sin.shape[1:], BF16)
        sin[2] = jnp.zeros(sin.shape[1:], BF16)

    @pl.when(last)
    def _():
        sin[1] = jnp.zeros(sin.shape[1:], BF16)
        sin[3] = jnp.zeros(sin.shape[1:], BF16)
        phr[...] = jnp.zeros(phr.shape, BF16)

    pl.semaphore_wait(barrier, n * reps - 1 + parts - 1)

    def w_swap(m, d):
        to, c = peer(d), m * parts + y
        return remote(
            w.at[:, pl.ds(pl.multiple_of(to * half + c * CW, CW), CW)],
            wg.at[c, me, pl.ds(r * FB, FB), :], wxs.at[m, d - 1], wxr.at[m, d - 1], me, to,
        )

    def act_swap(d):
        return remote(act, acta.at[pl.ds(r * TH + EDGE, T), :], axs.at[d - 1], axr.at[d - 1], me, peer(d))

    def act_edge(d):
        return remote(
            act.at[pl.ds(T - EDGE, EDGE), :], acta.at[pl.ds(r * TH, EDGE), :], ahs.at[d], ahr.at[d], right, peer(d)
        )

    def qk_edge(i):
        return remote((q, k)[i].at[pl.ds(T - EDGE, EDGE), :], qkh.at[i], qhs.at[i], qhr.at[i], right, r)

    for d in range(1, reps):
        w_swap(0, d).start()

    @pl.when(jnp.logical_not(last))
    def _():
        for i in range(2):
            qk_edge(i).start()

    for m in range(1, NM):
        for d in range(1, reps):
            w_swap(m, d).start()
    for d in range(1, reps):
        act_swap(d).start()

    @pl.when(jnp.logical_not(last))
    def _():
        for d in range(reps):
            act_edge(d).start()

    def hop(buf, c, m, o, way):
        mark = jnp.where(o == me, n, o) if way else o
        return remote(buf.at[c, o], buf.at[c, o], gas.at[m, mark], gar.at[c, o], (right, left)[way], r)

    def own(buf, c, m):
        @pl.when(jnp.logical_not(last))
        def _():
            hop(buf, c, m, me, 0).start()

        @pl.when(jnp.logical_not(first))
        def _():
            hop(buf, c, m, me, 1).start()

    def pass_on(buf, c, m, t, seen=None):
        lower, upper = me - t, me + t

        @pl.when(lower >= 0)
        def _():
            hop(buf, c, m, lower, 0).wait_recv()

            @pl.when(jnp.logical_not(last))
            def _():
                hop(buf, c, m, lower, 0).start()

            if seen is not None:
                seen(lower)

        @pl.when(upper < n)
        def _():
            hop(buf, c, m, upper, 1).wait_recv()

            @pl.when(jnp.logical_not(first))
            def _():
                hop(buf, c, m, upper, 1).start()

            if seen is not None:
                seen(upper)

    def sent(buf, chunks):
        def one(i, _):
            c, o = i // n, lax.rem(i, n)

            @pl.when(jnp.logical_and(jnp.logical_not(last), o <= me))
            def _():
                hop(buf, c, c, o, 0).wait_send()

            @pl.when(jnp.logical_and(jnp.logical_not(first), o >= me))
            def _():
                hop(buf, c, c, o, 1).wait_send()

            return 0

        lax.fori_loop(0, chunks * n, one, 0)

    def to_twin(m, dy, o):
        c = m * parts + y
        return remote(wg.at[c, o], wg.at[c, o], wys.at[dy - 1, m], gar.at[c, o], me, r, lax.rem(y + dy, parts))

    def to_mate(m, dy, o):
        c = m * parts + lax.rem(y + dy, parts)
        return remote(wg.at[c, o], wg.at[c, o], wms.at[dy - 1, m], gar.at[c, o], mate, r)

    def filtered(i, x, taps):
        out = taps[0:1] * x[i, EDGE : EDGE + T]
        for j in range(1, 4):
            out = out + taps[j : j + 1] * x[i, EDGE - j : EDGE - j + T]
        return out.astype(BF16)

    def load_rows(i, h):
        if i < 2:
            xf[i, 0:EDGE] = qkh[i, :, lanes(h)].astype(F32)
            xf[i, EDGE:] = (q, k)[i][:, lanes(h)].astype(F32)
        else:
            per = CC // D
            xf[i] = vr[h // per, :, pl.ds(pl.multiple_of(lax.rem(h, per) * D, D), D)].astype(F32)

    def prepare(h):
        cc = rise[h]
        fin = cc[T - 1 : T]
        rising = jnp.exp(cc)
        shrinking = jnp.exp(fin - cc)
        mixing = jnp.exp(-jnp.abs(cc - cumr[pl.ds(h, 1), :]))
        rise[h] = rising
        shrink[h] = shrinking
        mx[h] = mixing
        for i in range(2):
            load_rows(i, h)
        qv = filtered(0, xf, ck[0, :, lanes(h)])
        kv = filtered(1, xf, ck[1, :, lanes(h)])
        qh[h] = qv
        kh[h] = kv
        qf, kf = qv.astype(F32), kv.astype(F32)
        rq, sq = (rising * qf), (shrinking * qf)
        rk, sk = (rising * kf), (shrinking * kf)
        lhs1[h, :, 0:D] = (mixing * dot_t(qv, kv)).astype(BF16)
        lhs1[h, :, D : 2 * D] = rq.astype(BF16)
        lhs1[h, :, 2 * D :] = sq.astype(BF16)
        lhs2[h, :, 0:D] = (mixing * dot_t(kv, qv)).astype(BF16)
        lhs2[h, :, D : 2 * D] = rk.astype(BF16)
        lhs2[h, :, 2 * D :] = sk.astype(BF16)
        qt[h, 0:D] = sq.T.astype(BF16)
        qt[h, D:] = rq.T.astype(BF16)
        kt[h, 0:D] = sk.T.astype(BF16)
        kt[h, D:] = rk.T.astype(BF16)

    def turn(b):
        rows = pl.ds(pl.multiple_of(b * T, T), T)
        actt[rows, :] = act[:, rows].astype(F32).T.astype(BF16)

    def ready(m):
        for d in range(1, reps):
            w_swap(m, d).wait_recv()
        own(wg, m * parts + y, m)
        for dy in range(1, parts):
            to_twin(m, dy, me).start()

    def v_swap(c, d):
        to = peer(d)
        return remote(
            vout.at[c, pl.ds(to * TH, TH), :], vr.at[r * NM + c], vxs.at[c, d - 1], vxr.at[c, d - 1], me, to
        )

    @pl.when(jnp.logical_not(first))
    def _():
        for i in range(2):
            qk_edge(i).wait_recv()

    def jobs(work, count, step, steps):
        per = -(-count // steps)
        for j in range(per):
            @pl.when(step * per + j < count)
            def _():
                work(step * per + j)

    W_STEPS = n + TWIN_LAG + W_SKEW * (NM - 1)

    def w_step(s, _):
        for m in range(NM):
            t = s - W_SKEW * m

            @pl.when(t == 0)
            def _():
                ready(m)

            def twins(o):
                @pl.when(lax.rem(t, 2) == 0)
                def _():
                    for dy in range(1, parts):
                        to_twin(m, dy, o).start()

            @pl.when(jnp.logical_and(t >= 1, t < n))
            def _():
                pass_on(wg, m * parts + y, m, t, twins)

            for dy in range(1, parts):
                for near, source in ((True, me), (False, mate)):
                    u = t - (TWIN_LAG if near else TWIN_LAG + 1)

                    def take(o):
                        to_mate(m, dy, o).wait_recv()
                        if near:
                            to_mate(m, dy, o).start()

                    def even(ok):
                        return jnp.logical_and(jnp.logical_and(u >= 0, u < n), jnp.logical_and(lax.rem(u, 2) == 0, ok))

                    @pl.when(even(source - u >= 0))
                    def _():
                        take(source - u)

                    @pl.when(even(jnp.logical_and(u > 0, source + u < n)))
                    def _():
                        take(source + u)

            @pl.when(t == n - 1 + TWIN_LAG)
            def _():
                if m == 0:
                    for d in range(1, reps):
                        act_swap(d).wait_recv()

                    @pl.when(jnp.logical_not(first))
                    def _():
                        for d in range(reps):
                            act_edge(d).wait_recv()

                columns_of = [wg[m * parts + j].reshape(F, CW) for j in range(parts)]
                vout[m] = dot(acta[...], jnp.concatenate(columns_of, axis=1)).astype(BF16)
                for d in range(1, reps):
                    v_swap(m, d).start()
                vr[r * NM + m] = vout[m, pl.ds(r * TH, TH), :]

        jobs(prepare, H, s, n)
        jobs(turn, F // T, s, n)
        return 0

    lax.fori_loop(0, W_STEPS, w_step, 0)

    def a_swap(d):
        to = lax.rem(me + d, n)
        return remote(
            actt.at[pl.ds(to * reps * FB, reps * FB), :], actc.at[:, pl.ds(pl.multiple_of(me * T, T), T)],
            ats.at[0], atr.at[d - 1], to, r,
        )

    def a_swap_from(d):
        source = lax.rem(me + n - d, n)
        return remote(
            actt.at[pl.ds(0, reps * FB), :], actc.at[:, pl.ds(pl.multiple_of(source * T, T), T)],
            ats.at[0], atr.at[d - 1], source, r,
        )

    actc[:, pl.ds(pl.multiple_of(me * T, T), T)] = actt[pl.ds(me * reps * FB, reps * FB), :]

    def v_arrival(c, d):
        source = lax.rem(r + reps - d, reps)
        return remote(
            vout.at[c, pl.ds(0, TH), :], vr.at[source * NM + c], vxs.at[c, d - 1], vxr.at[c, d - 1], me, source
        )

    for c in range(NM):
        for d in range(1, reps):
            v_arrival(c, d).wait_recv()

    def values(h):
        load_rows(2, h)
        v = filtered(2, xf, ck[2, :, lanes(h)])
        vh[h] = v
        vf = v.astype(F32)
        rsv[h, :, 0:D] = (rise[h] * vf).astype(BF16)
        rsv[h, :, D:] = (shrink[h] * vf).astype(BF16)
        both = dot(kt[h], v)
        sums[0, h] = both[0:D]
        sums[1, h] = both[D:]

    def message(i, h):
        return remote(sout.at[i, h], sin.at[i, h], ss.at[i], sr.at[i, h], (right, left)[i % 2], r)

    def carry(i, h):
        begins, ends = ((first, last), (last, first))[i % 2]

        @pl.when(jnp.logical_not(begins))
        def _():
            message(i, h).wait_recv()

        @pl.when(jnp.logical_not(ends))
        def _():
            decay = rise[h, T - 1 : T]
            sout[i, h] = (decay * sin[i, h].astype(F32) + sums[i, h]).astype(BF16)
            message(i, h).start()

    def attend(h):
        v, before, after = vh[h], sin[0, h], sin[1, h]
        attn = dot(lhs1[h], jnp.concatenate([v, before, after], axis=0))
        inverse = lax.rsqrt(jnp.mean(attn * attn, axis=1, keepdims=True) + EPSILON)
        normed = attn * inverse
        ao[:, lanes(h)] = normed.astype(BF16)
        up = go[:, lanes(h)].astype(F32)
        g = ((up - normed * jnp.mean(up * normed, axis=1, keepdims=True)) * inverse).astype(BF16)
        gh[h] = g
        both = dot(qt[h], g)
        sums[2, h] = both[0:D]
        sums[3, h] = both[D:]

    def query_side(h):
        v, before, after, g, mixing = vh[h], sin[0, h], sin[1, h], gh[h], mx[h]
        gf = g.astype(F32)
        decayed = jnp.concatenate([(rise[h] * gf).astype(BF16), (shrink[h] * gf).astype(BF16)], axis=1)
        grad_scores = (mixing * dot_t(g, v)).astype(BF16)
        grad_scores_t = (mixing * dot_t(v, g)).astype(BF16)
        po[0, h, 0:T] = dot(grad_scores, kh[h]) + dot_t(decayed, jnp.concatenate([before, after], axis=1))
        po[1, h, 0:T] = dot(grad_scores_t, qh[h])

    def key_side(h):
        before, after = sin[2, h], sin[3, h]
        po[1, h, 0:T] = po[1, h, 0:T] + dot_t(rsv[h], jnp.concatenate([before, after], axis=1))
        po[2, h, 0:T] = dot(lhs2[h], jnp.concatenate([gh[h], before, after], axis=0))
        rows = []
        for i in range(3):
            load_rows(i, h)
            post = po[i, h, 0:T]
            phs[i, h] = post[0:EDGE].astype(BF16)
            for j in range(4):
                rows.append(jnp.sum(post * xf[i, EDGE - j : EDGE - j + T], axis=0, keepdims=True))
        zero = jnp.zeros((4, D), F32)
        gcp[2 * h] = jnp.concatenate(rows[0:8], axis=0)
        gcp[2 * h + 1] = jnp.concatenate(rows[8:12] + [zero], axis=0)

    far = (n - 1) * LAG

    def scan_step(s, _):
        def at(h, work):
            @pl.when(jnp.logical_and(h >= 0, h < H))
            def _():
                work(h)

        @pl.when(jnp.logical_and(lax.rem(s, SWAP_EVERY) == SWAP_EVERY - 1, s // SWAP_EVERY + 1 < n))
        def _():
            a_swap(s // SWAP_EVERY + 1).start()

        at(s, values)
        at(s - me * LAG, functools.partial(carry, 0))
        at(s - (n - 1 - me) * LAG, functools.partial(carry, 1))
        at(s - far, attend)
        at(s - far - me * LAG, functools.partial(carry, 2))
        at(s - far - (n - 1 - me) * LAG, functools.partial(carry, 3))
        at(s - far, query_side)
        at(s - 2 * far, key_side)
        return 0

    lax.fori_loop(0, H + 2 * far, scan_step, 0)

    def post_edge(i):
        return remote(phs.at[i], phr.at[i], phss.at[i], phsr.at[i], left, r)

    @pl.when(jnp.logical_not(first))
    def _():
        for i in (2, 0, 1):
            post_edge(i).start()

    def taps_out(d):
        to = lax.rem(me + d, n)
        return remote(gcp.at[pl.ds(to * UP, UP)], gca.at[me], cs1.at[0], cr1.at[d - 1], to, r)

    def taps_in(d):
        source = lax.rem(me + n - d, n)
        return remote(gcp.at[pl.ds(0, UP)], gca.at[source], cs1.at[0], cr1.at[d - 1], source, r)

    def taps_swap(d):
        return remote(gcb.at[r], gcb.at[r], cs2.at[d - 1], cr2.at[d - 1], me, peer(d))

    def taps_swap_in(d):
        source = lax.rem(r + reps - d, reps)
        return remote(gcb.at[r], gcb.at[source], cs2.at[d - 1], cr2.at[d - 1], me, source)

    def taps_back(d):
        to = lax.rem(me + d, n)
        return remote(gcf.at[pl.ds(me * UP, UP)], gcf.at[pl.ds(me * UP, UP)], cs3.at[0], cr3.at[d - 1], to, r)

    def taps_back_in(d):
        source = lax.rem(me + n - d, n)
        return remote(
            gcf.at[pl.ds(me * UP, UP)], gcf.at[pl.ds(source * UP, UP)], cs3.at[0], cr3.at[d - 1], source, r
        )

    for d in range(1, n):
        taps_out(d).start()
    gca[me] = gcp[pl.ds(me * UP, UP)]

    def back(i, h):
        po[i, h, T : T + 8] = phr[i, h].astype(F32)[0:8]
        taps = ck[i, :, lanes(h)]
        out = taps[0:1] * po[i, h, 0:T]
        for j in range(1, 4):
            out = out + taps[j : j + 1] * po[i, h, j : j + T]
        return out.astype(BF16)

    @pl.when(jnp.logical_not(last))
    def _():
        post_edge(2).wait_recv()

    def weight_sent(i, _):
        m, o = i // n, lax.rem(i, n)
        c = m * parts + y

        @pl.when(jnp.logical_and(jnp.logical_not(last), o <= me))
        def _():
            hop(wg, c, m, o, 0).wait_send()

        @pl.when(jnp.logical_and(jnp.logical_not(first), o >= me))
        def _():
            hop(wg, c, m, o, 1).wait_send()

        return 0

    lax.fori_loop(0, NM * n, weight_sent, 0)

    for c in range(NT):
        for j in range(CT // D):
            gvg[c, me, :, j * D : (j + 1) * D] = back(2, c * (CT // D) + j)
        if c == 0:
            own(gvg, c, c)

    def gx_swap(j, d):
        to = peer(d)
        return remote(gvg.at[to * NH + j, me], gxi.at[r, j], gxs.at[j, d - 1], gxr.at[j, d - 1], me, to)

    def gx_swap_in(j, d):
        source = lax.rem(r + reps - d, reps)
        return remote(gvg.at[j, me], gxi.at[source, j], gxs.at[j, d - 1], gxr.at[j, d - 1], me, source)

    for j in range(NH):
        for d in range(1, reps):
            gx_swap(j, d).start()
        gxi[r, j] = gvg[r * NH + j, me]

    @pl.when(jnp.logical_not(last))
    def _():
        for i in range(2):
            post_edge(i).wait_recv()

    def input_grad(b):
        rows = wg.shape[2]
        per = TILE // rows
        out = jnp.zeros((reps * T, TILE), F32)
        for m in range(NM):
            j, at = divmod(m * CC, CT)
            x = gxi[:, j, :, at : at + CC].reshape(reps * T, CC)
            rows_of = [wg[m * parts + i, pl.ds(b * per, per)].reshape(TILE, CW) for i in range(parts)]
            out = out + dot_t(x, jnp.concatenate(rows_of, axis=1))
        cols = pl.ds(pl.multiple_of(b * TILE, TILE), TILE)
        for i in range(reps):
            pxf[i, :, cols] = out[i * T : (i + 1) * T]
            pxs[i, :, cols] = out[i * T : (i + 1) * T].astype(BF16)

    def px_swap(d):
        to = peer(d)
        return remote(pxs.at[to], pxi.at[d - 1], pxss.at[d - 1], pxsr.at[d - 1], me, to)

    def gw_swap(c, d):
        to = peer(d)
        return remote(gws.at[c, pl.ds(to * FB, FB), :], gwi.at[c, d - 1], gwss.at[c, d - 1], gwsr.at[c, d - 1], me, to)

    X_TILES = F // TILE
    G_STEPS = n + G_SKEW * (NT - 1)

    def both_back(h):
        gq[:, lanes(h)] = back(0, h)
        gk[:, lanes(h)] = back(1, h)

    def last_step(s, _):
        for c in range(NT):
            t = s - G_SKEW * c
            if c:
                @pl.when(t == 0)
                def _():
                    own(gvg, c, c)

            @pl.when(jnp.logical_and(t >= 1, t < n))
            def _():
                pass_on(gvg, c, c, t)

            @pl.when(t == n - 1)
            def _():
                if c == 0:
                    for d in range(1, n):
                        a_swap_from(d).wait_recv()

                gwa[c] = dot(actc[...], gvg[c].reshape(n * T, CT))
                gws[c] = gwa[c].astype(BF16)
                for d in range(1, reps):
                    gw_swap(c, d).start()

        jobs(both_back, H, s, n)

        @pl.when(s == 1)
        def _():
            for d in range(1, n):
                taps_in(d).wait_recv()
            part = gca[0]
            for o in range(1, n):
                part = part + gca[o]
            gcb[r] = part
            for d in range(1, reps):
                taps_swap(d).start()

        @pl.when(s == 3)
        def _():
            for d in range(1, reps):
                taps_swap_in(d).wait_recv()
            part = gcb[0]
            for o in range(1, reps):
                part = part + gcb[o]
            gcf[pl.ds(me * UP, UP)] = part * scale
            for d in range(1, n):
                taps_back(d).start()

        @pl.when(s == 2)
        def _():
            for j in range(NH):
                for d in range(1, reps):
                    gx_swap_in(j, d).wait_recv()

        @pl.when(jnp.logical_and(s >= 3, s < 3 + X_TILES))
        def _():
            input_grad(s - 3)

        @pl.when(s == 3 + X_TILES)
        def _():
            for d in range(1, reps):
                px_swap(d).start()

        return 0

    lax.fori_loop(0, G_STEPS, last_step, 0)
    for d in range(1, reps):
        px_swap(d).wait_recv()
    out = pxf[r]
    for d in range(1, reps):
        out = out + pxi[d - 1].astype(F32)
    px[...] = out.astype(BF16)
    for d in range(1, n):
        taps_back_in(d).wait_recv()
    for h in range(H):
        gc[0, :, h * D : (h + 1) * D] = gcf[2 * h, 0:4]
        gc[1, :, h * D : (h + 1) * D] = gcf[2 * h, 4:8]
        gc[2, :, h * D : (h + 1) * D] = gcf[2 * h + 1, 0:4]
    for c in range(NT):
        for d in range(1, reps):
            gw_swap(c, d).wait_recv()
        out = gwa[c, pl.ds(r * FB, FB), :]
        for d in range(1, reps):
            out = out + gwi[c, d - 1].astype(F32)
        gw[:, c * CT : (c + 1) * CT] = out * scale

    for d in range(1, reps):
        act_swap(d).wait_send()
        px_swap(d).wait_send()
        taps_swap(d).wait_send()
        for m in range(NM):
            w_swap(m, d).wait_send()
            v_swap(m, d).wait_send()
        for c in range(NT):
            gw_swap(c, d).wait_send()
        for j in range(NH):
            gx_swap(j, d).wait_send()
    for dy in range(1, parts):
        for m in range(NM):
            blocks = wg.at[m, pl.ds(0, n // 2)]
            remote(blocks, blocks, wys.at[dy - 1, m], gar.at[0, 0], me, r, lax.rem(y + dy, parts)).wait_send()
            remote(blocks, blocks, wms.at[dy - 1, m], gar.at[0, 0], mate, r).wait_send()
    others = actt.at[pl.ds(0, (n - 1) * reps * FB), :]
    remote(others, others, ats.at[0], atr.at[0], right, r).wait_send()
    others = gcp.at[pl.ds(0, (n - 1) * UP)]
    remote(others, others, cs1.at[0], cr1.at[0], right, r).wait_send()
    remote(others, others, cs3.at[0], cr3.at[0], right, r).wait_send()

    @pl.when(jnp.logical_not(last))
    def _():
        for i in range(2):
            qk_edge(i).wait_send()
        for d in range(reps):
            act_edge(d).wait_send()

    @pl.when(jnp.logical_not(first))
    def _():
        for i in range(3):
            post_edge(i).wait_send()

    sent(gvg, NT)
    for i in range(4):
        @pl.when(jnp.logical_not((last, first)[i % 2]))
        def _():
            remote(sout.at[i], sin.at[i], ss.at[i], sr.at[i, 0], (right, left)[i % 2], r).wait_send()


def hand_over(*refs):
    count = len(refs) // 2
    sems = refs[-1]
    copies = [pltpu.make_async_copy(refs[i], refs[count + i], sems.at[i]) for i in range(count)]
    for copy in copies:
        copy.start()
    for copy in copies:
        copy.wait()


def local(n, reps, parts, activations, value_weight, query_in, key_in, grad_out, conv_kernel, log_gate):
    act = lax.all_gather(activations, "head", axis=2, tiled=True)[0]
    T, F = act.shape
    FB, C = value_weight.shape
    H = log_gate.shape[1]
    D = C // H
    TH = T + EDGE
    CW = D
    CC = CW * parts
    CT = min(512, C // reps)
    NW, NM, NT = C // reps // CW, C // reps // CC, C // CT
    NH = NT // reps
    UP = 2 * H // n
    scale = 1.0 / math.sqrt(n * reps * T)
    dma = pltpu.SemaphoreType.DMA
    peers = max(reps - 1, 1)
    scratch = [
        pltpu.VMEM((reps * TH, F), BF16),
        pltpu.VMEM((NW, n, reps * FB, CW), BF16),
        pltpu.VMEM((NM, reps * TH, CC), BF16),
        pltpu.VMEM((reps * NM, TH, CC), BF16),
        pltpu.VMEM((2, EDGE, C), BF16),
        pltpu.VMEM((3, TH, D), F32),
        pltpu.VMEM((H, T), F32),
        pltpu.VMEM((H, T, D), F32),
        pltpu.VMEM((H, T, D), F32),
        pltpu.VMEM((H, T, T), F32),
        pltpu.VMEM((H, T, D), BF16),
        pltpu.VMEM((H, T, D), BF16),
        pltpu.VMEM((H, T, D), BF16),
        pltpu.VMEM((H, T, D), BF16),
        pltpu.VMEM((H, T, 3 * D), BF16),
        pltpu.VMEM((H, T, 3 * D), BF16),
        pltpu.VMEM((H, 2 * D, T), BF16),
        pltpu.VMEM((H, 2 * D, T), BF16),
        pltpu.VMEM((H, T, 2 * D), BF16),
        pltpu.VMEM((4, H, D, D), F32),
        pltpu.VMEM((4, H, D, D), BF16),
        pltpu.VMEM((4, H, D, D), BF16),
        pltpu.VMEM((3, H, T + 8, D), F32),
        pltpu.VMEM((3, H, EDGE, D), BF16),
        pltpu.VMEM((3, H, EDGE, D), BF16),
        pltpu.VMEM((F, T), BF16),
        pltpu.VMEM((reps * FB, n * T), BF16),
        pltpu.VMEM((NT, n, T, CT), BF16),
        pltpu.VMEM((reps, NH, T, CT), BF16),
        pltpu.VMEM((reps, T, F), F32),
        pltpu.VMEM((reps, T, F), BF16),
        pltpu.VMEM((peers, T, F), BF16),
        pltpu.VMEM((NT, reps * FB, CT), BF16),
        pltpu.VMEM((NT, peers, FB, CT), BF16),
        pltpu.VMEM((NT, reps * FB, CT), F32),
        pltpu.VMEM((n * UP, 8, D), F32),
        pltpu.VMEM((n, UP, 8, D), F32),
        pltpu.VMEM((reps, UP, 8, D), F32),
        pltpu.VMEM((n * UP, 8, D), F32),
        dma((NM, peers)), dma((NM, peers)),
        dma((peers,)), dma((peers,)),
        dma((reps,)), dma((reps,)),
        dma((2,)), dma((2,)),
        dma((max(NM, NT), n + 1)), dma((max(NW, NT), n)),
        dma((max(parts - 1, 1), NM)), dma((max(parts - 1, 1), NM)),
        dma((NM, peers)), dma((NM, peers)),
        dma((1,)), dma((n - 1,)),
        dma((4,)), dma((4, H)),
        dma((3,)), dma((3,)),
        dma((NH, peers)), dma((NH, peers)),
        dma((peers,)), dma((peers,)),
        dma((NT, peers)), dma((NT, peers)),
        dma((1,)), dma((n - 1,)),
        dma((peers,)), dma((peers,)),
        dma((1,)), dma((n - 1,)),
    ]
    vmem = pl.BlockSpec(memory_space=pltpu.VMEM)
    results = pl.pallas_call(
        functools.partial(kernel, n, reps, parts, scale),
        out_shape=(
            jax.ShapeDtypeStruct((T, C), BF16),
            jax.ShapeDtypeStruct((T, C), BF16),
            jax.ShapeDtypeStruct((T, C), BF16),
            jax.ShapeDtypeStruct((T, F), BF16),
            jax.ShapeDtypeStruct((FB, C), F32),
            jax.ShapeDtypeStruct(conv_kernel.shape, F32),
        ),
        in_specs=[vmem] * 7,
        out_specs=[vmem] * 6,
        scratch_shapes=scratch,
        compiler_params=pltpu.CompilerParams(
            collective_id=0, has_side_effects=True, vmem_limit_bytes=60 * 2**20
        ),
        cost_estimate=pl.CostEstimate(flops=5 * 10**9, bytes_accessed=8 * 2**20, transcendentals=10**6),
    )(act, value_weight, query_in[0], key_in[0], grad_out[0], conv_kernel, log_gate[0])
    kept = pl.BlockSpec(memory_space=pl.ANY)
    attn_out, grad_query, grad_key, part_x, grad_w, grad_conv = pl.pallas_call(
        hand_over,
        out_shape=tuple(jax.ShapeDtypeStruct(a.shape, a.dtype) for a in results),
        in_specs=[vmem] * len(results),
        out_specs=(kept,) * len(results),
        scratch_shapes=[pltpu.SemaphoreType.DMA((len(results),))],
    )(*results)
    grad_x = lax.psum_scatter(part_x[None], "head", scatter_dimension=2, tiled=True)
    return attn_out[None], grad_query[None], grad_key[None], grad_x, grad_w, grad_conv


def solution(mesh):
    placed = (
        P(("parts", "rep"), "seq", "head"),
        P(("seq", "rep"), "head"),
        P(("parts", "rep"), "seq", "head"),
        P(("parts", "rep"), "seq", "head"),
        P(("parts", "rep"), "seq", "head"),
        P(None, None, "head"),
        P(("parts", "rep"), "head", "seq"),
    )
    return jax.shard_map(
        functools.partial(local, mesh.shape["seq"], mesh.shape["rep"], mesh.shape["parts"]),
        mesh=mesh,
        in_specs=placed,
        out_specs=(
            P(("parts", "rep"), "seq", "head"),
            P(("parts", "rep"), "seq", "head"),
            P(("parts", "rep"), "seq", "head"),
            P(("parts", "rep"), "seq", "head"),
            P(("parts", "seq", "rep"), "head"),
            P("parts", None, "head"),
        ),
        check_vma=False,
    )
```

```python
import functools
import math

import jax
import jax.numpy as jnp
from jax import lax
from jax.experimental import pallas as pl
from jax.experimental.pallas import tpu as pltpu
from jax.sharding import PartitionSpec as P

EPSILON = 1e-06
EDGE = 16
LAG = 4
TWIN_LAG = 3
W_SKEW = 0
G_SKEW = 2
SWAP_EVERY = 5
EDGE_LAG = 5
TILE = 512
F32 = jnp.float32
BF16 = jnp.bfloat16


def dot(a, b):
    return lax.dot_general(a, b, (((1,), (0,)), ((), ())), preferred_element_type=F32)


def dot_t(a, b):
    return lax.dot_general(a, b, (((1,), (1,)), ((), ())), preferred_element_type=F32)


def kernel(n, reps, parts, scale, *refs):
    (act, w, q, k, go, ck, lg) = refs[:7]
    (ao, gq, gk, px, gw, gc) = refs[7:13]
    (
        acta, wg, vout, vr, qkh, xf, cumr, rise, shrink, mx, qh, kh, vh, gh, lhs1, lhs2, kt, qt, rsv,
        sums, sin, raw, sout, mates, kept, decays, po, phs, phr, actt, actc, gvg, gxi, pxf, pxs, pxi, gws, gwi, gwa,
        gcp, gca, gcb, gcf,
        wxs, wxr, axs, axr, ahs, ahr, qhs, qhr, gas, gar, wys, wms, vxs, vxr, ats, atr, dcs, dcr, ss, rr, fs, sr, ms, mr, phss, phsr, pvs, pvr,
        gxs, gxr, pxss, pxsr, gwss, gwsr, cs1, cr1, cs2, cr2, cs3, cr3,
    ) = refs[13:]
    T, F = act.shape
    FB, C = w.shape
    H = lg.shape[0]
    D = C // H
    TH = T + EDGE
    NW, _, _, CW = wg.shape
    NM, _, CC = vout.shape
    NT, _, _, CT = gvg.shape
    half = C // reps
    NH = NT // reps
    UP = 2 * H // n
    me = lax.axis_index("seq")
    r = lax.axis_index("rep")
    y = lax.axis_index("parts")
    odd = lax.rem(me, 2)
    mate = me + 1 - 2 * odd
    way, pair, pairs = 1 - odd, me // 2, n // 2
    lead = jnp.where(odd == 1, pair, pairs - 1 - pair)
    follow = pairs - 1 - lead
    onward = lax.rem(jnp.where(odd == 1, me + 2, me + n - 2), n)
    leads_first, leads_last, follows_first = lead == 0, lead == pairs - 1, follow == 0
    first, last = me == 0, me == n - 1
    right, left = lax.rem(me + 1, n), lax.rem(me + n - 1, n)

    def peer(d):
        return lax.rem(r + d, reps)

    def remote(src, dst, send, recv, seq, rep, part=None):
        return pltpu.make_async_remote_copy(
            src_ref=src, dst_ref=dst, send_sem=send, recv_sem=recv,
            device_id={"parts": y if part is None else part, "seq": seq, "rep": rep},
            device_id_type=pl.DeviceIdType.MESH,
        )

    def lanes(h):
        return pl.ds(pl.multiple_of(h * D, D), D)

    barrier = pltpu.get_barrier_semaphore()
    for ds in range(n):
        for dr in range(reps):
            if ds or dr:
                pl.semaphore_signal(
                    barrier, inc=1, device_id={"seq": lax.rem(me + ds, n), "rep": peer(dr)},
                    device_id_type=pl.DeviceIdType.MESH,
                )
    for dy in range(1, parts):
        pl.semaphore_signal(
            barrier, inc=1, device_id={"parts": lax.rem(y + dy, parts)}, device_id_type=pl.DeviceIdType.MESH
        )

    total = lg[...]
    place = lax.broadcasted_iota(jnp.int32, total.shape, 1)
    distance = 1
    while distance < T:
        moved = pltpu.roll(total, distance, 1)
        total = total + jnp.where(place >= distance, moved, 0.0)
        distance *= 2
    cumr[...] = total
    columns = jnp.concatenate([total, jnp.zeros((T - H, T), F32)], axis=0).T
    for h in range(H):
        rise[h] = jnp.broadcast_to(columns[:, h : h + 1], (T, D))

    for m in range(NM):
        c = m * parts + y
        wg[c, me, pl.ds(r * FB, FB), :] = w[:, pl.ds(pl.multiple_of(r * half + c * CW, CW), CW)]
    acta[pl.ds(r * TH + EDGE, T), :] = act[...]

    @pl.when(first)
    def _():
        for d in range(reps):
            acta[pl.ds(d * TH, EDGE), :] = jnp.zeros((EDGE, F), BF16)
        qkh[...] = jnp.zeros(qkh.shape, BF16)

    @pl.when(leads_first)
    def _():
        raw[...] = jnp.zeros(raw.shape, BF16)

    @pl.when(follows_first)
    def _():
        sin[1 - way] = jnp.zeros(sin.shape[1:], BF16)
        sin[3 - way] = jnp.zeros(sin.shape[1:], BF16)

    decays[0] = jnp.exp(jnp.broadcast_to(total[:, T - 1 : T], (H, D)))

    @pl.when(last)
    def _():
        phr[...] = jnp.zeros(phr.shape, BF16)

    pl.semaphore_wait(barrier, n * reps - 1 + parts - 1)

    def w_swap(m, d):
        to, c = peer(d), m * parts + y
        return remote(
            w.at[:, pl.ds(pl.multiple_of(to * half + c * CW, CW), CW)],
            wg.at[c, me, pl.ds(r * FB, FB), :], wxs.at[m, d - 1], wxr.at[m, d - 1], me, to,
        )

    def act_swap(d):
        return remote(act, acta.at[pl.ds(r * TH + EDGE, T), :], axs.at[d - 1], axr.at[d - 1], me, peer(d))

    def act_edge(d):
        return remote(
            act.at[pl.ds(T - EDGE, EDGE), :], acta.at[pl.ds(r * TH, EDGE), :], ahs.at[d], ahr.at[d], right, peer(d)
        )

    def qk_edge(i):
        return remote((q, k)[i].at[pl.ds(T - EDGE, EDGE), :], qkh.at[i], qhs.at[i], qhr.at[i], right, r)

    for d in range(1, reps):
        w_swap(0, d).start()

    decay_swap = remote(decays.at[0], decays.at[1], dcs.at[0], dcr.at[0], mate, r)
    decay_swap.start()

    @pl.when(jnp.logical_not(last))
    def _():
        for i in range(2):
            qk_edge(i).start()

    for m in range(1, NM):
        for d in range(1, reps):
            w_swap(m, d).start()
    for d in range(1, reps):
        act_swap(d).start()

    @pl.when(jnp.logical_not(last))
    def _():
        for d in range(reps):
            act_edge(d).start()

    def hop(buf, c, m, o, way):
        mark = jnp.where(o == me, n, o) if way else o
        return remote(buf.at[c, o], buf.at[c, o], gas.at[m, mark], gar.at[c, o], (right, left)[way], r)

    def own(buf, c, m):
        @pl.when(jnp.logical_not(last))
        def _():
            hop(buf, c, m, me, 0).start()

        @pl.when(jnp.logical_not(first))
        def _():
            hop(buf, c, m, me, 1).start()

    def pass_on(buf, c, m, t, seen=None):
        lower, upper = me - t, me + t

        @pl.when(lower >= 0)
        def _():
            hop(buf, c, m, lower, 0).wait_recv()

            @pl.when(jnp.logical_not(last))
            def _():
                hop(buf, c, m, lower, 0).start()

            if seen is not None:
                seen(lower)

        @pl.when(upper < n)
        def _():
            hop(buf, c, m, upper, 1).wait_recv()

            @pl.when(jnp.logical_not(first))
            def _():
                hop(buf, c, m, upper, 1).start()

            if seen is not None:
                seen(upper)

    def sent(buf, chunks):
        def one(i, _):
            c, o = i // n, lax.rem(i, n)

            @pl.when(jnp.logical_and(jnp.logical_not(last), o <= me))
            def _():
                hop(buf, c, c, o, 0).wait_send()

            @pl.when(jnp.logical_and(jnp.logical_not(first), o >= me))
            def _():
                hop(buf, c, c, o, 1).wait_send()

            return 0

        lax.fori_loop(0, chunks * n, one, 0)

    def to_twin(m, dy, o):
        c = m * parts + y
        return remote(wg.at[c, o], wg.at[c, o], wys.at[dy - 1, m], gar.at[c, o], me, r, lax.rem(y + dy, parts))

    def to_mate(m, dy, o):
        c = m * parts + lax.rem(y + dy, parts)
        return remote(wg.at[c, o], wg.at[c, o], wms.at[dy - 1, m], gar.at[c, o], mate, r)

    def filtered(i, x, taps):
        out = taps[0:1] * x[i, EDGE : EDGE + T]
        for j in range(1, 4):
            out = out + taps[j : j + 1] * x[i, EDGE - j : EDGE - j + T]
        return out.astype(BF16)

    def load_rows(i, h):
        if i < 2:
            xf[i, 0:EDGE] = qkh[i, :, lanes(h)].astype(F32)
            xf[i, EDGE:] = (q, k)[i][:, lanes(h)].astype(F32)
        else:
            per = CC // D
            xf[i] = vr[h // per, :, pl.ds(pl.multiple_of(lax.rem(h, per) * D, D), D)].astype(F32)

    def prepare(h):
        cc = rise[h]
        fin = cc[T - 1 : T]
        rising = jnp.exp(cc)
        shrinking = jnp.exp(fin - cc)
        mixing = jnp.exp(-jnp.abs(cc - cumr[pl.ds(h, 1), :]))
        rise[h] = rising
        shrink[h] = shrinking
        mx[h] = mixing
        for i in range(2):
            load_rows(i, h)
        qv = filtered(0, xf, ck[0, :, lanes(h)])
        kv = filtered(1, xf, ck[1, :, lanes(h)])
        qh[h] = qv
        kh[h] = kv
        qf, kf = qv.astype(F32), kv.astype(F32)
        rq, sq = (rising * qf), (shrinking * qf)
        rk, sk = (rising * kf), (shrinking * kf)
        lhs1[h, :, 0:D] = (mixing * dot_t(qv, kv)).astype(BF16)
        lhs1[h, :, D : 2 * D] = rq.astype(BF16)
        lhs1[h, :, 2 * D :] = sq.astype(BF16)
        lhs2[h, :, 0:D] = (mixing * dot_t(kv, qv)).astype(BF16)
        lhs2[h, :, D : 2 * D] = rk.astype(BF16)
        lhs2[h, :, 2 * D :] = sk.astype(BF16)
        qt[h, 0:D] = sq.T.astype(BF16)
        qt[h, D:] = rq.T.astype(BF16)
        kt[h, 0:D] = sk.T.astype(BF16)
        kt[h, D:] = rk.T.astype(BF16)

    def turn(b):
        rows = pl.ds(pl.multiple_of(b * T, T), T)
        actt[rows, :] = act[:, rows].astype(F32).T.astype(BF16)

    def ready(m):
        for d in range(1, reps):
            w_swap(m, d).wait_recv()
        own(wg, m * parts + y, m)
        for dy in range(1, parts):
            to_twin(m, dy, me).start()

    def v_swap(c, d):
        to = peer(d)
        return remote(
            vout.at[c, pl.ds(to * TH, TH), :], vr.at[r * NM + c], vxs.at[c, d - 1], vxr.at[c, d - 1], me, to
        )

    @pl.when(jnp.logical_not(first))
    def _():
        for i in range(2):
            qk_edge(i).wait_recv()

    def jobs(work, count, step, steps):
        per = -(-count // steps)
        for j in range(per):
            @pl.when(step * per + j < count)
            def _():
                work(step * per + j)

    W_STEPS = n + TWIN_LAG + W_SKEW * (NM - 1)

    def w_step(s, _):
        for m in range(NM):
            t = s - W_SKEW * m

            @pl.when(t == 0)
            def _():
                ready(m)

            def twins(o):
                @pl.when(lax.rem(t, 2) == 0)
                def _():
                    for dy in range(1, parts):
                        to_twin(m, dy, o).start()

            @pl.when(jnp.logical_and(t >= 1, t < n))
            def _():
                pass_on(wg, m * parts + y, m, t, twins)

            for dy in range(1, parts):
                for near, source in ((True, me), (False, mate)):
                    u = t - (TWIN_LAG if near else TWIN_LAG + 1)

                    def take(o):
                        to_mate(m, dy, o).wait_recv()
                        if near:
                            to_mate(m, dy, o).start()

                    def even(ok):
                        return jnp.logical_and(jnp.logical_and(u >= 0, u < n), jnp.logical_and(lax.rem(u, 2) == 0, ok))

                    @pl.when(even(source - u >= 0))
                    def _():
                        take(source - u)

                    @pl.when(even(jnp.logical_and(u > 0, source + u < n)))
                    def _():
                        take(source + u)

            @pl.when(t == n - 1 + TWIN_LAG)
            def _():
                if m == 0:
                    for d in range(1, reps):
                        act_swap(d).wait_recv()

                    @pl.when(jnp.logical_not(first))
                    def _():
                        for d in range(reps):
                            act_edge(d).wait_recv()

                columns_of = [wg[m * parts + j].reshape(F, CW) for j in range(parts)]
                vout[m] = dot(acta[...], jnp.concatenate(columns_of, axis=1)).astype(BF16)
                for d in range(1, reps):
                    v_swap(m, d).start()
                vr[r * NM + m] = vout[m, pl.ds(r * TH, TH), :]

        jobs(prepare, H, s, n)
        jobs(turn, F // T, s, n)
        return 0

    lax.fori_loop(0, W_STEPS, w_step, 0)

    def a_swap(d):
        to = lax.rem(me + d, n)
        return remote(
            actt.at[pl.ds(to * reps * FB, reps * FB), :], actc.at[:, pl.ds(pl.multiple_of(me * T, T), T)],
            ats.at[0], atr.at[d - 1], to, r,
        )

    def a_swap_from(d):
        source = lax.rem(me + n - d, n)
        return remote(
            actt.at[pl.ds(0, reps * FB), :], actc.at[:, pl.ds(pl.multiple_of(source * T, T), T)],
            ats.at[0], atr.at[d - 1], source, r,
        )

    actc[:, pl.ds(pl.multiple_of(me * T, T), T)] = actt[pl.ds(me * reps * FB, reps * FB), :]

    def v_arrival(c, d):
        source = lax.rem(r + reps - d, reps)
        return remote(
            vout.at[c, pl.ds(0, TH), :], vr.at[source * NM + c], vxs.at[c, d - 1], vxr.at[c, d - 1], me, source
        )

    for c in range(NM):
        for d in range(1, reps):
            v_arrival(c, d).wait_recv()

    decay_swap.wait_recv()

    def values(h):
        load_rows(2, h)
        v = filtered(2, xf, ck[2, :, lanes(h)])
        vh[h] = v
        vf = v.astype(F32)
        rsv[h, :, 0:D] = (rise[h] * vf).astype(BF16)
        rsv[h, :, D:] = (shrink[h] * vf).astype(BF16)
        both = dot(kt[h], v)
        sums[0, h] = both[0:D]
        sums[1, h] = both[D:]
        share(0, h)

    def message(j, h):
        return remote(sout.at[j, h], raw.at[j, h], ss.at[j], rr.at[j, h], onward, r)

    def hand_in(j, h, which):
        return remote(raw.at[j, h], sin.at[2 * j + which, h], fs.at[j], sr.at[j, h], mate, r)

    def mate_sum(j, h):
        return remote(mates.at[j, h], kept.at[j, h], ms.at[j], mr.at[j, h], mate, r)

    def share(j, h):
        mates[j, h] = sums[2 * j + 1 - way, h].astype(BF16)
        mate_sum(j, h).start()

    def carry(j, h):
        @pl.when(jnp.logical_not(leads_first))
        def _():
            message(j, h).wait_recv()
            hand_in(j, h, way).start()

        mate_sum(j, h).wait_recv()
        i = 2 * j + way
        state = decays[1, pl.ds(h, 1), :] * raw[j, h].astype(F32) + kept[j, h].astype(F32)
        sin[i, h] = state.astype(BF16)

        @pl.when(jnp.logical_not(leads_last))
        def _():
            sout[j, h] = (decays[0, pl.ds(h, 1), :] * state + sums[i, h]).astype(BF16)
            message(j, h).start()

    def handed(j, h):
        @pl.when(jnp.logical_not(follows_first))
        def _():
            hand_in(j, h, 1 - way).wait_recv()

    def attend(h):
        handed(0, h)
        v, before, after = vh[h], sin[0, h], sin[1, h]
        attn = dot(lhs1[h], jnp.concatenate([v, before, after], axis=0))
        inverse = lax.rsqrt(jnp.mean(attn * attn, axis=1, keepdims=True) + EPSILON)
        normed = attn * inverse
        ao[:, lanes(h)] = normed.astype(BF16)
        up = go[:, lanes(h)].astype(F32)
        g = ((up - normed * jnp.mean(up * normed, axis=1, keepdims=True)) * inverse).astype(BF16)
        gh[h] = g
        both = dot(qt[h], g)
        sums[2, h] = both[0:D]
        sums[3, h] = both[D:]
        share(1, h)

    def query_side(h):
        v, before, after, g, mixing = vh[h], sin[0, h], sin[1, h], gh[h], mx[h]
        gf = g.astype(F32)
        decayed = jnp.concatenate([(rise[h] * gf).astype(BF16), (shrink[h] * gf).astype(BF16)], axis=1)
        grad_scores = (mixing * dot_t(g, v)).astype(BF16)
        grad_scores_t = (mixing * dot_t(v, g)).astype(BF16)
        po[0, h, 0:T] = dot(grad_scores, kh[h]) + dot_t(decayed, jnp.concatenate([before, after], axis=1))
        po[1, h, 0:T] = dot(grad_scores_t, qh[h])

    def key_side(h):
        handed(1, h)
        before, after = sin[2, h], sin[3, h]
        po[1, h, 0:T] = po[1, h, 0:T] + dot_t(rsv[h], jnp.concatenate([before, after], axis=1))
        po[2, h, 0:T] = dot(lhs2[h], jnp.concatenate([gh[h], before, after], axis=0))
        rows = []
        for i in range(3):
            load_rows(i, h)
            post = po[i, h, 0:T]
            phs[i, h] = post[0:EDGE].astype(BF16)
            for j in range(4):
                rows.append(jnp.sum(post * xf[i, EDGE - j : EDGE - j + T], axis=0, keepdims=True))
        zero = jnp.zeros((4, D), F32)
        gcp[2 * h] = jnp.concatenate(rows[0:8], axis=0)
        gcp[2 * h + 1] = jnp.concatenate(rows[8:12] + [zero], axis=0)

    PER = CT // D

    def post_edge(i):
        return remote(phs.at[i], phr.at[i], phss.at[i], phsr.at[i], left, r)

    def value_edge(c):
        heads = pl.ds(c * PER, PER)
        return remote(phs.at[2, heads], phr.at[2, heads], pvs.at[c], pvr.at[c], left, r)

    def back(i, h):
        po[i, h, T : T + 8] = phr[i, h].astype(F32)[0:8]
        taps = ck[i, :, lanes(h)]
        out = taps[0:1] * po[i, h, 0:T]
        for j in range(1, 4):
            out = out + taps[j : j + 1] * po[i, h, j : j + T]
        return out.astype(BF16)

    def gx_swap(j, d):
        to = peer(d)
        return remote(gvg.at[to * NH + j, me], gxi.at[r, j], gxs.at[j, d - 1], gxr.at[j, d - 1], me, to)

    def weight_sent(i, _):
        m, o = i // n, lax.rem(i, n)
        c = m * parts + y

        @pl.when(jnp.logical_and(jnp.logical_not(last), o <= me))
        def _():
            hop(wg, c, m, o, 0).wait_send()

        @pl.when(jnp.logical_and(jnp.logical_not(first), o >= me))
        def _():
            hop(wg, c, m, o, 1).wait_send()

        return 0

    def send_value_edge(c):
        @pl.when(jnp.logical_not(first))
        def _():
            value_edge(c).start()

    def value_grad(c):
        @pl.when(jnp.logical_not(last))
        def _():
            value_edge(c).wait_recv()

        for j in range(PER):
            gvg[c, me, :, j * D : (j + 1) * D] = back(2, c * PER + j)
        own(gvg, c, c)
        for d in range(1, reps):
            j = c - peer(d) * NH

            @pl.when(jnp.logical_and(j >= 0, j < NH))
            def _():
                gx_swap(j, d).start()

    far = (pairs - 1) * LAG + 2

    def scan_step(s, _):
        def at(h, work):
            @pl.when(jnp.logical_and(h >= 0, h < H))
            def _():
                work(h)

        @pl.when(jnp.logical_and(lax.rem(s, SWAP_EVERY) == SWAP_EVERY - 1, s // SWAP_EVERY + 1 < n))
        def _():
            a_swap(s // SWAP_EVERY + 1).start()

        at(s, values)
        at(s - lead * LAG - 1, functools.partial(carry, 0))
        at(s - far, attend)
        at(s - far - lead * LAG - 1, functools.partial(carry, 1))
        at(s - far, query_side)
        at(s - 2 * far, key_side)

        @pl.when(s == 2 * far - 1)
        def _():
            lax.fori_loop(0, NM * n, weight_sent, 0)

        def at_chunk(h, work):
            @pl.when(jnp.logical_and(jnp.logical_and(h >= 0, h < H), lax.rem(h + PER, PER) == PER - 1))
            def _():
                work(h // PER)

        at_chunk(s - 2 * far, send_value_edge)
        at_chunk(s - 2 * far - EDGE_LAG, value_grad)
        return 0

    lax.fori_loop(0, H + 2 * far + EDGE_LAG, scan_step, 0)

    @pl.when(jnp.logical_not(first))
    def _():
        for i in range(2):
            post_edge(i).start()

    def taps_out(d):
        to = lax.rem(me + d, n)
        return remote(gcp.at[pl.ds(to * UP, UP)], gca.at[me], cs1.at[0], cr1.at[d - 1], to, r)

    def taps_in(d):
        source = lax.rem(me + n - d, n)
        return remote(gcp.at[pl.ds(0, UP)], gca.at[source], cs1.at[0], cr1.at[d - 1], source, r)

    def taps_swap(d):
        return remote(gcb.at[r], gcb.at[r], cs2.at[d - 1], cr2.at[d - 1], me, peer(d))

    def taps_swap_in(d):
        source = lax.rem(r + reps - d, reps)
        return remote(gcb.at[r], gcb.at[source], cs2.at[d - 1], cr2.at[d - 1], me, source)

    def taps_back(d):
        to = lax.rem(me + d, n)
        return remote(gcf.at[pl.ds(me * UP, UP)], gcf.at[pl.ds(me * UP, UP)], cs3.at[0], cr3.at[d - 1], to, r)

    def taps_back_in(d):
        source = lax.rem(me + n - d, n)
        return remote(
            gcf.at[pl.ds(me * UP, UP)], gcf.at[pl.ds(source * UP, UP)], cs3.at[0], cr3.at[d - 1], source, r
        )

    for d in range(1, n):
        taps_out(d).start()
    gca[me] = gcp[pl.ds(me * UP, UP)]

    def gx_swap_in(j, d):
        source = lax.rem(r + reps - d, reps)
        return remote(gvg.at[j, me], gxi.at[source, j], gxs.at[j, d - 1], gxr.at[j, d - 1], me, source)

    for j in range(NH):
        gxi[r, j] = gvg[r * NH + j, me]

    @pl.when(jnp.logical_not(last))
    def _():
        for i in range(2):
            post_edge(i).wait_recv()

    def input_grad(b):
        rows = wg.shape[2]
        per = TILE // rows
        out = jnp.zeros((reps * T, TILE), F32)
        for m in range(NM):
            j, at = divmod(m * CC, CT)
            x = gxi[:, j, :, at : at + CC].reshape(reps * T, CC)
            rows_of = [wg[m * parts + i, pl.ds(b * per, per)].reshape(TILE, CW) for i in range(parts)]
            out = out + dot_t(x, jnp.concatenate(rows_of, axis=1))
        cols = pl.ds(pl.multiple_of(b * TILE, TILE), TILE)
        for i in range(reps):
            pxf[i, :, cols] = out[i * T : (i + 1) * T]
            pxs[i, :, cols] = out[i * T : (i + 1) * T].astype(BF16)

    def px_swap(d):
        to = peer(d)
        return remote(pxs.at[to], pxi.at[d - 1], pxss.at[d - 1], pxsr.at[d - 1], me, to)

    def gw_swap(c, d):
        to = peer(d)
        return remote(gws.at[c, pl.ds(to * FB, FB), :], gwi.at[c, d - 1], gwss.at[c, d - 1], gwsr.at[c, d - 1], me, to)

    X_TILES = F // TILE
    G_STEPS = n + G_SKEW * (NT - 1)

    def both_back(h):
        gq[:, lanes(h)] = back(0, h)
        gk[:, lanes(h)] = back(1, h)

    def last_step(s, _):
        for c in range(NT):
            t = s - G_SKEW * c

            @pl.when(jnp.logical_and(t >= 1, t < n))
            def _():
                pass_on(gvg, c, c, t)

            @pl.when(t == n - 1)
            def _():
                if c == 0:
                    for d in range(1, n):
                        a_swap_from(d).wait_recv()

                gwa[c] = dot(actc[...], gvg[c].reshape(n * T, CT))
                gws[c] = gwa[c].astype(BF16)
                for d in range(1, reps):
                    gw_swap(c, d).start()

        jobs(both_back, H, s, n)

        @pl.when(s == 1)
        def _():
            for d in range(1, n):
                taps_in(d).wait_recv()
            part = gca[0]
            for o in range(1, n):
                part = part + gca[o]
            gcb[r] = part
            for d in range(1, reps):
                taps_swap(d).start()

        @pl.when(s == 3)
        def _():
            for d in range(1, reps):
                taps_swap_in(d).wait_recv()
            part = gcb[0]
            for o in range(1, reps):
                part = part + gcb[o]
            gcf[pl.ds(me * UP, UP)] = part * scale
            for d in range(1, n):
                taps_back(d).start()

        @pl.when(s == 2)
        def _():
            for j in range(NH):
                for d in range(1, reps):
                    gx_swap_in(j, d).wait_recv()

        @pl.when(jnp.logical_and(s >= 3, s < 3 + X_TILES))
        def _():
            input_grad(s - 3)

        @pl.when(s == 3 + X_TILES)
        def _():
            for d in range(1, reps):
                px_swap(d).start()

        return 0

    lax.fori_loop(0, G_STEPS, last_step, 0)
    for d in range(1, reps):
        px_swap(d).wait_recv()
    out = pxf[r]
    for d in range(1, reps):
        out = out + pxi[d - 1].astype(F32)
    px[...] = out.astype(BF16)
    for d in range(1, n):
        taps_back_in(d).wait_recv()
    for h in range(H):
        gc[0, :, h * D : (h + 1) * D] = gcf[2 * h, 0:4]
        gc[1, :, h * D : (h + 1) * D] = gcf[2 * h, 4:8]
        gc[2, :, h * D : (h + 1) * D] = gcf[2 * h + 1, 0:4]
    for c in range(NT):
        for d in range(1, reps):
            gw_swap(c, d).wait_recv()
        out = gwa[c, pl.ds(r * FB, FB), :]
        for d in range(1, reps):
            out = out + gwi[c, d - 1].astype(F32)
        gw[:, c * CT : (c + 1) * CT] = out * scale

    for d in range(1, reps):
        act_swap(d).wait_send()
        px_swap(d).wait_send()
        taps_swap(d).wait_send()
        for m in range(NM):
            w_swap(m, d).wait_send()
            v_swap(m, d).wait_send()
        for c in range(NT):
            gw_swap(c, d).wait_send()
        for j in range(NH):
            gx_swap(j, d).wait_send()
    for dy in range(1, parts):
        for m in range(NM):
            blocks = wg.at[m, pl.ds(0, n // 2)]
            remote(blocks, blocks, wys.at[dy - 1, m], gar.at[0, 0], me, r, lax.rem(y + dy, parts)).wait_send()
            remote(blocks, blocks, wms.at[dy - 1, m], gar.at[0, 0], mate, r).wait_send()
    others = actt.at[pl.ds(0, (n - 1) * reps * FB), :]
    remote(others, others, ats.at[0], atr.at[0], right, r).wait_send()
    others = gcp.at[pl.ds(0, (n - 1) * UP)]
    remote(others, others, cs1.at[0], cr1.at[0], right, r).wait_send()
    remote(others, others, cs3.at[0], cr3.at[0], right, r).wait_send()

    @pl.when(jnp.logical_not(last))
    def _():
        for i in range(2):
            qk_edge(i).wait_send()
        for d in range(reps):
            act_edge(d).wait_send()

    @pl.when(jnp.logical_not(first))
    def _():
        for i in range(2):
            post_edge(i).wait_send()
        for c in range(NT):
            value_edge(c).wait_send()

    sent(gvg, NT)
    decay_swap.wait_send()
    for j in range(2):
        remote(mates.at[j], kept.at[j], ms.at[j], mr.at[j, 0], mate, r).wait_send()

        @pl.when(jnp.logical_not(leads_last))
        def _():
            remote(sout.at[j], raw.at[j], ss.at[j], rr.at[j, 0], onward, r).wait_send()

        @pl.when(jnp.logical_not(leads_first))
        def _():
            remote(raw.at[j], sin.at[2 * j], fs.at[j], sr.at[j, 0], mate, r).wait_send()


def hand_over(*refs):
    count = len(refs) // 2
    sems = refs[-1]
    copies = [pltpu.make_async_copy(refs[i], refs[count + i], sems.at[i]) for i in range(count)]
    for copy in copies:
        copy.start()
    for copy in copies:
        copy.wait()


def local(n, reps, parts, activations, value_weight, query_in, key_in, grad_out, conv_kernel, log_gate):
    act = lax.all_gather(activations, "head", axis=2, tiled=True)[0]
    T, F = act.shape
    FB, C = value_weight.shape
    H = log_gate.shape[1]
    D = C // H
    TH = T + EDGE
    CW = D
    CC = CW * parts
    CT = min(512, C // reps)
    NW, NM, NT = C // reps // CW, C // reps // CC, C // CT
    NH = NT // reps
    UP = 2 * H // n
    scale = 1.0 / math.sqrt(n * reps * T)
    dma = pltpu.SemaphoreType.DMA
    peers = max(reps - 1, 1)
    scratch = [
        pltpu.VMEM((reps * TH, F), BF16),
        pltpu.VMEM((NW, n, reps * FB, CW), BF16),
        pltpu.VMEM((NM, reps * TH, CC), BF16),
        pltpu.VMEM((reps * NM, TH, CC), BF16),
        pltpu.VMEM((2, EDGE, C), BF16),
        pltpu.VMEM((3, TH, D), F32),
        pltpu.VMEM((H, T), F32),
        pltpu.VMEM((H, T, D), F32),
        pltpu.VMEM((H, T, D), F32),
        pltpu.VMEM((H, T, T), F32),
        pltpu.VMEM((H, T, D), BF16),
        pltpu.VMEM((H, T, D), BF16),
        pltpu.VMEM((H, T, D), BF16),
        pltpu.VMEM((H, T, D), BF16),
        pltpu.VMEM((H, T, 3 * D), BF16),
        pltpu.VMEM((H, T, 3 * D), BF16),
        pltpu.VMEM((H, 2 * D, T), BF16),
        pltpu.VMEM((H, 2 * D, T), BF16),
        pltpu.VMEM((H, T, 2 * D), BF16),
        pltpu.VMEM((4, H, D, D), F32),
        pltpu.VMEM((4, H, D, D), BF16),
        pltpu.VMEM((2, H, D, D), BF16),
        pltpu.VMEM((2, H, D, D), BF16),
        pltpu.VMEM((2, H, D, D), BF16),
        pltpu.VMEM((2, H, D, D), BF16),
        pltpu.VMEM((2, H, D), F32),
        pltpu.VMEM((3, H, T + 8, D), F32),
        pltpu.VMEM((3, H, EDGE, D), BF16),
        pltpu.VMEM((3, H, EDGE, D), BF16),
        pltpu.VMEM((F, T), BF16),
        pltpu.VMEM((reps * FB, n * T), BF16),
        pltpu.VMEM((NT, n, T, CT), BF16),
        pltpu.VMEM((reps, NH, T, CT), BF16),
        pltpu.VMEM((reps, T, F), F32),
        pltpu.VMEM((reps, T, F), BF16),
        pltpu.VMEM((peers, T, F), BF16),
        pltpu.VMEM((NT, reps * FB, CT), BF16),
        pltpu.VMEM((NT, peers, FB, CT), BF16),
        pltpu.VMEM((NT, reps * FB, CT), F32),
        pltpu.VMEM((n * UP, 8, D), F32),
        pltpu.VMEM((n, UP, 8, D), F32),
        pltpu.VMEM((reps, UP, 8, D), F32),
        pltpu.VMEM((n * UP, 8, D), F32),
        dma((NM, peers)), dma((NM, peers)),
        dma((peers,)), dma((peers,)),
        dma((reps,)), dma((reps,)),
        dma((2,)), dma((2,)),
        dma((max(NM, NT), n + 1)), dma((max(NW, NT), n)),
        dma((max(parts - 1, 1), NM)), dma((max(parts - 1, 1), NM)),
        dma((NM, peers)), dma((NM, peers)),
        dma((1,)), dma((n - 1,)),
        dma((1,)), dma((1,)),
        dma((2,)), dma((2, H)),
        dma((2,)), dma((2, H)),
        dma((2,)), dma((2, H)),
        dma((2,)), dma((2,)),
        dma((NT,)), dma((NT,)),
        dma((NH, peers)), dma((NH, peers)),
        dma((peers,)), dma((peers,)),
        dma((NT, peers)), dma((NT, peers)),
        dma((1,)), dma((n - 1,)),
        dma((peers,)), dma((peers,)),
        dma((1,)), dma((n - 1,)),
    ]
    vmem = pl.BlockSpec(memory_space=pltpu.VMEM)
    results = pl.pallas_call(
        functools.partial(kernel, n, reps, parts, scale),
        out_shape=(
            jax.ShapeDtypeStruct((T, C), BF16),
            jax.ShapeDtypeStruct((T, C), BF16),
            jax.ShapeDtypeStruct((T, C), BF16),
            jax.ShapeDtypeStruct((T, F), BF16),
            jax.ShapeDtypeStruct((FB, C), F32),
            jax.ShapeDtypeStruct(conv_kernel.shape, F32),
        ),
        in_specs=[vmem] * 7,
        out_specs=[vmem] * 6,
        scratch_shapes=scratch,
        compiler_params=pltpu.CompilerParams(
            collective_id=0, has_side_effects=True, vmem_limit_bytes=60 * 2**20
        ),
        cost_estimate=pl.CostEstimate(flops=5 * 10**9, bytes_accessed=8 * 2**20, transcendentals=10**6),
    )(act, value_weight, query_in[0], key_in[0], grad_out[0], conv_kernel, log_gate[0])
    kept = pl.BlockSpec(memory_space=pl.ANY)
    attn_out, grad_query, grad_key, part_x, grad_w, grad_conv = pl.pallas_call(
        hand_over,
        out_shape=tuple(jax.ShapeDtypeStruct(a.shape, a.dtype) for a in results),
        in_specs=[vmem] * len(results),
        out_specs=(kept,) * len(results),
        scratch_shapes=[pltpu.SemaphoreType.DMA((len(results),))],
    )(*results)
    grad_x = lax.psum_scatter(part_x[None], "head", scatter_dimension=2, tiled=True)
    return attn_out[None], grad_query[None], grad_key[None], grad_x, grad_w, grad_conv


def solution(mesh):
    placed = (
        P(("parts", "rep"), "seq", "head"),
        P(("seq", "rep"), "head"),
        P(("parts", "rep"), "seq", "head"),
        P(("parts", "rep"), "seq", "head"),
        P(("parts", "rep"), "seq", "head"),
        P(None, None, "head"),
        P(("parts", "rep"), "head", "seq"),
    )
    return jax.shard_map(
        functools.partial(local, mesh.shape["seq"], mesh.shape["rep"], mesh.shape["parts"]),
        mesh=mesh,
        in_specs=placed,
        out_specs=(
            P(("parts", "rep"), "seq", "head"),
            P(("parts", "rep"), "seq", "head"),
            P(("parts", "rep"), "seq", "head"),
            P(("parts", "rep"), "seq", "head"),
            P(("parts", "seq", "rep"), "head"),
            P("parts", None, "head"),
        ),
        check_vma=False,
    )
```

```python
import functools
import math

import jax
import jax.numpy as jnp
from jax import lax
from jax.experimental import pallas as pl
from jax.experimental.pallas import tpu as pltpu
from jax.sharding import PartitionSpec as P

EPSILON = 1e-06
EDGE = 16
LAG = 4
TWIN_LAG = 3
W_SKEW = 0
G_SKEW = 1
SWAP_EVERY = 5
EDGE_LAG = 5
TILE = 512
F32 = jnp.float32
BF16 = jnp.bfloat16


def dot(a, b):
    return lax.dot_general(a, b, (((1,), (0,)), ((), ())), preferred_element_type=F32)


def dot_t(a, b):
    return lax.dot_general(a, b, (((1,), (1,)), ((), ())), preferred_element_type=F32)


def kernel(n, reps, parts, scale, *refs):
    (act, w, q, k, go, ck, lg) = refs[:7]
    (ao, gq, gk, px, gw, gc) = refs[7:13]
    (
        acta, wg, vout, vr, qkh, xf, cumr, rise, shrink, mx, qh, kh, vh, gh, lhs1, lhs2, kt, qt, rsv,
        sums, sin, raw, sout, mates, kept, decays, po, phs, phr, actt, actc, gvg, gxi, pxf, pxs, pxi, gws, gwi, gwa,
        gcp, gca, gcb, gcf,
        wxs, wxr, axs, axr, ahs, ahr, qhs, qhr, gas, gar, wys, wms, vxs, vxr, ats, atr, dcs, dcr, ss, rr, fs, sr, ms, mr, phss, phsr, pvs, pvr,
        gxs, gxr, pxss, pxsr, gwss, gwsr, cs1, cr1, cs2, cr2, cs3, cr3,
    ) = refs[13:]
    T, F = act.shape
    FB, C = w.shape
    H = lg.shape[0]
    D = C // H
    TH = T + EDGE
    NW, _, _, CW = wg.shape
    NM, _, CC = vout.shape
    NT, _, _, CT = gvg.shape
    half = C // reps
    NH = NT // reps
    UP = 2 * H // n
    me = lax.axis_index("seq")
    r = lax.axis_index("rep")
    y = lax.axis_index("parts")
    odd = lax.rem(me, 2)
    mate = me + 1 - 2 * odd
    way, pair, pairs = 1 - odd, me // 2, n // 2
    lead = jnp.where(odd == 1, pair, pairs - 1 - pair)
    follow = pairs - 1 - lead
    onward = lax.rem(jnp.where(odd == 1, me + 2, me + n - 2), n)
    leads_first, leads_last, follows_first = lead == 0, lead == pairs - 1, follow == 0
    first, last = me == 0, me == n - 1
    right, left = lax.rem(me + 1, n), lax.rem(me + n - 1, n)

    def peer(d):
        return lax.rem(r + d, reps)

    def remote(src, dst, send, recv, seq, rep, part=None):
        return pltpu.make_async_remote_copy(
            src_ref=src, dst_ref=dst, send_sem=send, recv_sem=recv,
            device_id={"parts": y if part is None else part, "seq": seq, "rep": rep},
            device_id_type=pl.DeviceIdType.MESH,
        )

    def lanes(h):
        return pl.ds(pl.multiple_of(h * D, D), D)

    barrier = pltpu.get_barrier_semaphore()
    for ds in range(n):
        for dr in range(reps):
            if ds or dr:
                pl.semaphore_signal(
                    barrier, inc=1, device_id={"seq": lax.rem(me + ds, n), "rep": peer(dr)},
                    device_id_type=pl.DeviceIdType.MESH,
                )
    for dy in range(1, parts):
        pl.semaphore_signal(
            barrier, inc=1, device_id={"parts": lax.rem(y + dy, parts)}, device_id_type=pl.DeviceIdType.MESH
        )

    total = lg[...]
    place = lax.broadcasted_iota(jnp.int32, total.shape, 1)
    distance = 1
    while distance < T:
        moved = pltpu.roll(total, distance, 1)
        total = total + jnp.where(place >= distance, moved, 0.0)
        distance *= 2
    cumr[...] = total
    columns = jnp.concatenate([total, jnp.zeros((T - H, T), F32)], axis=0).T
    for h in range(H):
        rise[h] = jnp.broadcast_to(columns[:, h : h + 1], (T, D))

    for m in range(NM):
        c = m * parts + y
        wg[c, me, pl.ds(r * FB, FB), :] = w[:, pl.ds(pl.multiple_of(r * half + c * CW, CW), CW)]
    acta[pl.ds(r * TH + EDGE, T), :] = act[...]

    @pl.when(first)
    def _():
        for d in range(reps):
            acta[pl.ds(d * TH, EDGE), :] = jnp.zeros((EDGE, F), BF16)
        qkh[...] = jnp.zeros(qkh.shape, BF16)

    @pl.when(leads_first)
    def _():
        raw[...] = jnp.zeros(raw.shape, BF16)

    @pl.when(follows_first)
    def _():
        sin[1 - way] = jnp.zeros(sin.shape[1:], BF16)
        sin[3 - way] = jnp.zeros(sin.shape[1:], BF16)

    decays[0] = jnp.exp(jnp.broadcast_to(total[:, T - 1 : T], (H, D)))

    @pl.when(last)
    def _():
        phr[...] = jnp.zeros(phr.shape, BF16)

    pl.semaphore_wait(barrier, n * reps - 1 + parts - 1)

    def w_swap(m, d):
        to, c = peer(d), m * parts + y
        return remote(
            w.at[:, pl.ds(pl.multiple_of(to * half + c * CW, CW), CW)],
            wg.at[c, me, pl.ds(r * FB, FB), :], wxs.at[m, d - 1], wxr.at[m, d - 1], me, to,
        )

    def act_swap(d):
        return remote(act, acta.at[pl.ds(r * TH + EDGE, T), :], axs.at[d - 1], axr.at[d - 1], me, peer(d))

    def act_edge(d):
        return remote(
            act.at[pl.ds(T - EDGE, EDGE), :], acta.at[pl.ds(r * TH, EDGE), :], ahs.at[d], ahr.at[d], right, peer(d)
        )

    def qk_edge(i):
        return remote((q, k)[i].at[pl.ds(T - EDGE, EDGE), :], qkh.at[i], qhs.at[i], qhr.at[i], right, r)

    for d in range(1, reps):
        w_swap(0, d).start()

    decay_swap = remote(decays.at[0], decays.at[1], dcs.at[0], dcr.at[0], mate, r)
    decay_swap.start()

    @pl.when(jnp.logical_not(last))
    def _():
        for i in range(2):
            qk_edge(i).start()

    for m in range(1, NM):
        for d in range(1, reps):
            w_swap(m, d).start()
    for d in range(1, reps):
        act_swap(d).start()

    @pl.when(jnp.logical_not(last))
    def _():
        for d in range(reps):
            act_edge(d).start()

    def hop(buf, c, m, o, way):
        mark = jnp.where(o == me, n, o) if way else o
        return remote(buf.at[c, o], buf.at[c, o], gas.at[m, mark], gar.at[c, o], (right, left)[way], r)

    def own(buf, c, m):
        @pl.when(jnp.logical_not(last))
        def _():
            hop(buf, c, m, me, 0).start()

        @pl.when(jnp.logical_not(first))
        def _():
            hop(buf, c, m, me, 1).start()

    def pass_on(buf, c, m, t, seen=None):
        lower, upper = me - t, me + t

        @pl.when(lower >= 0)
        def _():
            hop(buf, c, m, lower, 0).wait_recv()

            @pl.when(jnp.logical_not(last))
            def _():
                hop(buf, c, m, lower, 0).start()

            if seen is not None:
                seen(lower)

        @pl.when(upper < n)
        def _():
            hop(buf, c, m, upper, 1).wait_recv()

            @pl.when(jnp.logical_not(first))
            def _():
                hop(buf, c, m, upper, 1).start()

            if seen is not None:
                seen(upper)

    def sent(buf, chunks):
        def one(i, _):
            c, o = i // n, lax.rem(i, n)

            @pl.when(jnp.logical_and(jnp.logical_not(last), o <= me))
            def _():
                hop(buf, c, c, o, 0).wait_send()

            @pl.when(jnp.logical_and(jnp.logical_not(first), o >= me))
            def _():
                hop(buf, c, c, o, 1).wait_send()

            return 0

        lax.fori_loop(0, chunks * n, one, 0)

    def to_twin(m, dy, o):
        c = m * parts + y
        return remote(wg.at[c, o], wg.at[c, o], wys.at[dy - 1, m], gar.at[c, o], me, r, lax.rem(y + dy, parts))

    def to_mate(m, dy, o):
        c = m * parts + lax.rem(y + dy, parts)
        return remote(wg.at[c, o], wg.at[c, o], wms.at[dy - 1, m], gar.at[c, o], mate, r)

    def filtered(i, x, taps):
        out = taps[0:1] * x[i, EDGE : EDGE + T]
        for j in range(1, 4):
            out = out + taps[j : j + 1] * x[i, EDGE - j : EDGE - j + T]
        return out.astype(BF16)

    def load_rows(i, h):
        if i < 2:
            xf[i, 0:EDGE] = qkh[i, :, lanes(h)].astype(F32)
            xf[i, EDGE:] = (q, k)[i][:, lanes(h)].astype(F32)
        else:
            per = CC // D
            xf[i] = vr[h // per, :, pl.ds(pl.multiple_of(lax.rem(h, per) * D, D), D)].astype(F32)

    def prepare(h):
        cc = rise[h]
        fin = cc[T - 1 : T]
        rising = jnp.exp(cc)
        shrinking = jnp.exp(fin - cc)
        mixing = jnp.exp(-jnp.abs(cc - cumr[pl.ds(h, 1), :]))
        rise[h] = rising
        shrink[h] = shrinking
        mx[h] = mixing
        for i in range(2):
            load_rows(i, h)
        qv = filtered(0, xf, ck[0, :, lanes(h)])
        kv = filtered(1, xf, ck[1, :, lanes(h)])
        qh[h] = qv
        kh[h] = kv
        qf, kf = qv.astype(F32), kv.astype(F32)
        rq, sq = (rising * qf), (shrinking * qf)
        rk, sk = (rising * kf), (shrinking * kf)
        lhs1[h, :, 0:D] = (mixing * dot_t(qv, kv)).astype(BF16)
        lhs1[h, :, D : 2 * D] = rq.astype(BF16)
        lhs1[h, :, 2 * D :] = sq.astype(BF16)
        lhs2[h, :, 0:D] = (mixing * dot_t(kv, qv)).astype(BF16)
        lhs2[h, :, D : 2 * D] = rk.astype(BF16)
        lhs2[h, :, 2 * D :] = sk.astype(BF16)
        qt[h, 0:D] = sq.T.astype(BF16)
        qt[h, D:] = rq.T.astype(BF16)
        kt[h, 0:D] = sk.T.astype(BF16)
        kt[h, D:] = rk.T.astype(BF16)

    def turn(b):
        rows = pl.ds(pl.multiple_of(b * T, T), T)
        actt[rows, :] = act[:, rows].astype(F32).T.astype(BF16)

    def ready(m):
        for d in range(1, reps):
            w_swap(m, d).wait_recv()
        own(wg, m * parts + y, m)
        for dy in range(1, parts):
            to_twin(m, dy, me).start()

    def v_swap(c, d):
        to = peer(d)
        return remote(
            vout.at[c, pl.ds(to * TH, TH), :], vr.at[r * NM + c], vxs.at[c, d - 1], vxr.at[c, d - 1], me, to
        )

    @pl.when(jnp.logical_not(first))
    def _():
        for i in range(2):
            qk_edge(i).wait_recv()

    def jobs(work, count, step, steps):
        per = -(-count // steps)
        for j in range(per):
            @pl.when(step * per + j < count)
            def _():
                work(step * per + j)

    W_STEPS = n + TWIN_LAG + W_SKEW * (NM - 1)

    def w_step(s, _):
        for m in range(NM):
            t = s - W_SKEW * m

            @pl.when(t == 0)
            def _():
                ready(m)

            def twins(o):
                @pl.when(lax.rem(t, 2) == 0)
                def _():
                    for dy in range(1, parts):
                        to_twin(m, dy, o).start()

            @pl.when(jnp.logical_and(t >= 1, t < n))
            def _():
                pass_on(wg, m * parts + y, m, t, twins)

            for dy in range(1, parts):
                for near, source in ((True, me), (False, mate)):
                    u = t - (TWIN_LAG if near else TWIN_LAG + 1)

                    def take(o):
                        to_mate(m, dy, o).wait_recv()
                        if near:
                            to_mate(m, dy, o).start()

                    def even(ok):
                        return jnp.logical_and(jnp.logical_and(u >= 0, u < n), jnp.logical_and(lax.rem(u, 2) == 0, ok))

                    @pl.when(even(source - u >= 0))
                    def _():
                        take(source - u)

                    @pl.when(even(jnp.logical_and(u > 0, source + u < n)))
                    def _():
                        take(source + u)

            @pl.when(t == n - 1 + TWIN_LAG)
            def _():
                if m == 0:
                    for d in range(1, reps):
                        act_swap(d).wait_recv()

                    @pl.when(jnp.logical_not(first))
                    def _():
                        for d in range(reps):
                            act_edge(d).wait_recv()

                columns_of = [wg[m * parts + j].reshape(F, CW) for j in range(parts)]
                vout[m] = dot(acta[...], jnp.concatenate(columns_of, axis=1)).astype(BF16)
                for d in range(1, reps):
                    v_swap(m, d).start()
                vr[r * NM + m] = vout[m, pl.ds(r * TH, TH), :]

        jobs(prepare, H, s, n)
        jobs(turn, F // T, s, n)
        return 0

    lax.fori_loop(0, W_STEPS, w_step, 0)

    def a_swap(d):
        to = lax.rem(me + d, n)
        return remote(
            actt.at[pl.ds(to * reps * FB, reps * FB), :], actc.at[:, pl.ds(pl.multiple_of(me * T, T), T)],
            ats.at[0], atr.at[d - 1], to, r,
        )

    def a_swap_from(d):
        source = lax.rem(me + n - d, n)
        return remote(
            actt.at[pl.ds(0, reps * FB), :], actc.at[:, pl.ds(pl.multiple_of(source * T, T), T)],
            ats.at[0], atr.at[d - 1], source, r,
        )

    actc[:, pl.ds(pl.multiple_of(me * T, T), T)] = actt[pl.ds(me * reps * FB, reps * FB), :]

    def v_arrival(c, d):
        source = lax.rem(r + reps - d, reps)
        return remote(
            vout.at[c, pl.ds(0, TH), :], vr.at[source * NM + c], vxs.at[c, d - 1], vxr.at[c, d - 1], me, source
        )

    for c in range(NM):
        for d in range(1, reps):
            v_arrival(c, d).wait_recv()

    decay_swap.wait_recv()

    def values(h):
        load_rows(2, h)
        v = filtered(2, xf, ck[2, :, lanes(h)])
        vh[h] = v
        vf = v.astype(F32)
        rsv[h, :, 0:D] = (rise[h] * vf).astype(BF16)
        rsv[h, :, D:] = (shrink[h] * vf).astype(BF16)
        both = dot(kt[h], v)
        sums[0, h] = both[0:D]
        sums[1, h] = both[D:]
        share(0, h)

    def message(j, h):
        return remote(sout.at[j, h], raw.at[j, h], ss.at[j], rr.at[j, h], onward, r)

    def hand_in(j, h, which):
        return remote(raw.at[j, h], sin.at[2 * j + which, h], fs.at[j], sr.at[j, h], mate, r)

    def mate_sum(j, h):
        return remote(mates.at[j, h], kept.at[j, h], ms.at[j], mr.at[j, h], mate, r)

    def share(j, h):
        mates[j, h] = sums[2 * j + 1 - way, h].astype(BF16)
        mate_sum(j, h).start()

    def carry(j, h):
        @pl.when(jnp.logical_not(leads_first))
        def _():
            message(j, h).wait_recv()
            hand_in(j, h, way).start()

        mate_sum(j, h).wait_recv()
        i = 2 * j + way
        state = decays[1, pl.ds(h, 1), :] * raw[j, h].astype(F32) + kept[j, h].astype(F32)
        sin[i, h] = state.astype(BF16)

        @pl.when(jnp.logical_not(leads_last))
        def _():
            sout[j, h] = (decays[0, pl.ds(h, 1), :] * state + sums[i, h]).astype(BF16)
            message(j, h).start()

    def handed(j, h):
        @pl.when(jnp.logical_not(follows_first))
        def _():
            hand_in(j, h, 1 - way).wait_recv()

    def attend(h):
        handed(0, h)
        v, before, after = vh[h], sin[0, h], sin[1, h]
        attn = dot(lhs1[h], jnp.concatenate([v, before, after], axis=0))
        inverse = lax.rsqrt(jnp.mean(attn * attn, axis=1, keepdims=True) + EPSILON)
        normed = attn * inverse
        ao[:, lanes(h)] = normed.astype(BF16)
        up = go[:, lanes(h)].astype(F32)
        g = ((up - normed * jnp.mean(up * normed, axis=1, keepdims=True)) * inverse).astype(BF16)
        gh[h] = g
        both = dot(qt[h], g)
        sums[2, h] = both[0:D]
        sums[3, h] = both[D:]
        share(1, h)

    def query_side(h):
        v, before, after, g, mixing = vh[h], sin[0, h], sin[1, h], gh[h], mx[h]
        gf = g.astype(F32)
        decayed = jnp.concatenate([(rise[h] * gf).astype(BF16), (shrink[h] * gf).astype(BF16)], axis=1)
        grad_scores = (mixing * dot_t(g, v)).astype(BF16)
        grad_scores_t = (mixing * dot_t(v, g)).astype(BF16)
        po[0, h, 0:T] = dot(grad_scores, kh[h]) + dot_t(decayed, jnp.concatenate([before, after], axis=1))
        po[1, h, 0:T] = dot(grad_scores_t, qh[h])

    def key_side(h):
        handed(1, h)
        before, after = sin[2, h], sin[3, h]
        po[1, h, 0:T] = po[1, h, 0:T] + dot_t(rsv[h], jnp.concatenate([before, after], axis=1))
        po[2, h, 0:T] = dot(lhs2[h], jnp.concatenate([gh[h], before, after], axis=0))
        rows = []
        for i in range(3):
            load_rows(i, h)
            post = po[i, h, 0:T]
            phs[i, h] = post[0:EDGE].astype(BF16)
            for j in range(4):
                rows.append(jnp.sum(post * xf[i, EDGE - j : EDGE - j + T], axis=0, keepdims=True))
        zero = jnp.zeros((4, D), F32)
        gcp[2 * h] = jnp.concatenate(rows[0:8], axis=0)
        gcp[2 * h + 1] = jnp.concatenate(rows[8:12] + [zero], axis=0)

    PER = CT // D

    def post_edge(i):
        return remote(phs.at[i], phr.at[i], phss.at[i], phsr.at[i], left, r)

    def value_edge(c):
        heads = pl.ds(c * PER, PER)
        return remote(phs.at[2, heads], phr.at[2, heads], pvs.at[c], pvr.at[c], left, r)

    def back(i, h):
        po[i, h, T : T + 8] = phr[i, h].astype(F32)[0:8]
        taps = ck[i, :, lanes(h)]
        out = taps[0:1] * po[i, h, 0:T]
        for j in range(1, 4):
            out = out + taps[j : j + 1] * po[i, h, j : j + T]
        return out.astype(BF16)

    def gx_swap(j, d):
        to = peer(d)
        return remote(gvg.at[to * NH + j, me], gxi.at[r, j], gxs.at[j, d - 1], gxr.at[j, d - 1], me, to)

    def weight_sent(i, _):
        m, o = i // n, lax.rem(i, n)
        c = m * parts + y

        @pl.when(jnp.logical_and(jnp.logical_not(last), o <= me))
        def _():
            hop(wg, c, m, o, 0).wait_send()

        @pl.when(jnp.logical_and(jnp.logical_not(first), o >= me))
        def _():
            hop(wg, c, m, o, 1).wait_send()

        return 0

    def send_value_edge(c):
        @pl.when(jnp.logical_not(first))
        def _():
            value_edge(c).start()

    def value_grad(c):
        @pl.when(jnp.logical_not(last))
        def _():
            value_edge(c).wait_recv()

        for j in range(PER):
            gvg[c, me, :, j * D : (j + 1) * D] = back(2, c * PER + j)
        own(gvg, c, c)
        for d in range(1, reps):
            j = c - peer(d) * NH

            @pl.when(jnp.logical_and(j >= 0, j < NH))
            def _():
                gx_swap(j, d).start()

    far = (pairs - 1) * LAG + 2

    def scan_step(s, _):
        def at(h, work):
            @pl.when(jnp.logical_and(h >= 0, h < H))
            def _():
                work(h)

        @pl.when(jnp.logical_and(lax.rem(s, SWAP_EVERY) == SWAP_EVERY - 1, s // SWAP_EVERY + 1 < n))
        def _():
            a_swap(s // SWAP_EVERY + 1).start()

        at(s, values)
        at(s - lead * LAG - 1, functools.partial(carry, 0))
        at(s - far, attend)
        at(s - far - lead * LAG - 1, functools.partial(carry, 1))
        at(s - far, query_side)
        at(s - 2 * far, key_side)

        @pl.when(s == 2 * far - 1)
        def _():
            lax.fori_loop(0, NM * n, weight_sent, 0)

        def at_chunk(h, work):
            @pl.when(jnp.logical_and(jnp.logical_and(h >= 0, h < H), lax.rem(h + PER, PER) == PER - 1))
            def _():
                work(h // PER)

        at_chunk(s - 2 * far, send_value_edge)
        at_chunk(s - 2 * far - EDGE_LAG, value_grad)
        return 0

    lax.fori_loop(0, H + 2 * far + EDGE_LAG, scan_step, 0)

    @pl.when(jnp.logical_not(first))
    def _():
        for i in range(2):
            post_edge(i).start()

    def taps_out(d):
        to = lax.rem(me + d, n)
        return remote(gcp.at[pl.ds(to * UP, UP)], gca.at[me], cs1.at[0], cr1.at[d - 1], to, r)

    def taps_in(d):
        source = lax.rem(me + n - d, n)
        return remote(gcp.at[pl.ds(0, UP)], gca.at[source], cs1.at[0], cr1.at[d - 1], source, r)

    def taps_swap(d):
        return remote(gcb.at[r], gcb.at[r], cs2.at[d - 1], cr2.at[d - 1], me, peer(d))

    def taps_swap_in(d):
        source = lax.rem(r + reps - d, reps)
        return remote(gcb.at[r], gcb.at[source], cs2.at[d - 1], cr2.at[d - 1], me, source)

    def taps_back(d):
        to = lax.rem(me + d, n)
        return remote(gcf.at[pl.ds(me * UP, UP)], gcf.at[pl.ds(me * UP, UP)], cs3.at[0], cr3.at[d - 1], to, r)

    def taps_back_in(d):
        source = lax.rem(me + n - d, n)
        return remote(
            gcf.at[pl.ds(me * UP, UP)], gcf.at[pl.ds(source * UP, UP)], cs3.at[0], cr3.at[d - 1], source, r
        )

    for d in range(1, n):
        taps_out(d).start()
    gca[me] = gcp[pl.ds(me * UP, UP)]

    def gx_swap_in(j, d):
        source = lax.rem(r + reps - d, reps)
        return remote(gvg.at[j, me], gxi.at[source, j], gxs.at[j, d - 1], gxr.at[j, d - 1], me, source)

    for j in range(NH):
        gxi[r, j] = gvg[r * NH + j, me]

    @pl.when(jnp.logical_not(last))
    def _():
        for i in range(2):
            post_edge(i).wait_recv()

    def input_grad(b):
        rows = wg.shape[2]
        per = TILE // rows
        out = jnp.zeros((reps * T, TILE), F32)
        for m in range(NM):
            j, at = divmod(m * CC, CT)
            x = gxi[:, j, :, at : at + CC].reshape(reps * T, CC)
            rows_of = [wg[m * parts + i, pl.ds(b * per, per)].reshape(TILE, CW) for i in range(parts)]
            out = out + dot_t(x, jnp.concatenate(rows_of, axis=1))
        cols = pl.ds(pl.multiple_of(b * TILE, TILE), TILE)
        for i in range(reps):
            pxf[i, :, cols] = out[i * T : (i + 1) * T]
            pxs[i, :, cols] = out[i * T : (i + 1) * T].astype(BF16)

    def px_swap(d):
        to = peer(d)
        return remote(pxs.at[to], pxi.at[d - 1], pxss.at[d - 1], pxsr.at[d - 1], me, to)

    def gw_swap(c, d):
        to = peer(d)
        return remote(gws.at[c, pl.ds(to * FB, FB), :], gwi.at[c, d - 1], gwss.at[c, d - 1], gwsr.at[c, d - 1], me, to)

    X_TILES = F // TILE
    G_STEPS = n + G_SKEW * (NT - 1)

    def both_back(h):
        gq[:, lanes(h)] = back(0, h)
        gk[:, lanes(h)] = back(1, h)

    def last_step(s, _):
        for c in range(NT):
            t = s - G_SKEW * c

            @pl.when(jnp.logical_and(t >= 1, t < n))
            def _():
                pass_on(gvg, c, c, t)

            @pl.when(t == n - 1)
            def _():
                if c == 0:
                    for d in range(1, n):
                        a_swap_from(d).wait_recv()

                gwa[c] = dot(actc[...], gvg[c].reshape(n * T, CT))
                gws[c] = gwa[c].astype(BF16)
                for d in range(1, reps):
                    gw_swap(c, d).start()

        jobs(both_back, H, s, n)

        @pl.when(s == 1)
        def _():
            for d in range(1, n):
                taps_in(d).wait_recv()
            part = gca[0]
            for o in range(1, n):
                part = part + gca[o]
            gcb[r] = part
            for d in range(1, reps):
                taps_swap(d).start()

        @pl.when(s == 3)
        def _():
            for d in range(1, reps):
                taps_swap_in(d).wait_recv()
            part = gcb[0]
            for o in range(1, reps):
                part = part + gcb[o]
            gcf[pl.ds(me * UP, UP)] = part * scale
            for d in range(1, n):
                taps_back(d).start()

        @pl.when(s == 0)
        def _():
            for j in range(NH):
                for d in range(1, reps):
                    gx_swap_in(j, d).wait_recv()

        @pl.when(jnp.logical_and(s >= 1, s < 1 + X_TILES))
        def _():
            input_grad(s - 1)

        @pl.when(s == 1 + X_TILES)
        def _():
            for d in range(1, reps):
                px_swap(d).start()

        return 0

    lax.fori_loop(0, G_STEPS, last_step, 0)
    for d in range(1, reps):
        px_swap(d).wait_recv()
    out = pxf[r]
    for d in range(1, reps):
        out = out + pxi[d - 1].astype(F32)
    px[...] = out.astype(BF16)
    for d in range(1, n):
        taps_back_in(d).wait_recv()
    for h in range(H):
        gc[0, :, h * D : (h + 1) * D] = gcf[2 * h, 0:4]
        gc[1, :, h * D : (h + 1) * D] = gcf[2 * h, 4:8]
        gc[2, :, h * D : (h + 1) * D] = gcf[2 * h + 1, 0:4]
    for c in range(NT):
        for d in range(1, reps):
            gw_swap(c, d).wait_recv()
        out = gwa[c, pl.ds(r * FB, FB), :]
        for d in range(1, reps):
            out = out + gwi[c, d - 1].astype(F32)
        gw[:, c * CT : (c + 1) * CT] = out * scale

    for d in range(1, reps):
        act_swap(d).wait_send()
        px_swap(d).wait_send()
        taps_swap(d).wait_send()
        for m in range(NM):
            w_swap(m, d).wait_send()
            v_swap(m, d).wait_send()
        for c in range(NT):
            gw_swap(c, d).wait_send()
        for j in range(NH):
            gx_swap(j, d).wait_send()
    for dy in range(1, parts):
        for m in range(NM):
            blocks = wg.at[m, pl.ds(0, n // 2)]
            remote(blocks, blocks, wys.at[dy - 1, m], gar.at[0, 0], me, r, lax.rem(y + dy, parts)).wait_send()
            remote(blocks, blocks, wms.at[dy - 1, m], gar.at[0, 0], mate, r).wait_send()
    others = actt.at[pl.ds(0, (n - 1) * reps * FB), :]
    remote(others, others, ats.at[0], atr.at[0], right, r).wait_send()
    others = gcp.at[pl.ds(0, (n - 1) * UP)]
    remote(others, others, cs1.at[0], cr1.at[0], right, r).wait_send()
    remote(others, others, cs3.at[0], cr3.at[0], right, r).wait_send()

    @pl.when(jnp.logical_not(last))
    def _():
        for i in range(2):
            qk_edge(i).wait_send()
        for d in range(reps):
            act_edge(d).wait_send()

    @pl.when(jnp.logical_not(first))
    def _():
        for i in range(2):
            post_edge(i).wait_send()
        for c in range(NT):
            value_edge(c).wait_send()

    sent(gvg, NT)
    decay_swap.wait_send()
    for j in range(2):
        remote(mates.at[j], kept.at[j], ms.at[j], mr.at[j, 0], mate, r).wait_send()

        @pl.when(jnp.logical_not(leads_last))
        def _():
            remote(sout.at[j], raw.at[j], ss.at[j], rr.at[j, 0], onward, r).wait_send()

        @pl.when(jnp.logical_not(leads_first))
        def _():
            remote(raw.at[j], sin.at[2 * j], fs.at[j], sr.at[j, 0], mate, r).wait_send()


def hand_over(*refs):
    count = len(refs) // 2
    sems = refs[-1]
    copies = [pltpu.make_async_copy(refs[i], refs[count + i], sems.at[i]) for i in range(count)]
    for copy in copies:
        copy.start()
    for copy in copies:
        copy.wait()


def local(n, reps, parts, activations, value_weight, query_in, key_in, grad_out, conv_kernel, log_gate):
    act = lax.all_gather(activations, "head", axis=2, tiled=True)[0]
    T, F = act.shape
    FB, C = value_weight.shape
    H = log_gate.shape[1]
    D = C // H
    TH = T + EDGE
    CW = D
    CC = CW * parts
    CT = min(512, C // reps)
    NW, NM, NT = C // reps // CW, C // reps // CC, C // CT
    NH = NT // reps
    UP = 2 * H // n
    scale = 1.0 / math.sqrt(n * reps * T)
    dma = pltpu.SemaphoreType.DMA
    peers = max(reps - 1, 1)
    scratch = [
        pltpu.VMEM((reps * TH, F), BF16),
        pltpu.VMEM((NW, n, reps * FB, CW), BF16),
        pltpu.VMEM((NM, reps * TH, CC), BF16),
        pltpu.VMEM((reps * NM, TH, CC), BF16),
        pltpu.VMEM((2, EDGE, C), BF16),
        pltpu.VMEM((3, TH, D), F32),
        pltpu.VMEM((H, T), F32),
        pltpu.VMEM((H, T, D), F32),
        pltpu.VMEM((H, T, D), F32),
        pltpu.VMEM((H, T, T), F32),
        pltpu.VMEM((H, T, D), BF16),
        pltpu.VMEM((H, T, D), BF16),
        pltpu.VMEM((H, T, D), BF16),
        pltpu.VMEM((H, T, D), BF16),
        pltpu.VMEM((H, T, 3 * D), BF16),
        pltpu.VMEM((H, T, 3 * D), BF16),
        pltpu.VMEM((H, 2 * D, T), BF16),
        pltpu.VMEM((H, 2 * D, T), BF16),
        pltpu.VMEM((H, T, 2 * D), BF16),
        pltpu.VMEM((4, H, D, D), F32),
        pltpu.VMEM((4, H, D, D), BF16),
        pltpu.VMEM((2, H, D, D), BF16),
        pltpu.VMEM((2, H, D, D), BF16),
        pltpu.VMEM((2, H, D, D), BF16),
        pltpu.VMEM((2, H, D, D), BF16),
        pltpu.VMEM((2, H, D), F32),
        pltpu.VMEM((3, H, T + 8, D), F32),
        pltpu.VMEM((3, H, EDGE, D), BF16),
        pltpu.VMEM((3, H, EDGE, D), BF16),
        pltpu.VMEM((F, T), BF16),
        pltpu.VMEM((reps * FB, n * T), BF16),
        pltpu.VMEM((NT, n, T, CT), BF16),
        pltpu.VMEM((reps, NH, T, CT), BF16),
        pltpu.VMEM((reps, T, F), F32),
        pltpu.VMEM((reps, T, F), BF16),
        pltpu.VMEM((peers, T, F), BF16),
        pltpu.VMEM((NT, reps * FB, CT), BF16),
        pltpu.VMEM((NT, peers, FB, CT), BF16),
        pltpu.VMEM((NT, reps * FB, CT), F32),
        pltpu.VMEM((n * UP, 8, D), F32),
        pltpu.VMEM((n, UP, 8, D), F32),
        pltpu.VMEM((reps, UP, 8, D), F32),
        pltpu.VMEM((n * UP, 8, D), F32),
        dma((NM, peers)), dma((NM, peers)),
        dma((peers,)), dma((peers,)),
        dma((reps,)), dma((reps,)),
        dma((2,)), dma((2,)),
        dma((max(NM, NT), n + 1)), dma((max(NW, NT), n)),
        dma((max(parts - 1, 1), NM)), dma((max(parts - 1, 1), NM)),
        dma((NM, peers)), dma((NM, peers)),
        dma((1,)), dma((n - 1,)),
        dma((1,)), dma((1,)),
        dma((2,)), dma((2, H)),
        dma((2,)), dma((2, H)),
        dma((2,)), dma((2, H)),
        dma((2,)), dma((2,)),
        dma((NT,)), dma((NT,)),
        dma((NH, peers)), dma((NH, peers)),
        dma((peers,)), dma((peers,)),
        dma((NT, peers)), dma((NT, peers)),
        dma((1,)), dma((n - 1,)),
        dma((peers,)), dma((peers,)),
        dma((1,)), dma((n - 1,)),
    ]
    vmem = pl.BlockSpec(memory_space=pltpu.VMEM)
    results = pl.pallas_call(
        functools.partial(kernel, n, reps, parts, scale),
        out_shape=(
            jax.ShapeDtypeStruct((T, C), BF16),
            jax.ShapeDtypeStruct((T, C), BF16),
            jax.ShapeDtypeStruct((T, C), BF16),
            jax.ShapeDtypeStruct((T, F), BF16),
            jax.ShapeDtypeStruct((FB, C), F32),
            jax.ShapeDtypeStruct(conv_kernel.shape, F32),
        ),
        in_specs=[vmem] * 7,
        out_specs=[vmem] * 6,
        scratch_shapes=scratch,
        compiler_params=pltpu.CompilerParams(
            collective_id=0, has_side_effects=True, vmem_limit_bytes=60 * 2**20
        ),
        cost_estimate=pl.CostEstimate(flops=5 * 10**9, bytes_accessed=8 * 2**20, transcendentals=10**6),
    )(act, value_weight, query_in[0], key_in[0], grad_out[0], conv_kernel, log_gate[0])
    kept = pl.BlockSpec(memory_space=pl.ANY)
    attn_out, grad_query, grad_key, part_x, grad_w, grad_conv = pl.pallas_call(
        hand_over,
        out_shape=tuple(jax.ShapeDtypeStruct(a.shape, a.dtype) for a in results),
        in_specs=[vmem] * len(results),
        out_specs=(kept,) * len(results),
        scratch_shapes=[pltpu.SemaphoreType.DMA((len(results),))],
    )(*results)
    grad_x = lax.psum_scatter(part_x[None], "head", scatter_dimension=2, tiled=True)
    return attn_out[None], grad_query[None], grad_key[None], grad_x, grad_w, grad_conv


def solution(mesh):
    placed = (
        P(("parts", "rep"), "seq", "head"),
        P(("seq", "rep"), "head"),
        P(("parts", "rep"), "seq", "head"),
        P(("parts", "rep"), "seq", "head"),
        P(("parts", "rep"), "seq", "head"),
        P(None, None, "head"),
        P(("parts", "rep"), "head", "seq"),
    )
    return jax.shard_map(
        functools.partial(local, mesh.shape["seq"], mesh.shape["rep"], mesh.shape["parts"]),
        mesh=mesh,
        in_specs=placed,
        out_specs=(
            P(("parts", "rep"), "seq", "head"),
            P(("parts", "rep"), "seq", "head"),
            P(("parts", "rep"), "seq", "head"),
            P(("parts", "rep"), "seq", "head"),
            P(("parts", "seq", "rep"), "head"),
            P("parts", None, "head"),
        ),
        check_vma=False,
    )
```

```python
import functools
import math

import jax
import jax.numpy as jnp
from jax import lax
from jax.experimental import pallas as pl
from jax.experimental.pallas import tpu as pltpu
from jax.sharding import PartitionSpec as P

EPSILON = 1e-06
EDGE = 16
LAG = 4
TWIN_LAG = 3
W_SKEW = 0
G_SKEW = 1
SWAP_EVERY = 5
EDGE_LAG = 5
TILE = 512
F32 = jnp.float32
BF16 = jnp.bfloat16


def dot(a, b):
    return lax.dot_general(a, b, (((1,), (0,)), ((), ())), preferred_element_type=F32)


def dot_t(a, b):
    return lax.dot_general(a, b, (((1,), (1,)), ((), ())), preferred_element_type=F32)


def kernel(n, reps, parts, scale, *refs):
    (act, w, q, k, go, ck, lg) = refs[:7]
    (ao, gq, gk, px, gw, gc) = refs[7:13]
    (
        acta, wg, vout, vr, qkh, xf, cumr, rise, shrink, mx, qh, kh, vh, gh, lhs1, lhs2, kt, qt, rsv,
        sums, sin, raw, sout, mates, kept, decays, po, phs, phr, actt, actc, gvg, gxi, pxf, pxs, pxi, gws, gwi, gwa,
        gcp, gca, gcb, gcf,
        wxs, wxr, axs, axr, ahs, ahr, qhs, qhr, gas, gar, wys, wms, vxs, vxr, ats, atr, dcs, dcr, ss, rr, fs, sr, ms, mr, phss, phsr, pvs, pvr,
        gxs, gxr, pxss, pxsr, gwss, gwsr, cs1, cr1, cs2, cr2, cs3, cr3,
    ) = refs[13:]
    T, F = act.shape
    FB, C = w.shape
    H = lg.shape[0]
    D = C // H
    TH = T + EDGE
    NW, _, _, CW = wg.shape
    NM, _, CC = vout.shape
    NT, _, _, CT = gvg.shape
    half = C // reps
    NH = NT // reps
    UP = 2 * H // n
    me = lax.axis_index("seq")
    r = lax.axis_index("rep")
    y = lax.axis_index("parts")
    odd = lax.rem(me, 2)
    mate = me + 1 - 2 * odd
    way, pair, pairs = 1 - odd, me // 2, n // 2
    lead = jnp.where(odd == 1, pair, pairs - 1 - pair)
    follow = pairs - 1 - lead
    onward = lax.rem(jnp.where(odd == 1, me + 2, me + n - 2), n)
    leads_first, leads_last, follows_first = lead == 0, lead == pairs - 1, follow == 0
    first, last = me == 0, me == n - 1
    right, left = lax.rem(me + 1, n), lax.rem(me + n - 1, n)

    def peer(d):
        return lax.rem(r + d, reps)

    def remote(src, dst, send, recv, seq, rep, part=None):
        return pltpu.make_async_remote_copy(
            src_ref=src, dst_ref=dst, send_sem=send, recv_sem=recv,
            device_id={"parts": y if part is None else part, "seq": seq, "rep": rep},
            device_id_type=pl.DeviceIdType.MESH,
        )

    def lanes(h):
        return pl.ds(pl.multiple_of(h * D, D), D)

    barrier = pltpu.get_barrier_semaphore()
    for ds in range(n):
        for dr in range(reps):
            if ds or dr:
                pl.semaphore_signal(
                    barrier, inc=1, device_id={"seq": lax.rem(me + ds, n), "rep": peer(dr)},
                    device_id_type=pl.DeviceIdType.MESH,
                )
    for dy in range(1, parts):
        pl.semaphore_signal(
            barrier, inc=1, device_id={"parts": lax.rem(y + dy, parts)}, device_id_type=pl.DeviceIdType.MESH
        )

    total = lg[...]
    place = lax.broadcasted_iota(jnp.int32, total.shape, 1)
    distance = 1
    while distance < T:
        moved = pltpu.roll(total, distance, 1)
        total = total + jnp.where(place >= distance, moved, 0.0)
        distance *= 2
    cumr[...] = total
    columns = jnp.concatenate([total, jnp.zeros((T - H, T), F32)], axis=0).T
    for h in range(H):
        rise[h] = jnp.broadcast_to(columns[:, h : h + 1], (T, D))

    for m in range(NM):
        c = m * parts + y
        wg[c, me, pl.ds(r * FB, FB), :] = w[:, pl.ds(pl.multiple_of(r * half + c * CW, CW), CW)]
    acta[pl.ds(r * TH + EDGE, T), :] = act[...]

    @pl.when(first)
    def _():
        for d in range(reps):
            acta[pl.ds(d * TH, EDGE), :] = jnp.zeros((EDGE, F), BF16)
        qkh[...] = jnp.zeros(qkh.shape, BF16)

    @pl.when(leads_first)
    def _():
        raw[...] = jnp.zeros(raw.shape, BF16)

    @pl.when(follows_first)
    def _():
        sin[1 - way] = jnp.zeros(sin.shape[1:], BF16)
        sin[3 - way] = jnp.zeros(sin.shape[1:], BF16)

    decays[0] = jnp.exp(jnp.broadcast_to(total[:, T - 1 : T], (H, D)))

    @pl.when(last)
    def _():
        phr[...] = jnp.zeros(phr.shape, BF16)

    pl.semaphore_wait(barrier, n * reps - 1 + parts - 1)

    def w_swap(m, d):
        to, c = peer(d), m * parts + y
        return remote(
            w.at[:, pl.ds(pl.multiple_of(to * half + c * CW, CW), CW)],
            wg.at[c, me, pl.ds(r * FB, FB), :], wxs.at[m, d - 1], wxr.at[m, d - 1], me, to,
        )

    def act_swap(d):
        return remote(act, acta.at[pl.ds(r * TH + EDGE, T), :], axs.at[d - 1], axr.at[d - 1], me, peer(d))

    def act_edge(d):
        return remote(
            act.at[pl.ds(T - EDGE, EDGE), :], acta.at[pl.ds(r * TH, EDGE), :], ahs.at[d], ahr.at[d], right, peer(d)
        )

    def qk_edge(i):
        return remote((q, k)[i].at[pl.ds(T - EDGE, EDGE), :], qkh.at[i], qhs.at[i], qhr.at[i], right, r)

    for d in range(1, reps):
        w_swap(0, d).start()

    decay_swap = remote(decays.at[0], decays.at[1], dcs.at[0], dcr.at[0], mate, r)
    decay_swap.start()

    @pl.when(jnp.logical_not(last))
    def _():
        for i in range(2):
            qk_edge(i).start()

    for m in range(1, NM):
        for d in range(1, reps):
            w_swap(m, d).start()
    for d in range(1, reps):
        act_swap(d).start()

    @pl.when(jnp.logical_not(last))
    def _():
        for d in range(reps):
            act_edge(d).start()

    def hop(buf, c, m, o, way):
        mark = jnp.where(o == me, n, o) if way else o
        return remote(buf.at[c, o], buf.at[c, o], gas.at[m, mark], gar.at[c, o], (right, left)[way], r)

    def own(buf, c, m):
        @pl.when(jnp.logical_not(last))
        def _():
            hop(buf, c, m, me, 0).start()

        @pl.when(jnp.logical_not(first))
        def _():
            hop(buf, c, m, me, 1).start()

    def pass_on(buf, c, m, t, seen=None):
        lower, upper = me - t, me + t

        @pl.when(lower >= 0)
        def _():
            hop(buf, c, m, lower, 0).wait_recv()

            @pl.when(jnp.logical_not(last))
            def _():
                hop(buf, c, m, lower, 0).start()

            if seen is not None:
                seen(lower)

        @pl.when(upper < n)
        def _():
            hop(buf, c, m, upper, 1).wait_recv()

            @pl.when(jnp.logical_not(first))
            def _():
                hop(buf, c, m, upper, 1).start()

            if seen is not None:
                seen(upper)

    def sent(buf, chunks):
        def one(i, _):
            c, o = i // n, lax.rem(i, n)

            @pl.when(jnp.logical_and(jnp.logical_not(last), o <= me))
            def _():
                hop(buf, c, c, o, 0).wait_send()

            @pl.when(jnp.logical_and(jnp.logical_not(first), o >= me))
            def _():
                hop(buf, c, c, o, 1).wait_send()

            return 0

        lax.fori_loop(0, chunks * n, one, 0)

    def to_twin(m, dy, o):
        c = m * parts + y
        return remote(wg.at[c, o], wg.at[c, o], wys.at[dy - 1, m], gar.at[c, o], me, r, lax.rem(y + dy, parts))

    def to_mate(m, dy, o):
        c = m * parts + lax.rem(y + dy, parts)
        return remote(wg.at[c, o], wg.at[c, o], wms.at[dy - 1, m], gar.at[c, o], mate, r)

    def filtered(i, x, taps):
        out = taps[0:1] * x[i, EDGE : EDGE + T]
        for j in range(1, 4):
            out = out + taps[j : j + 1] * x[i, EDGE - j : EDGE - j + T]
        return out.astype(BF16)

    def load_rows(i, h):
        if i < 2:
            xf[i, 0:EDGE] = qkh[i, :, lanes(h)].astype(F32)
            xf[i, EDGE:] = (q, k)[i][:, lanes(h)].astype(F32)
        else:
            per = CC // D
            xf[i] = vr[h // per, :, pl.ds(pl.multiple_of(lax.rem(h, per) * D, D), D)].astype(F32)

    def prepare(h):
        cc = rise[h]
        fin = cc[T - 1 : T]
        rising = jnp.exp(cc)
        shrinking = jnp.exp(fin - cc)
        mixing = jnp.exp(-jnp.abs(cc - cumr[pl.ds(h, 1), :]))
        rise[h] = rising
        shrink[h] = shrinking
        mx[h] = mixing
        for i in range(2):
            load_rows(i, h)
        qv = filtered(0, xf, ck[0, :, lanes(h)])
        kv = filtered(1, xf, ck[1, :, lanes(h)])
        qh[h] = qv
        kh[h] = kv
        qf, kf = qv.astype(F32), kv.astype(F32)
        rq, sq = (rising * qf), (shrinking * qf)
        rk, sk = (rising * kf), (shrinking * kf)
        lhs1[h, :, 0:D] = (mixing * dot_t(qv, kv)).astype(BF16)
        lhs1[h, :, D : 2 * D] = rq.astype(BF16)
        lhs1[h, :, 2 * D :] = sq.astype(BF16)
        lhs2[h, :, 0:D] = (mixing * dot_t(kv, qv)).astype(BF16)
        lhs2[h, :, D : 2 * D] = rk.astype(BF16)
        lhs2[h, :, 2 * D :] = sk.astype(BF16)
        qt[h, 0:D] = sq.T.astype(BF16)
        qt[h, D:] = rq.T.astype(BF16)
        kt[h, 0:D] = sk.T.astype(BF16)
        kt[h, D:] = rk.T.astype(BF16)

    def turn(b):
        rows = pl.ds(pl.multiple_of(b * T, T), T)
        actt[rows, :] = act[:, rows].astype(F32).T.astype(BF16)

    def ready(m):
        for d in range(1, reps):
            w_swap(m, d).wait_recv()
        own(wg, m * parts + y, m)
        for dy in range(1, parts):
            to_twin(m, dy, me).start()

    def v_swap(c, d):
        to = peer(d)
        return remote(
            vout.at[c, pl.ds(to * TH, TH), :], vr.at[r * NM + c], vxs.at[c, d - 1], vxr.at[c, d - 1], me, to
        )

    @pl.when(jnp.logical_not(first))
    def _():
        for i in range(2):
            qk_edge(i).wait_recv()

    def jobs(work, count, step, steps):
        per = -(-count // steps)
        for j in range(per):
            @pl.when(step * per + j < count)
            def _():
                work(step * per + j)

    W_STEPS = n + TWIN_LAG + W_SKEW * (NM - 1)

    def w_step(s, _):
        for m in range(NM):
            t = s - W_SKEW * m

            @pl.when(t == 0)
            def _():
                ready(m)

            def twins(o):
                @pl.when(lax.rem(t, 2) == 0)
                def _():
                    for dy in range(1, parts):
                        to_twin(m, dy, o).start()

            @pl.when(jnp.logical_and(t >= 1, t < n))
            def _():
                pass_on(wg, m * parts + y, m, t, twins)

            for dy in range(1, parts):
                for near, source in ((True, me), (False, mate)):
                    u = t - (TWIN_LAG if near else TWIN_LAG + 1)

                    def take(o):
                        to_mate(m, dy, o).wait_recv()
                        if near:
                            to_mate(m, dy, o).start()

                    def even(ok):
                        return jnp.logical_and(jnp.logical_and(u >= 0, u < n), jnp.logical_and(lax.rem(u, 2) == 0, ok))

                    @pl.when(even(source - u >= 0))
                    def _():
                        take(source - u)

                    @pl.when(even(jnp.logical_and(u > 0, source + u < n)))
                    def _():
                        take(source + u)

            @pl.when(t == n - 1 + TWIN_LAG)
            def _():
                if m == 0:
                    for d in range(1, reps):
                        act_swap(d).wait_recv()

                    @pl.when(jnp.logical_not(first))
                    def _():
                        for d in range(reps):
                            act_edge(d).wait_recv()

                columns_of = [wg[m * parts + j].reshape(F, CW) for j in range(parts)]
                vout[m] = dot(acta[...], jnp.concatenate(columns_of, axis=1)).astype(BF16)
                for d in range(1, reps):
                    v_swap(m, d).start()
                vr[r * NM + m] = vout[m, pl.ds(r * TH, TH), :]

        jobs(prepare, H, s, n)
        jobs(turn, F // T, s, n)
        return 0

    lax.fori_loop(0, W_STEPS, w_step, 0)

    def a_swap(d):
        to = lax.rem(me + d, n)
        return remote(
            actt.at[pl.ds(to * reps * FB, reps * FB), :], actc.at[:, pl.ds(pl.multiple_of(me * T, T), T)],
            ats.at[0], atr.at[d - 1], to, r,
        )

    def a_swap_from(d):
        source = lax.rem(me + n - d, n)
        return remote(
            actt.at[pl.ds(0, reps * FB), :], actc.at[:, pl.ds(pl.multiple_of(source * T, T), T)],
            ats.at[0], atr.at[d - 1], source, r,
        )

    actc[:, pl.ds(pl.multiple_of(me * T, T), T)] = actt[pl.ds(me * reps * FB, reps * FB), :]

    def v_arrival(c, d):
        source = lax.rem(r + reps - d, reps)
        return remote(
            vout.at[c, pl.ds(0, TH), :], vr.at[source * NM + c], vxs.at[c, d - 1], vxr.at[c, d - 1], me, source
        )

    for c in range(NM):
        for d in range(1, reps):
            v_arrival(c, d).wait_recv()

    decay_swap.wait_recv()

    def values(h):
        load_rows(2, h)
        v = filtered(2, xf, ck[2, :, lanes(h)])
        vh[h] = v
        vf = v.astype(F32)
        rsv[h, :, 0:D] = (rise[h] * vf).astype(BF16)
        rsv[h, :, D:] = (shrink[h] * vf).astype(BF16)
        both = dot(kt[h], v)
        sums[0, h] = both[0:D]
        sums[1, h] = both[D:]
        share(0, h)

    def message(j, h):
        return remote(sout.at[j, h], raw.at[j, h], ss.at[j], rr.at[j, h], onward, r)

    def hand_in(j, h, which):
        return remote(raw.at[j, h], sin.at[2 * j + which, h], fs.at[j], sr.at[j, h], mate, r)

    def mate_sum(j, h):
        return remote(mates.at[j, h], kept.at[j, h], ms.at[j], mr.at[j, h], mate, r)

    def share(j, h):
        mates[j, h] = sums[2 * j + 1 - way, h].astype(BF16)
        mate_sum(j, h).start()

    def carry(j, h):
        @pl.when(jnp.logical_not(leads_first))
        def _():
            message(j, h).wait_recv()
            hand_in(j, h, way).start()

        mate_sum(j, h).wait_recv()
        i = 2 * j + way
        state = decays[1, pl.ds(h, 1), :] * raw[j, h].astype(F32) + kept[j, h].astype(F32)
        sin[i, h] = state.astype(BF16)

        @pl.when(jnp.logical_not(leads_last))
        def _():
            sout[j, h] = (decays[0, pl.ds(h, 1), :] * state + sums[i, h]).astype(BF16)
            message(j, h).start()

    def handed(j, h):
        @pl.when(jnp.logical_not(follows_first))
        def _():
            hand_in(j, h, 1 - way).wait_recv()

    def attend(h):
        handed(0, h)
        v, before, after = vh[h], sin[0, h], sin[1, h]
        attn = dot(lhs1[h], jnp.concatenate([v, before, after], axis=0))
        inverse = lax.rsqrt(jnp.mean(attn * attn, axis=1, keepdims=True) + EPSILON)
        normed = attn * inverse
        ao[:, lanes(h)] = normed.astype(BF16)
        up = go[:, lanes(h)].astype(F32)
        g = ((up - normed * jnp.mean(up * normed, axis=1, keepdims=True)) * inverse).astype(BF16)
        gh[h] = g
        both = dot(qt[h], g)
        sums[2, h] = both[0:D]
        sums[3, h] = both[D:]
        share(1, h)

    def query_side(h):
        v, before, after, g, mixing = vh[h], sin[0, h], sin[1, h], gh[h], mx[h]
        gf = g.astype(F32)
        decayed = jnp.concatenate([(rise[h] * gf).astype(BF16), (shrink[h] * gf).astype(BF16)], axis=1)
        grad_scores = (mixing * dot_t(g, v)).astype(BF16)
        grad_scores_t = (mixing * dot_t(v, g)).astype(BF16)
        po[0, h, 0:T] = dot(grad_scores, kh[h]) + dot_t(decayed, jnp.concatenate([before, after], axis=1))
        po[1, h, 0:T] = dot(grad_scores_t, qh[h])

    def key_side(h):
        handed(1, h)
        before, after = sin[2, h], sin[3, h]
        po[1, h, 0:T] = po[1, h, 0:T] + dot_t(rsv[h], jnp.concatenate([before, after], axis=1))
        po[2, h, 0:T] = dot(lhs2[h], jnp.concatenate([gh[h], before, after], axis=0))
        rows = []
        for i in range(3):
            load_rows(i, h)
            post = po[i, h, 0:T]
            phs[i, h] = post[0:EDGE].astype(BF16)
            for j in range(4):
                rows.append(jnp.sum(post * xf[i, EDGE - j : EDGE - j + T], axis=0, keepdims=True))
        zero = jnp.zeros((4, D), F32)
        gcp[2 * h] = jnp.concatenate(rows[0:8], axis=0)
        gcp[2 * h + 1] = jnp.concatenate(rows[8:12] + [zero], axis=0)

    PER = CT // D

    def post_edge(i):
        return remote(phs.at[i], phr.at[i], phss.at[i], phsr.at[i], left, r)

    def value_edge(c):
        heads = pl.ds(c * PER, PER)
        return remote(phs.at[2, heads], phr.at[2, heads], pvs.at[c], pvr.at[c], left, r)

    def back(i, h):
        po[i, h, T : T + 8] = phr[i, h].astype(F32)[0:8]
        taps = ck[i, :, lanes(h)]
        out = taps[0:1] * po[i, h, 0:T]
        for j in range(1, 4):
            out = out + taps[j : j + 1] * po[i, h, j : j + T]
        return out.astype(BF16)

    def gx_swap(j, d):
        to = peer(d)
        return remote(gvg.at[to * NH + j, me], gxi.at[r, j], gxs.at[j, d - 1], gxr.at[j, d - 1], me, to)

    def weight_sent(i, _):
        m, o = i // n, lax.rem(i, n)
        c = m * parts + y

        @pl.when(jnp.logical_and(jnp.logical_not(last), o <= me))
        def _():
            hop(wg, c, m, o, 0).wait_send()

        @pl.when(jnp.logical_and(jnp.logical_not(first), o >= me))
        def _():
            hop(wg, c, m, o, 1).wait_send()

        return 0

    def send_value_edge(c):
        @pl.when(jnp.logical_not(first))
        def _():
            value_edge(c).start()

    def value_grad(c):
        @pl.when(jnp.logical_not(last))
        def _():
            value_edge(c).wait_recv()

        for j in range(PER):
            gvg[c, me, :, j * D : (j + 1) * D] = back(2, c * PER + j)
        own(gvg, c, c)
        for d in range(1, reps):
            j = c - peer(d) * NH

            @pl.when(jnp.logical_and(j >= 0, j < NH))
            def _():
                gx_swap(j, d).start()

    far = (pairs - 1) * LAG + 2

    def scan_step(s, _):
        def at(h, work):
            @pl.when(jnp.logical_and(h >= 0, h < H))
            def _():
                work(h)

        @pl.when(jnp.logical_and(lax.rem(s, SWAP_EVERY) == SWAP_EVERY - 1, s // SWAP_EVERY + 1 < n))
        def _():
            a_swap(s // SWAP_EVERY + 1).start()

        at(s, values)
        at(s - lead * LAG - 1, functools.partial(carry, 0))
        at(s - far, attend)
        at(s - far - lead * LAG - 1, functools.partial(carry, 1))
        at(s - far, query_side)
        at(s - 2 * far, key_side)

        @pl.when(s == 2 * far - 1)
        def _():
            lax.fori_loop(0, NM * n, weight_sent, 0)

        def at_chunk(h, work):
            @pl.when(jnp.logical_and(jnp.logical_and(h >= 0, h < H), lax.rem(h + PER, PER) == PER - 1))
            def _():
                work(h // PER)

        at_chunk(s - 2 * far, send_value_edge)
        at_chunk(s - 2 * far - EDGE_LAG, value_grad)
        return 0

    lax.fori_loop(0, H + 2 * far + EDGE_LAG, scan_step, 0)

    @pl.when(jnp.logical_not(first))
    def _():
        for i in range(2):
            post_edge(i).start()

    def taps_out(d):
        to = lax.rem(me + d, n)
        return remote(gcp.at[pl.ds(to * UP, UP)], gca.at[me], cs1.at[0], cr1.at[d - 1], to, r)

    def taps_in(d):
        source = lax.rem(me + n - d, n)
        return remote(gcp.at[pl.ds(0, UP)], gca.at[source], cs1.at[0], cr1.at[d - 1], source, r)

    def taps_swap(d):
        return remote(gcb.at[r], gcb.at[r], cs2.at[d - 1], cr2.at[d - 1], me, peer(d))

    def taps_swap_in(d):
        source = lax.rem(r + reps - d, reps)
        return remote(gcb.at[r], gcb.at[source], cs2.at[d - 1], cr2.at[d - 1], me, source)

    def taps_back(d):
        to = lax.rem(me + d, n)
        return remote(gcf.at[pl.ds(me * UP, UP)], gcf.at[pl.ds(me * UP, UP)], cs3.at[0], cr3.at[d - 1], to, r)

    def taps_back_in(d):
        source = lax.rem(me + n - d, n)
        return remote(
            gcf.at[pl.ds(me * UP, UP)], gcf.at[pl.ds(source * UP, UP)], cs3.at[0], cr3.at[d - 1], source, r
        )

    for d in range(1, n):
        taps_out(d).start()
    gca[me] = gcp[pl.ds(me * UP, UP)]

    def gx_swap_in(j, d):
        source = lax.rem(r + reps - d, reps)
        return remote(gvg.at[j, me], gxi.at[source, j], gxs.at[j, d - 1], gxr.at[j, d - 1], me, source)

    for j in range(NH):
        gxi[r, j] = gvg[r * NH + j, me]

    @pl.when(jnp.logical_not(last))
    def _():
        for i in range(2):
            post_edge(i).wait_recv()

    def input_grad(b):
        rows = wg.shape[2]
        per = TILE // rows
        out = jnp.zeros((reps * T, TILE), F32)
        for m in range(NM):
            j, at = divmod(m * CC, CT)
            x = gxi[:, j, :, at : at + CC].reshape(reps * T, CC)
            rows_of = [wg[m * parts + i, pl.ds(b * per, per)].reshape(TILE, CW) for i in range(parts)]
            out = out + dot_t(x, jnp.concatenate(rows_of, axis=1))
        cols = pl.ds(pl.multiple_of(b * TILE, TILE), TILE)
        for i in range(reps):
            pxf[i, :, cols] = out[i * T : (i + 1) * T]
            pxs[i, :, cols] = out[i * T : (i + 1) * T].astype(BF16)

    def px_swap(d):
        to = peer(d)
        return remote(pxs.at[to], pxi.at[d - 1], pxss.at[d - 1], pxsr.at[d - 1], me, to)

    def gw_swap(c, d):
        to = peer(d)
        return remote(gws.at[c, pl.ds(to * FB, FB), :], gwi.at[c, d - 1], gwss.at[c, d - 1], gwsr.at[c, d - 1], me, to)

    X_TILES = F // TILE
    G_STEPS = n + G_SKEW * (NT - 1)

    def both_back(h):
        gq[:, lanes(h)] = back(0, h)
        gk[:, lanes(h)] = back(1, h)

    def last_step(s, _):
        for c in range(NT):
            t = s - G_SKEW * c

            @pl.when(jnp.logical_and(t >= 1, t < n))
            def _():
                pass_on(gvg, c, c, t)

            @pl.when(t == n - 1)
            def _():
                if c == 0:
                    for d in range(1, n):
                        a_swap_from(d).wait_recv()

                gwa[c] = dot(actc[...], gvg[c].reshape(n * T, CT))
                gws[c] = gwa[c].astype(BF16)
                for d in range(1, reps):
                    gw_swap(c, d).start()

        jobs(both_back, H, s, n)

        @pl.when(s == 1)
        def _():
            for d in range(1, n):
                taps_in(d).wait_recv()
            part = gca[0]
            for o in range(1, n):
                part = part + gca[o]
            gcb[r] = part
            for d in range(1, reps):
                taps_swap(d).start()

        @pl.when(s == 3)
        def _():
            for d in range(1, reps):
                taps_swap_in(d).wait_recv()
            part = gcb[0]
            for o in range(1, reps):
                part = part + gcb[o]
            gcf[pl.ds(me * UP, UP)] = part * scale
            for d in range(1, n):
                taps_back(d).start()

        @pl.when(s == 0)
        def _():
            for j in range(NH):
                for d in range(1, reps):
                    gx_swap_in(j, d).wait_recv()

        @pl.when(jnp.logical_and(s >= 1, s < 1 + X_TILES))
        def _():
            input_grad(s - 1)

        @pl.when(s == 1 + X_TILES)
        def _():
            for d in range(1, reps):
                px_swap(d).start()

        return 0

    lax.fori_loop(0, G_STEPS, last_step, 0)
    for d in range(1, reps):
        px_swap(d).wait_recv()
    out = pxf[r]
    for d in range(1, reps):
        out = out + pxi[d - 1].astype(F32)
    px[...] = out.astype(BF16)
    for d in range(1, n):
        taps_back_in(d).wait_recv()
    for h in range(H):
        gc[0, :, h * D : (h + 1) * D] = gcf[2 * h, 0:4]
        gc[1, :, h * D : (h + 1) * D] = gcf[2 * h, 4:8]
        gc[2, :, h * D : (h + 1) * D] = gcf[2 * h + 1, 0:4]
    for c in range(NT):
        for d in range(1, reps):
            gw_swap(c, d).wait_recv()
        out = gwa[c, pl.ds(r * FB, FB), :]
        for d in range(1, reps):
            out = out + gwi[c, d - 1].astype(F32)
        gw[:, c * CT : (c + 1) * CT] = out * scale

    for d in range(1, reps):
        act_swap(d).wait_send()
        px_swap(d).wait_send()
        taps_swap(d).wait_send()
        for m in range(NM):
            w_swap(m, d).wait_send()
            v_swap(m, d).wait_send()
        for c in range(NT):
            gw_swap(c, d).wait_send()
        for j in range(NH):
            gx_swap(j, d).wait_send()
    for dy in range(1, parts):
        for m in range(NM):
            blocks = wg.at[m, pl.ds(0, n // 2)]
            remote(blocks, blocks, wys.at[dy - 1, m], gar.at[0, 0], me, r, lax.rem(y + dy, parts)).wait_send()
            remote(blocks, blocks, wms.at[dy - 1, m], gar.at[0, 0], mate, r).wait_send()
    others = actt.at[pl.ds(0, (n - 1) * reps * FB), :]
    remote(others, others, ats.at[0], atr.at[0], right, r).wait_send()
    others = gcp.at[pl.ds(0, (n - 1) * UP)]
    remote(others, others, cs1.at[0], cr1.at[0], right, r).wait_send()
    remote(others, others, cs3.at[0], cr3.at[0], right, r).wait_send()

    @pl.when(jnp.logical_not(last))
    def _():
        for i in range(2):
            qk_edge(i).wait_send()
        for d in range(reps):
            act_edge(d).wait_send()

    @pl.when(jnp.logical_not(first))
    def _():
        for i in range(2):
            post_edge(i).wait_send()
        for c in range(NT):
            value_edge(c).wait_send()

    sent(gvg, NT)
    decay_swap.wait_send()
    for j in range(2):
        remote(mates.at[j], kept.at[j], ms.at[j], mr.at[j, 0], mate, r).wait_send()

        @pl.when(jnp.logical_not(leads_last))
        def _():
            remote(sout.at[j], raw.at[j], ss.at[j], rr.at[j, 0], onward, r).wait_send()

        @pl.when(jnp.logical_not(leads_first))
        def _():
            remote(raw.at[j], sin.at[2 * j], fs.at[j], sr.at[j, 0], mate, r).wait_send()


def hand_over(count, *refs):
    sources, targets, held = refs[:count], refs[count : 2 * count], refs[2 * count : 3 * count]
    come, go = refs[3 * count :]
    arrive = [pltpu.make_async_copy(sources[i], held[i], come.at[i]) for i in range(count)]
    leave = [pltpu.make_async_copy(held[i], targets[i], go.at[i]) for i in range(count)]
    for copy in arrive:
        copy.start()
    for i in range(count):
        arrive[i].wait()
        leave[i].start()
    for copy in leave:
        copy.wait()


def local(n, reps, parts, activations, value_weight, query_in, key_in, grad_out, conv_kernel, log_gate):
    act = lax.all_gather(activations, "head", axis=2, tiled=True)[0]
    T, F = act.shape
    FB, C = value_weight.shape
    H = log_gate.shape[1]
    D = C // H
    TH = T + EDGE
    CW = D
    CC = CW * parts
    CT = min(512, C // reps)
    NW, NM, NT = C // reps // CW, C // reps // CC, C // CT
    NH = NT // reps
    UP = 2 * H // n
    scale = 1.0 / math.sqrt(n * reps * T)
    dma = pltpu.SemaphoreType.DMA
    peers = max(reps - 1, 1)
    scratch = [
        pltpu.VMEM((reps * TH, F), BF16),
        pltpu.VMEM((NW, n, reps * FB, CW), BF16),
        pltpu.VMEM((NM, reps * TH, CC), BF16),
        pltpu.VMEM((reps * NM, TH, CC), BF16),
        pltpu.VMEM((2, EDGE, C), BF16),
        pltpu.VMEM((3, TH, D), F32),
        pltpu.VMEM((H, T), F32),
        pltpu.VMEM((H, T, D), F32),
        pltpu.VMEM((H, T, D), F32),
        pltpu.VMEM((H, T, T), F32),
        pltpu.VMEM((H, T, D), BF16),
        pltpu.VMEM((H, T, D), BF16),
        pltpu.VMEM((H, T, D), BF16),
        pltpu.VMEM((H, T, D), BF16),
        pltpu.VMEM((H, T, 3 * D), BF16),
        pltpu.VMEM((H, T, 3 * D), BF16),
        pltpu.VMEM((H, 2 * D, T), BF16),
        pltpu.VMEM((H, 2 * D, T), BF16),
        pltpu.VMEM((H, T, 2 * D), BF16),
        pltpu.VMEM((4, H, D, D), F32),
        pltpu.VMEM((4, H, D, D), BF16),
        pltpu.VMEM((2, H, D, D), BF16),
        pltpu.VMEM((2, H, D, D), BF16),
        pltpu.VMEM((2, H, D, D), BF16),
        pltpu.VMEM((2, H, D, D), BF16),
        pltpu.VMEM((2, H, D), F32),
        pltpu.VMEM((3, H, T + 8, D), F32),
        pltpu.VMEM((3, H, EDGE, D), BF16),
        pltpu.VMEM((3, H, EDGE, D), BF16),
        pltpu.VMEM((F, T), BF16),
        pltpu.VMEM((reps * FB, n * T), BF16),
        pltpu.VMEM((NT, n, T, CT), BF16),
        pltpu.VMEM((reps, NH, T, CT), BF16),
        pltpu.VMEM((reps, T, F), F32),
        pltpu.VMEM((reps, T, F), BF16),
        pltpu.VMEM((peers, T, F), BF16),
        pltpu.VMEM((NT, reps * FB, CT), BF16),
        pltpu.VMEM((NT, peers, FB, CT), BF16),
        pltpu.VMEM((NT, reps * FB, CT), F32),
        pltpu.VMEM((n * UP, 8, D), F32),
        pltpu.VMEM((n, UP, 8, D), F32),
        pltpu.VMEM((reps, UP, 8, D), F32),
        pltpu.VMEM((n * UP, 8, D), F32),
        dma((NM, peers)), dma((NM, peers)),
        dma((peers,)), dma((peers,)),
        dma((reps,)), dma((reps,)),
        dma((2,)), dma((2,)),
        dma((max(NM, NT), n + 1)), dma((max(NW, NT), n)),
        dma((max(parts - 1, 1), NM)), dma((max(parts - 1, 1), NM)),
        dma((NM, peers)), dma((NM, peers)),
        dma((1,)), dma((n - 1,)),
        dma((1,)), dma((1,)),
        dma((2,)), dma((2, H)),
        dma((2,)), dma((2, H)),
        dma((2,)), dma((2, H)),
        dma((2,)), dma((2,)),
        dma((NT,)), dma((NT,)),
        dma((NH, peers)), dma((NH, peers)),
        dma((peers,)), dma((peers,)),
        dma((NT, peers)), dma((NT, peers)),
        dma((1,)), dma((n - 1,)),
        dma((peers,)), dma((peers,)),
        dma((1,)), dma((n - 1,)),
    ]
    vmem = pl.BlockSpec(memory_space=pltpu.VMEM)
    results = pl.pallas_call(
        functools.partial(kernel, n, reps, parts, scale),
        out_shape=(
            jax.ShapeDtypeStruct((T, C), BF16),
            jax.ShapeDtypeStruct((T, C), BF16),
            jax.ShapeDtypeStruct((T, C), BF16),
            jax.ShapeDtypeStruct((T, F), BF16),
            jax.ShapeDtypeStruct((FB, C), F32),
            jax.ShapeDtypeStruct(conv_kernel.shape, F32),
        ),
        in_specs=[vmem] * 7,
        out_specs=[vmem] * 6,
        scratch_shapes=scratch,
        compiler_params=pltpu.CompilerParams(
            collective_id=0, has_side_effects=True, vmem_limit_bytes=60 * 2**20
        ),
        cost_estimate=pl.CostEstimate(flops=5 * 10**9, bytes_accessed=8 * 2**20, transcendentals=10**6),
    )(act, value_weight, query_in[0], key_in[0], grad_out[0], conv_kernel, log_gate[0])
    kept = pl.BlockSpec(memory_space=pl.ANY)
    attn_out, grad_query, grad_key, part_x, grad_w, grad_conv = pl.pallas_call(
        functools.partial(hand_over, len(results)),
        out_shape=tuple(jax.ShapeDtypeStruct(a.shape, a.dtype) for a in results),
        in_specs=[kept] * len(results),
        out_specs=(kept,) * len(results),
        scratch_shapes=[pltpu.VMEM(a.shape, a.dtype) for a in results]
        + [pltpu.SemaphoreType.DMA((len(results),))] * 2,
    )(*results)
    grad_x = lax.psum_scatter(part_x[None], "head", scatter_dimension=2, tiled=True)
    return attn_out[None], grad_query[None], grad_key[None], grad_x, grad_w, grad_conv


def solution(mesh):
    placed = (
        P(("parts", "rep"), "seq", "head"),
        P(("seq", "rep"), "head"),
        P(("parts", "rep"), "seq", "head"),
        P(("parts", "rep"), "seq", "head"),
        P(("parts", "rep"), "seq", "head"),
        P(None, None, "head"),
        P(("parts", "rep"), "head", "seq"),
    )
    return jax.shard_map(
        functools.partial(local, mesh.shape["seq"], mesh.shape["rep"], mesh.shape["parts"]),
        mesh=mesh,
        in_specs=placed,
        out_specs=(
            P(("parts", "rep"), "seq", "head"),
            P(("parts", "rep"), "seq", "head"),
            P(("parts", "rep"), "seq", "head"),
            P(("parts", "rep"), "seq", "head"),
            P(("parts", "seq", "rep"), "head"),
            P("parts", None, "head"),
        ),
        check_vma=False,
    )
```
